32 devices in a mesh: groups: 2 (over y), blk: 4 (over z), feat: 4 (over x, core).
Axes of the slice: x: 2, y: 2, z: 4, core: 2. Of those that a mesh axis runs over, the one named last changes fastest.
Arguments:
- embeddings: bfloat16 [32768, 2048], P(('groups', 'blk'), 'feat'), parts along dimension 0, may hold values from -64 to 64
- centroids: bfloat16 [4096, 2048], P(('groups', 'blk')), parts along dimension 0, may hold values from -9 to 9
- pair_list: int32 [112, 2], P('groups'), parts along dimension 0, may hold values from 0 to 31, as said below
Outputs:
- new_centroids: float32 [4096, 2048], P(('groups', 'blk', 'feat')), parts along dimension 0
- log_norm: float32 [32768], P(('groups', 'blk', 'feat')), parts along dimension 0
The draws below stay inside these ranges and needn't reach their ends.
There are 2 independent parts, one for each index of `groups`. The reference program is written for one: setup_inputs(seed, part) draws one part's arguments, and reference() takes and returns one part's arrays. A program takes and returns all parts, laid end to end along the dimension named above; each array names one. Nothing has to cross between parts.
Inputs may be any that keep to these rules, and one draw needn't show every extreme that they name: `pair_list`: rows are ordered by row block; each row block has 1 to 4 distinct centroid blocks; a quarter of the row blocks have exactly 4 and the others exactly 1.
All inputs are finite; a program needn't handle non-finite values.
Results may differ from the reference program's by a relative error of at most 0.0003.
Values may be sent and summed in bfloat16 or wider, within the bound.
A program may use at most 128 MiB of HBM per device.

```python
import math
import jax
import jax.numpy as jnp
from jax import lax

D = 2048
K = 2048
RB = 512
CB = 256
N = 16384
NRB = 32
NCB = 8
P_SIZE = 56


def pair_layout(key):
    base_key = jax.random.fold_in(key, 11)
    ranking = jax.random.permutation(jax.random.fold_in(base_key, 1), NRB)
    heavy_rows = (ranking < NRB // 4).astype(jnp.int32)
    pair_counts = 1 + 3 * heavy_rows
    order_key = jax.random.fold_in(base_key, 2)
    row_keys = jax.vmap(lambda index_row: jax.random.fold_in(order_key, index_row))(jnp.arange(NRB))
    block_order = jax.vmap(lambda one_key: jax.random.permutation(one_key, NCB))(row_keys)[:, :4]
    return (pair_counts, block_order.astype(jnp.int32))


def centroid_values(key):
    value_key = jax.random.fold_in(key, 22)
    drawn = 1.5 * jax.random.normal(value_key, (K, D), jnp.float32)
    return jnp.clip(drawn, -9.0, 9.0).astype(jnp.bfloat16).astype(jnp.float32)


def draw_pair_list(key, part):
    pair_counts, block_order = pair_layout(key)
    slot_index = jnp.arange(4, dtype=jnp.int32)
    live_slots = (slot_index[None, :] < pair_counts[:, None]).reshape(-1)
    picked = jnp.nonzero(live_slots, size=P_SIZE)[0]
    row_ids = jnp.repeat(jnp.arange(NRB, dtype=jnp.int32), 4)
    return jnp.stack([row_ids[picked], block_order.reshape(-1)[picked]], axis=1).astype(jnp.int32)


def draw_centroids(key, part):
    return centroid_values(key).astype(jnp.bfloat16)


def draw_embeddings(key, part):
    value_key = jax.random.fold_in(key, 33)
    drawn = jax.random.normal(value_key, (N, D), jnp.float32)
    drawn = jnp.clip(drawn, -6.0, 6.0)
    return jnp.clip(drawn, -64.0, 64.0).astype(jnp.bfloat16)


def setup_inputs(seed: int = 0, part: int = 0) -> dict:
    key_of = jax.random.split(jax.random.key(seed), 4)
    own_keys = jax.random.split(jax.random.fold_in(key_of[3], part), 4)
    return {
        "embeddings": draw_embeddings(jax.random.fold_in(jax.random.fold_in(key_of[3], part), 71), part),
        "centroids": draw_centroids(jax.random.fold_in(jax.random.fold_in(key_of[3], part), 71), part),
        "pair_list": draw_pair_list(jax.random.fold_in(jax.random.fold_in(key_of[3], part), 71), part),
    }


def reference(embeddings, centroids, pair_list):
    row_data = embeddings.astype(jnp.float32)
    centroid_f32 = centroids.astype(jnp.float32)
    offsets = 0.5 * lax.optimization_barrier(jnp.sum(centroid_f32 * centroid_f32, axis=1))
    score_scale = 1.0 / math.sqrt(D)

    def score_tile(pair_entry):
        row_block = pair_entry[0].astype(jnp.int32)
        col_block = pair_entry[1].astype(jnp.int32)
        row_part = lax.dynamic_slice_in_dim(row_data, row_block * RB, RB, 0)
        block_rows = lax.dynamic_slice_in_dim(centroid_f32, col_block * CB, CB, 0)
        block_offs = lax.dynamic_slice_in_dim(offsets, col_block * CB, CB, 0)
        raw_scores = jnp.dot(row_part, block_rows.T, precision=lax.Precision.HIGHEST)
        return (row_part, (raw_scores - block_offs[None, :]) * score_scale)

    def first_pass(state_now, pair_entry):
        running_max, running_sum = state_now
        row_block = pair_entry[0].astype(jnp.int32)
        row_part, scores = score_tile(pair_entry)
        old_max = lax.dynamic_slice_in_dim(running_max, row_block * RB, RB, 0)
        old_sum = lax.dynamic_slice_in_dim(running_sum, row_block * RB, RB, 0)
        new_max = jnp.maximum(old_max, lax.optimization_barrier(jnp.max(scores, axis=1)))
        new_sum = old_sum * jnp.exp(old_max - new_max) + lax.optimization_barrier(jnp.sum(jnp.exp(scores - new_max[:, None]), axis=1))
        running_max = lax.dynamic_update_slice_in_dim(running_max, new_max, row_block * RB, 0)
        running_sum = lax.dynamic_update_slice_in_dim(running_sum, new_sum, row_block * RB, 0)
        return ((running_max, running_sum), None)
    start_state = (jnp.full((N,), -1e+30, jnp.float32), jnp.zeros((N,), jnp.float32))
    (running_max, running_sum), _ = lax.scan(first_pass, start_state, pair_list)
    log_norm = running_max + jnp.log(running_sum)

    def second_pass(state_now, pair_entry):
        numerator, denominator = state_now
        row_block = pair_entry[0].astype(jnp.int32)
        col_block = pair_entry[1].astype(jnp.int32)
        row_part, scores = score_tile(pair_entry)
        row_norm = lax.dynamic_slice_in_dim(log_norm, row_block * RB, RB, 0)
        weights = jnp.exp(scores - row_norm[:, None]).astype(jnp.bfloat16)
        weights = lax.optimization_barrier(weights).astype(jnp.float32)
        term_tile = jnp.dot(weights.T, row_part, precision=lax.Precision.HIGHEST)
        mass_tile = lax.optimization_barrier(jnp.sum(weights, axis=0))
        old_num = lax.dynamic_slice_in_dim(numerator, col_block * CB, CB, 0)
        old_den = lax.dynamic_slice_in_dim(denominator, col_block * CB, CB, 0)
        numerator = lax.dynamic_update_slice_in_dim(numerator, old_num + term_tile, col_block * CB, 0)
        denominator = lax.dynamic_update_slice_in_dim(denominator, old_den + mass_tile, col_block * CB, 0)
        return ((numerator, denominator), None)
    sums_start = (jnp.zeros((K, D), jnp.float32), jnp.zeros((K,), jnp.float32))
    (numerator, denominator), _ = lax.scan(second_pass, sums_start, pair_list)
    new_centroids = (numerator + 16.0 * centroid_f32) / (denominator[:, None] + 16.0)
    return (new_centroids, log_norm)
```

```python
import functools
import math

import jax
import jax.numpy as jnp
from jax import lax
from jax.experimental import pallas as pl
from jax.experimental.pallas import tpu as pltpu
from jax.sharding import PartitionSpec as P

D = 2048
K = 2048
RB = 512
CB = 256
NCB = K // CB
SLOTS = 4
PARTS = 8
PIECES = 8
CHUNKS = 4

neg_big = -1e30
prior_mass = 16.0
MESH = pl.DeviceIdType.MESH


def meet(peers):
    barrier = pltpu.get_barrier_semaphore()
    for peer in peers:
        pl.semaphore_signal(barrier, inc=1, device_id=peer, device_id_type=MESH)
    pl.semaphore_wait(barrier, len(peers))


def fetch_kernel(
    nb, nf, emb_ref, cen_ref, rows_ref, all_ref, row_send, row_recv, send, recv, own_sem,
    emb_hold, cen_hold,
):
    z = lax.axis_index("blk")
    f = lax.axis_index("feat")
    nx = nf // 2
    c = lax.rem(f, 2)
    x = f // 2
    rows, width = rows_ref.shape[0], emb_ref.shape[1]
    half = cen_ref.shape[0] // 2
    thin = D * 3 // 8 // nx // 128 * 128
    wide = D - nx * thin
    sibling = x * 2 + 1 - c

    def across(dx):
        return lax.rem(x + dx, nx)

    meet(
        [{"blk": z, "feat": lax.rem(f + d, nf)} for d in range(1, nf)]
        + [{"blk": lax.rem(z + d, nb), "feat": f} for d in range(1, nb)]
    )

    def spot(zz, cc, col, size):
        return all_ref.at[
            pl.ds(pl.multiple_of(zz * 2 * half + cc * half, half), half),
            pl.ds(pl.multiple_of(col, 128), size),
        ]

    def remote(src, dst, kind, d, blk, feat):
        return pltpu.make_async_remote_copy(
            src_ref=src,
            dst_ref=dst,
            send_sem=send.at[kind, d],
            recv_sem=recv.at[kind, d],
            device_id={"blk": blk, "feat": feat},
            device_id_type=MESH,
        )

    def own_part(col, size):
        return cen_ref.at[
            pl.ds(pl.multiple_of(c * half, half), half), pl.ds(pl.multiple_of(col, 128), size)
        ]

    thin_col = wide + x * thin
    started = []

    def go(cond, copy):
        pl.when(cond)(copy.start)
        started.append((cond, copy))

    def row_copy(d, piece):
        to = lax.rem(f + d, nf)
        size = rows // PIECES
        return pltpu.make_async_remote_copy(
            src_ref=emb_ref.at[pl.ds(pl.multiple_of(to * rows + piece * size, size), size), :],
            dst_ref=rows_ref.at[
                pl.ds(piece * size, size), pl.ds(pl.multiple_of(f * width, width), width)
            ],
            send_sem=row_send.at[d, piece],
            recv_sem=row_recv.at[d, piece],
            device_id={"blk": z, "feat": to},
            device_id_type=MESH,
        )

    def step(way):
        return jnp.clip(z + 1 - 2 * way, 0, nb - 1)

    def onward(way):
        return (z + 1 < nb) if way == 0 else (z > 0)

    for way in range(2):
        go(
            onward(way),
            remote(own_part(thin_col, thin), spot(z, c, thin_col, thin), 1, way * nb + 1, step(way), f),
        )
    for way in range(2):
        go(onward(way), remote(own_part(0, wide), spot(z, c, 0, wide), 0, way * nb + 1, step(way), f))
    row_copies = [row_copy(d, piece) for piece in range(PIECES) for d in range(1, nf)]
    for copy in row_copies:
        copy.start()
    holds = [
        (
            emb_ref.at[pl.ds(pl.multiple_of(f * rows, rows), rows), :],
            emb_hold,
            rows_ref.at[:, pl.ds(pl.multiple_of(f * width, width), width)],
        ),
        (
            cen_ref,
            cen_hold,
            all_ref.at[pl.ds(pl.multiple_of(z * 2 * half, half), 2 * half), :],
        ),
    ]
    loads = [pltpu.make_async_copy(src, hold, own_sem.at[i]) for i, (src, hold, _) in enumerate(holds)]
    stores = [
        pltpu.make_async_copy(hold, dst, own_sem.at[2 + i]) for i, (_, hold, dst) in enumerate(holds)
    ]
    for copy in loads:
        copy.start()
    for load, store in zip(loads, stores):
        load.wait()
        store.start()

    def source(way, hop):
        zz = z - hop if way == 0 else z + hop
        return (zz >= 0) if way == 0 else (zz < nb), jnp.clip(zz, 0, nb - 1)

    def arrived(cond, kind, d, zz, cc, col, size):
        here = spot(zz, cc, col, size)
        pl.when(cond)(remote(here, here, kind, d, z, sibling).wait_recv)
        return here

    turns = [(way, hop) for hop in range(1, nb) for way in range(2)]

    def pass_thin(way, hop):
        cond, zz = source(way, hop)
        d = way * nb + hop
        here = arrived(cond, 1, d, zz, c, thin_col, thin)
        if hop + 1 < nb:
            go(jnp.logical_and(cond, onward(way)), remote(here, here, 1, d + 1, step(way), f))
        for dx in range(1, nx):
            go(cond, remote(here, here, 4 + dx, d, z, across(dx) * 2 + c))
        go(cond, remote(here, here, 3, d, z, sibling))

    def pass_wide(way, hop):
        cond, zz = source(way, hop)
        d = way * nb + hop
        here = arrived(cond, 0, d, zz, c, 0, wide)
        if hop + 1 < nb:
            go(jnp.logical_and(cond, onward(way)), remote(here, here, 0, d + 1, step(way), f))
        go(cond, remote(here, here, 2, d, z, sibling))

    def pass_across(way, hop):
        cond, zz = source(way, hop)
        d = way * nb + hop
        for dx in range(1, nx):
            col = wide + lax.rem(x + nx - dx, nx) * thin
            here = arrived(cond, 4 + dx, d, zz, c, col, thin)
            go(cond, remote(here, here, 4 + nx + dx, d, z, sibling))

    for hop in range(1, nb):
        for way in range(2):
            pass_thin(way, hop)
        for way in range(2):
            pass_wide(way, hop)
    for way, hop in turns:
        pass_across(way, hop)
    for way, hop in turns:
        cond, zz = source(way, hop)
        d = way * nb + hop
        arrived(cond, 2, d, zz, 1 - c, 0, wide)
        arrived(cond, 3, d, zz, 1 - c, thin_col, thin)
        for dx in range(1, nx):
            col = wide + lax.rem(x + nx - dx, nx) * thin
            arrived(cond, 4 + nx + dx, d, zz, 1 - c, col, thin)
    for copy in stores:
        copy.wait()
    for copy in row_copies:
        copy.wait()
    for cond, copy in started:
        pl.when(cond)(copy.wait_send)


def fetch(embeddings, centroids, nb, nf):
    rows = embeddings.shape[0] // nf
    kinds = 4 + 2 * (nf // 2) + 1
    return pl.pallas_call(
        functools.partial(fetch_kernel, nb, nf),
        out_shape=(
            jax.ShapeDtypeStruct((rows, D), jnp.bfloat16),
            jax.ShapeDtypeStruct((K, D), jnp.bfloat16),
        ),
        in_specs=[pl.BlockSpec(memory_space=pltpu.HBM)] * 2,
        out_specs=(pl.BlockSpec(memory_space=pl.ANY),) * 2,
        scratch_shapes=[
            pltpu.SemaphoreType.DMA((nf, PIECES)),
            pltpu.SemaphoreType.DMA((nf, PIECES)),
            pltpu.SemaphoreType.DMA((kinds, 2 * nb)),
            pltpu.SemaphoreType.DMA((kinds, 2 * nb)),
            pltpu.SemaphoreType.DMA((4,)),
            pltpu.VMEM((rows, D // nf), jnp.bfloat16),
            pltpu.VMEM((K // nb, D), jnp.bfloat16),
        ],
        compiler_params=pltpu.CompilerParams(
            collective_id=0, has_side_effects=True, vmem_limit_bytes=6 * 2**20
        ),
        name="fetch",
    )(embeddings, centroids)


def term_kernel(nb, nf, tab_ref, rows_ref, all_ref, num_ref, mass_ref, norm_ref, score_ref, weight_ref, acc_ref, row_mass):
    local = rows_ref.shape[0] // RB
    scale = 1.0 / math.sqrt(D)
    own = K // (nb * nf)
    nx = nf // 2
    transposed = (((1,), (1,)), ((), ()))

    for r in range(local):
        part = rows_ref[r * RB : (r + 1) * RB, :]
        count = tab_ref[r, 0]

        def score_turn(slot, top):
            col = tab_ref[r, 1 + slot]
            panel = all_ref[pl.ds(pl.multiple_of(col * CB, CB), CB), :]
            wide = panel.astype(jnp.float32)
            offs = 0.5 * jnp.sum(wide * wide, axis=1, keepdims=True)
            raw = lax.dot_general(panel, part, transposed, preferred_element_type=jnp.float32)
            scores = (raw - offs) * scale
            score_ref[slot] = scores
            return jnp.maximum(top, jnp.max(scores, axis=0, keepdims=True))

        top = lax.fori_loop(0, count, score_turn, jnp.full((1, RB), neg_big, jnp.float32))

        def sum_turn(slot, total):
            return total + jnp.sum(jnp.exp(score_ref[slot] - top), axis=0, keepdims=True)

        total = lax.fori_loop(0, count, sum_turn, jnp.zeros((1, RB), jnp.float32))
        norm = top + jnp.log(total)
        norm_ref[r] = norm

        def weight_turn(slot, carry):
            col = tab_ref[r, 1 + slot]
            weight_ref[r, col] = jnp.exp(score_ref[slot] - norm).astype(jnp.bfloat16)
            return carry

        lax.fori_loop(0, count, weight_turn, 0)

    def col_turn(col, carry):
        acc_ref[...] = jnp.zeros_like(acc_ref)
        row_mass[...] = jnp.zeros_like(row_mass)
        for r in range(local):
            hit = jnp.int32(0)
            for slot in range(SLOTS):
                found = jnp.logical_and(tab_ref[r, 1 + slot] == col, slot < tab_ref[r, 0])
                hit = hit + found.astype(jnp.int32)

            @pl.when(hit > 0)
            def _():
                weights = weight_ref[r, col]
                acc_ref[...] += jnp.dot(
                    weights, rows_ref[r * RB : (r + 1) * RB, :], preferred_element_type=jnp.float32
                )
                row_mass[...] += lax.dot_general(
                    jnp.ones((8, RB), jnp.bfloat16),
                    weights,
                    transposed,
                    preferred_element_type=jnp.float32,
                )

        for j in range(CB // own):
            owner = col * (CB // own) + j
            zz, ff = owner // nf, lax.rem(owner, nf)
            num_ref[lax.rem(ff, 2), ff // 2, zz] = acc_ref[j * own : (j + 1) * own, :].astype(
                jnp.bfloat16
            )
            mass_ref[owner] = row_mass[:, j * own : (j + 1) * own]
        return carry

    lax.fori_loop(0, NCB, col_turn, 0)


def terms(table, row_data, panels, nb, nf):
    local = row_data.shape[0] // RB
    own = K // (nb * nf)
    vmem = pl.BlockSpec(memory_space=pltpu.VMEM)
    return pl.pallas_call(
        functools.partial(term_kernel, nb, nf),
        out_shape=(
            jax.ShapeDtypeStruct((2, nf // 2, nb, own, D), jnp.bfloat16),
            jax.ShapeDtypeStruct((nb * nf, 8, own), jnp.float32),
            jax.ShapeDtypeStruct((local, 1, RB), jnp.float32),
        ),
        in_specs=[pl.BlockSpec(memory_space=pltpu.SMEM), vmem, vmem],
        out_specs=(vmem,) * 3,
        scratch_shapes=[
            pltpu.VMEM((SLOTS, CB, RB), jnp.float32),
            pltpu.VMEM((local, NCB, CB, RB), jnp.bfloat16),
            pltpu.VMEM((CB, D), jnp.float32),
            pltpu.VMEM((8, CB), jnp.float32),
        ],
        compiler_params=pltpu.CompilerParams(vmem_limit_bytes=32 * 2**20),
        name="terms",
    )(table, row_data, panels)


def reduce_kernel(
    nb, nf, num_ref, mass_ref, out_ref, out_mass,
    from_sib, to_x, from_x, to_z, from_z, from_mass,
    a_send, a_recv, b_send, b_recv, c_send, c_recv, m_send, m_recv,
):
    z = lax.axis_index("blk")
    f = lax.axis_index("feat")
    nx = nf // 2
    n = nb * nf
    me = z * nf + f
    c = lax.rem(f, 2)
    x = f // 2
    sibling = x * 2 + 1 - c
    size = D // PARTS

    def at_offset(d):
        other = lax.rem(me + d, n)
        return {"blk": other // nf, "feat": lax.rem(other, nf)}

    barrier = pltpu.get_barrier_semaphore()

    def greet(d, carry):
        pl.semaphore_signal(barrier, inc=1, device_id=at_offset(d), device_id_type=MESH)
        return carry

    lax.fori_loop(1, n, greet, 0)
    pl.semaphore_wait(barrier, n - 1)

    def cols(t):
        return pl.ds(t * size, size)

    def a_copy(dx, t):
        xx = lax.rem(x + dx, nx)
        return pltpu.make_async_remote_copy(
            src_ref=num_ref.at[1 - c, xx, :, :, cols(t)],
            dst_ref=from_sib.at[xx, :, :, cols(t)],
            send_sem=a_send.at[dx, t],
            recv_sem=a_recv.at[dx, t],
            device_id={"blk": z, "feat": sibling},
            device_id_type=MESH,
        )

    def b_copy(dx, t):
        return pltpu.make_async_remote_copy(
            src_ref=to_x.at[dx - 1, :, :, cols(t)],
            dst_ref=from_x.at[dx - 1, :, :, cols(t)],
            send_sem=b_send.at[dx, t],
            recv_sem=b_recv.at[dx, t],
            device_id={"blk": z, "feat": lax.rem(x + dx, nx) * 2 + c},
            device_id_type=MESH,
        )

    def c_copy(d, t):
        return pltpu.make_async_remote_copy(
            src_ref=to_z.at[d - 1, :, cols(t)],
            dst_ref=from_z.at[d - 1, :, cols(t)],
            send_sem=c_send.at[d, t],
            recv_sem=c_recv.at[d, t],
            device_id={"blk": lax.rem(z + d, nb), "feat": f},
            device_id_type=MESH,
        )

    def m_copy(d):
        return pltpu.make_async_remote_copy(
            src_ref=mass_ref.at[lax.rem(me + d, n)],
            dst_ref=from_mass.at[d],
            send_sem=m_send.at[d],
            recv_sem=m_recv.at[d],
            device_id=at_offset(d),
            device_id_type=MESH,
        )

    def wide(value):
        return value.astype(jnp.float32)

    for t in range(PARTS):
        for dx in range(1, nx):
            a_copy(dx, t).start()
    for t in range(PARTS):
        a_copy(0, t).start()

    def mass_start(d, carry):
        m_copy(d).start()
        return carry

    lax.fori_loop(1, n, mass_start, 0)

    for t in range(PARTS):
        for dx in range(1, nx):
            xx = lax.rem(x + dx, nx)
            a_copy(dx, t).wait()
            for zz in range(nb):
                to_x[dx - 1, zz, :, cols(t)] = (
                    wide(num_ref[c, xx, zz, :, cols(t)]) + wide(from_sib[xx, zz, :, cols(t)])
                ).astype(jnp.bfloat16)
            b_copy(dx, t).start()

    def blk_sum(zz, t):
        total = wide(num_ref[c, x, zz, :, cols(t)]) + wide(from_sib[x, zz, :, cols(t)])
        for dx in range(1, nx):
            total = total + wide(from_x[dx - 1, zz, :, cols(t)])
        return total

    for t in range(PARTS):
        a_copy(0, t).wait()
        for dx in range(1, nx):
            b_copy(dx, t).wait()
        for d in range(1, nb):
            to_z[d - 1, :, cols(t)] = blk_sum(lax.rem(z + d, nb), t).astype(jnp.bfloat16)
            c_copy(d, t).start()
        out_ref[:, cols(t)] = blk_sum(z, t)

    def mass_end(d, total):
        m_copy(d).wait()
        return total + from_mass[d]

    out_mass[...] = lax.fori_loop(1, n, mass_end, mass_ref[me])

    for t in range(PARTS):
        total = out_ref[:, cols(t)]
        for d in range(1, nb):
            c_copy(d, t).wait()
            total = total + wide(from_z[d - 1, :, cols(t)])
        out_ref[:, cols(t)] = total


def reduce_sums(num, mass, nb, nf):
    own = K // (nb * nf)
    nx = nf // 2
    n = nb * nf
    vmem = pl.BlockSpec(memory_space=pltpu.VMEM)
    dma = pltpu.SemaphoreType.DMA
    return pl.pallas_call(
        functools.partial(reduce_kernel, nb, nf),
        out_shape=(
            jax.ShapeDtypeStruct((own, D), jnp.float32),
            jax.ShapeDtypeStruct((8, own), jnp.float32),
        ),
        in_specs=[vmem] * 2,
        out_specs=(vmem,) * 2,
        scratch_shapes=[
            pltpu.VMEM((nx, nb, own, D), jnp.bfloat16),
            pltpu.VMEM((nx - 1, nb, own, D), jnp.bfloat16),
            pltpu.VMEM((nx - 1, nb, own, D), jnp.bfloat16),
            pltpu.VMEM((nb - 1, own, D), jnp.bfloat16),
            pltpu.VMEM((nb - 1, own, D), jnp.bfloat16),
            pltpu.VMEM((n, 8, own), jnp.float32),
        ]
        + [dma((nx, PARTS))] * 4
        + [dma((nb, PARTS))] * 2
        + [dma((n,))] * 2,
        compiler_params=pltpu.CompilerParams(
            collective_id=1, has_side_effects=True, vmem_limit_bytes=24 * 2**20
        ),
        name="reduce_sums",
    )(num, mass)


def fused_kernel(
    nb, nf, allow_ref, emb_ref, cen_ref, num_ref, mass_ref, norm_ref,
    rows_ref, all_ref, offs_ref, score_ref, top_ref, sum_ref, weight_ref, keep_ref,
    to_sib, from_sib, to_x, from_x, part_ref, to_z, from_z, to_mass, from_mass,
    row_send, row_recv, send, recv, own_sem, a_send, a_recv, b_send, b_recv, z_send, z_recv,
    m_send, m_recv,
):
    z = lax.axis_index("blk")
    f = lax.axis_index("feat")
    nx = nf // 2
    n = nb * nf
    me = z * nf + f
    c = lax.rem(f, 2)
    x = f // 2
    rows, width = rows_ref.shape[0], emb_ref.shape[1]
    local = rows // RB
    per = K // nb // CB
    half = cen_ref.shape[0] // 2
    own = K // n
    thin = D * 3 // 8 // nx // 128 * 128
    wide = D - nx * thin
    sibling = x * 2 + 1 - c
    size = D // CHUNKS
    scale = 1.0 / math.sqrt(D)
    transposed = (((1,), (1,)), ((), ()))

    def at_offset(d):
        other = lax.rem(me + d, n)
        return {"blk": other // nf, "feat": lax.rem(other, nf)}

    barrier = pltpu.get_barrier_semaphore()

    def greet(d, carry):
        pl.semaphore_signal(barrier, inc=1, device_id=at_offset(d), device_id_type=MESH)
        return carry

    lax.fori_loop(1, n, greet, 0)
    pl.semaphore_wait(barrier, n - 1)

    def across(dx):
        return lax.rem(x + dx, nx)

    def spot(zz, cc, col, count):
        return all_ref.at[
            pl.ds(pl.multiple_of(zz * 2 * half + cc * half, half), half),
            pl.ds(pl.multiple_of(col, 128), count),
        ]

    def remote(src, dst, kind, d, blk, feat):
        return pltpu.make_async_remote_copy(
            src_ref=src,
            dst_ref=dst,
            send_sem=send.at[kind, d],
            recv_sem=recv.at[kind, d],
            device_id={"blk": blk, "feat": feat},
            device_id_type=MESH,
        )

    def own_part(col, count):
        return cen_ref.at[
            pl.ds(pl.multiple_of(c * half, half), half), pl.ds(pl.multiple_of(col, 128), count)
        ]

    thin_col = wide + x * thin
    started = []

    def go(cond, copy):
        pl.when(cond)(copy.start)
        started.append((cond, copy))

    piece_rows = rows // PIECES

    def row_copy(d, piece):
        to = lax.rem(f + d, nf)
        return pltpu.make_async_remote_copy(
            src_ref=emb_ref.at[
                pl.ds(pl.multiple_of(to * rows + piece * piece_rows, piece_rows), piece_rows), :
            ],
            dst_ref=rows_ref.at[
                pl.ds(piece * piece_rows, piece_rows),
                pl.ds(pl.multiple_of(f * width, width), width),
            ],
            send_sem=row_send.at[d, piece],
            recv_sem=row_recv.at[d, piece],
            device_id={"blk": z, "feat": to},
            device_id_type=MESH,
        )

    def step(way):
        return jnp.clip(z + 1 - 2 * way, 0, nb - 1)

    def onward(way):
        return (z + 1 < nb) if way == 0 else (z > 0)

    def source(way, hop):
        zz = z - hop if way == 0 else z + hop
        return (zz >= 0) if way == 0 else (zz < nb), jnp.clip(zz, 0, nb - 1)

    def arrived(cond, kind, d, zz, cc, col, count):
        here = spot(zz, cc, col, count)
        pl.when(cond)(remote(here, here, kind, d, z, sibling).wait_recv)
        return here

    def pass_thin(way, hop):
        cond, zz = source(way, hop)
        d = way * nb + hop
        here = arrived(cond, 1, d, zz, c, thin_col, thin)
        if hop + 1 < nb:
            go(jnp.logical_and(cond, onward(way)), remote(here, here, 1, d + 1, step(way), f))
        for dx in range(1, nx):
            go(cond, remote(here, here, 4 + dx, d, z, across(dx) * 2 + c))
        go(cond, remote(here, here, 3, d, z, sibling))

    def pass_wide(way, hop):
        cond, zz = source(way, hop)
        d = way * nb + hop
        here = arrived(cond, 0, d, zz, c, 0, wide)
        if hop + 1 < nb:
            go(jnp.logical_and(cond, onward(way)), remote(here, here, 0, d + 1, step(way), f))
        go(cond, remote(here, here, 2, d, z, sibling))

    def pass_across(way, hop):
        cond, zz = source(way, hop)
        d = way * nb + hop
        for dx in range(1, nx):
            col = wide + lax.rem(x + nx - dx, nx) * thin
            here = arrived(cond, 4 + dx, d, zz, c, col, thin)
            go(cond, remote(here, here, 4 + nx + dx, d, z, sibling))

    def complete(way, hop):
        cond, zz = source(way, hop)
        d = way * nb + hop
        arrived(cond, 2, d, zz, 1 - c, 0, wide)
        arrived(cond, 3, d, zz, 1 - c, thin_col, thin)
        for dx in range(1, nx):
            col = wide + lax.rem(x + nx - dx, nx) * thin
            arrived(cond, 4 + nx + dx, d, zz, 1 - c, col, thin)

    def both(turn, hop):
        for way in range(2):
            turn(way, hop)

    def block_turns(hop_first, hop_last, turn):
        def one(t, carry):
            hop, rest = t // (2 * per), lax.rem(t, 2 * per)
            way, j = rest // per, lax.rem(rest, per)
            zz = z + (2 * way - 1) * hop
            fits = jnp.logical_and(zz >= 0, zz < nb)
            fits = jnp.logical_and(fits, jnp.logical_or(hop > 0, way == 0))

            @pl.when(fits)
            def _():
                turn(zz * per + j)

            return carry

        lax.fori_loop(hop_first * 2 * per, hop_last * 2 * per, one, 0)

    def offsets(hop):
        def turn(col):
            panel = all_ref[pl.ds(pl.multiple_of(col * CB, CB), CB), :].astype(jnp.float32)
            offs_ref[col] = 0.5 * jnp.sum(panel * panel, axis=1, keepdims=True)

        block_turns(hop, hop + 1, turn)

    def scores(hop_first, hop_last, row_first, row_last):
        def turn(col):
            def row_turn(r, carry):
                raw = lax.dot_general(
                    all_ref[pl.ds(pl.multiple_of(col * CB, CB), CB), :],
                    rows_ref[pl.ds(pl.multiple_of(r * RB, RB), RB), :],
                    transposed,
                    preferred_element_type=jnp.float32,
                )
                value = jnp.where(allow_ref[r, col] > 0, (raw - offs_ref[col]) * scale, neg_big)
                score_ref[r, col] = value
                old = top_ref[r]
                top = jnp.maximum(old, jnp.max(value, axis=0, keepdims=True))
                sum_ref[r] = sum_ref[r] * jnp.exp(old - top) + jnp.sum(
                    jnp.exp(value - top), axis=0, keepdims=True
                )
                top_ref[r] = top
                return carry

            lax.fori_loop(row_first, row_last, row_turn, 0)

        block_turns(hop_first, hop_last, turn)

    first_pieces = PIECES // local
    for way in range(2):
        go(
            onward(way),
            remote(own_part(thin_col, thin), spot(z, c, thin_col, thin), 1, way * nb + 1, step(way), f),
        )
    for way in range(2):
        go(onward(way), remote(own_part(0, wide), spot(z, c, 0, wide), 0, way * nb + 1, step(way), f))
    row_copies = [[row_copy(d, piece) for d in range(1, nf)] for piece in range(PIECES)]
    for piece in range(first_pieces):
        for copy in row_copies[piece]:
            copy.start()
    loads = [
        pltpu.make_async_copy(
            emb_ref.at[pl.ds(pl.multiple_of(f * rows, rows), rows), :],
            rows_ref.at[:, pl.ds(pl.multiple_of(f * width, width), width)],
            own_sem.at[0],
        ),
        pltpu.make_async_copy(
            cen_ref, all_ref.at[pl.ds(pl.multiple_of(z * 2 * half, half), 2 * half), :], own_sem.at[1]
        ),
    ]
    for copy in loads:
        copy.start()
    top_ref[...] = jnp.full_like(top_ref, neg_big)
    sum_ref[...] = jnp.zeros_like(sum_ref)
    both(pass_thin, 1)
    for piece in range(first_pieces, PIECES):
        for copy in row_copies[piece]:
            copy.start()
    for copy in loads:
        copy.wait()
    offsets(0)
    both(pass_wide, 1)
    both(pass_thin, 2)
    for piece in range(first_pieces):
        for copy in row_copies[piece]:
            copy.wait_recv()
    scores(0, 1, 0, 1)
    both(pass_across, 1)
    both(complete, 1)
    offsets(1)
    scores(1, 2, 0, 1)
    both(pass_wide, 2)
    for hop in range(3, nb):
        both(pass_thin, hop)
    for piece in range(first_pieces, PIECES):
        for copy in row_copies[piece]:
            copy.wait_recv()
    scores(0, 2, 1, local)
    for hop in range(2, nb):
        if hop > 2:
            both(pass_wide, hop)
        both(pass_across, hop)
        both(complete, hop)
        offsets(hop)
        scores(hop, hop + 1, 0, local)

    for r in range(local):
        norm = top_ref[r] + jnp.log(sum_ref[r])
        norm_ref[r] = norm
        top_ref[r] = norm

    def cols(t):
        return pl.ds(pl.multiple_of(t * size, size), size)

    left, right = jnp.int32(0), jnp.int32(nb - 1)
    turns = []
    for _ in range(nb):
        pick = (z - left) >= (right - z)
        turns.append(jnp.where(pick, left, right))
        left, right = jnp.where(pick, left + 1, left), jnp.where(pick, right, right - 1)

    def a_copy(q):
        return pltpu.make_async_remote_copy(
            src_ref=to_sib.at[q],
            dst_ref=from_sib.at[q],
            send_sem=a_send.at[q],
            recv_sem=a_recv.at[q],
            device_id={"blk": z, "feat": sibling},
            device_id_type=MESH,
        )

    def b_copy(i, t):
        return pltpu.make_async_remote_copy(
            src_ref=to_x.at[i, :, cols(t)],
            dst_ref=from_x.at[i, :, cols(t)],
            send_sem=b_send.at[i, t],
            recv_sem=b_recv.at[i, t],
            device_id={"blk": z, "feat": (1 - x) * 2 + c},
            device_id_type=MESH,
        )

    def z_copy(zz, way, t):
        return pltpu.make_async_remote_copy(
            src_ref=to_z.at[zz, :, cols(t)],
            dst_ref=from_z.at[way, zz, :, cols(t)],
            send_sem=z_send.at[zz, t],
            recv_sem=z_recv.at[way, zz, t],
            device_id={"blk": jnp.clip(z + 1 - 2 * way, 0, nb - 1), "feat": f},
            device_id_type=MESH,
        )

    def m_copy(d):
        return pltpu.make_async_remote_copy(
            src_ref=to_mass.at[lax.rem(me + d, n)],
            dst_ref=from_mass.at[d],
            send_sem=m_send.at[d],
            recv_sem=m_recv.at[d],
            device_id=at_offset(d),
            device_id_type=MESH,
        )

    def wide_of(value):
        return value.astype(jnp.float32)

    def place(i):
        zz = turns[nb - 1]
        for t in range(nb - 1):
            zz = jnp.where(i == t, turns[t], zz)
        return zz

    def sums(i, side):
        zz = place(i)
        xx = jnp.where(side == 0, 1 - x, x)
        q = side * nb + i
        col = zz * per + xx
        for cc in range(2):
            at = jnp.where(cc == 0, c, 1 - c)
            for r in range(local):
                value = score_ref[r, col, pl.ds(pl.multiple_of(at * own, own), own), :]
                weight_ref[cc * own : (cc + 1) * own, r * RB : (r + 1) * RB] = jnp.exp(
                    value - top_ref[r]
                ).astype(jnp.bfloat16)
        mass = lax.dot_general(
            jnp.ones((8, rows), jnp.bfloat16),
            weight_ref[...],
            transposed,
            preferred_element_type=jnp.float32,
        )
        to_mass[zz * nf + xx * 2 + c] = mass[:, :own]
        to_mass[zz * nf + xx * 2 + 1 - c] = mass[:, own:]

        def chunk(t, carry):
            total = jnp.dot(
                weight_ref[...], rows_ref[:, cols(t)], preferred_element_type=jnp.float32
            )
            keep_ref[q, :, cols(t)] = total[:own]
            to_sib[q, :, cols(t)] = total[own:].astype(jnp.bfloat16)
            return carry

        lax.fori_loop(0, CHUNKS, chunk, 0)
        a_copy(q).start()

    def send_x(i):
        a_copy(i).wait()

        def chunk(t, carry):
            to_x[i, :, cols(t)] = (
                keep_ref[i, :, cols(t)] + wide_of(from_sib[i, :, cols(t)])
            ).astype(jnp.bfloat16)
            b_copy(i, t).start()
            return carry

        lax.fori_loop(0, CHUNKS, chunk, 0)

    def send_z(i):
        zz = place(i)
        q = nb + i
        a_copy(q).wait()
        way = (zz < z).astype(jnp.int32)
        away = zz != z
        fed = jnp.logical_or(
            jnp.logical_and(zz > z, z > 0), jnp.logical_and(zz < z, z < nb - 1)
        )

        def chunk(t, carry):
            b_copy(i, t).wait()
            part_ref[...] = (
                keep_ref[q, :, cols(t)]
                + wide_of(from_sib[q, :, cols(t)])
                + wide_of(from_x[i, :, cols(t)])
            )

            @pl.when(fed)
            def _():
                z_copy(zz, way, t).wait_recv()
                part_ref[...] += wide_of(from_z[way, zz, :, cols(t)])

            @pl.when(away)
            def _():
                to_z[zz, :, cols(t)] = part_ref[...].astype(jnp.bfloat16)
                z_copy(zz, way, t).start()

            @pl.when(jnp.logical_not(away))
            def _():
                num_ref[:, cols(t)] = part_ref[...]

            return carry

        lax.fori_loop(0, CHUNKS, chunk, 0)

    def turn(i, carry):
        @pl.when(i < nb)
        def _():
            def one(side, carry):
                sums(i, side)

                @pl.when(side == 0)
                def _():
                    send_x(i)

                return carry

            lax.fori_loop(0, 2, one, 0)

        @pl.when(i == nb - 1)
        def _():
            def mass_start(d, carry):
                m_copy(d).start()
                return carry

            lax.fori_loop(1, n, mass_start, 0)

        @pl.when(i > 0)
        def _():
            send_z(i - 1)

        return carry

    lax.fori_loop(0, nb + 1, turn, 0)

    def mass_end(d, total):
        m_copy(d).wait()
        return total + from_mass[d]

    mass_ref[...] = lax.fori_loop(1, n, mass_end, to_mass[me])

    def last(t, carry):
        for way in range(2):

            @pl.when((z > 0) if way == 0 else (z < nb - 1))
            def _():
                z_copy(z, way, t).wait_recv()
                num_ref[:, cols(t)] += wide_of(from_z[way, z, :, cols(t)])

        for zz in range(nb):

            @pl.when(z != zz)
            def _():
                z_copy(zz, 0, t).wait_send()

        return carry

    lax.fori_loop(0, CHUNKS, last, 0)
    for group in row_copies:
        for copy in group:
            copy.wait_send()
    for cond, copy in started:
        pl.when(cond)(copy.wait_send)


def fused(allow, embeddings, centroids, nb, nf):
    rows = embeddings.shape[0] // nf
    local = rows // RB
    nx = nf // 2
    n = nb * nf
    own = K // n
    kinds = 4 + 2 * nx + 1
    vmem = pl.BlockSpec(memory_space=pltpu.VMEM)
    hbm = pl.BlockSpec(memory_space=pltpu.HBM)
    dma = pltpu.SemaphoreType.DMA
    bf16, f32 = jnp.bfloat16, jnp.float32
    return pl.pallas_call(
        functools.partial(fused_kernel, nb, nf),
        out_shape=(
            jax.ShapeDtypeStruct((own, D), f32),
            jax.ShapeDtypeStruct((8, own), f32),
            jax.ShapeDtypeStruct((local, 1, RB), f32),
        ),
        in_specs=[pl.BlockSpec(memory_space=pltpu.SMEM), hbm, hbm],
        out_specs=(vmem,) * 3,
        scratch_shapes=[
            pltpu.VMEM((rows, D), bf16),
            pltpu.VMEM((K, D), bf16),
            pltpu.VMEM((NCB, CB, 1), f32),
            pltpu.VMEM((local, NCB, CB, RB), f32),
            pltpu.VMEM((local, 1, RB), f32),
            pltpu.VMEM((local, 1, RB), f32),
            pltpu.VMEM((CB, rows), bf16),
            pltpu.VMEM((2 * nb, own, D), f32),
            pltpu.VMEM((2 * nb, own, D), bf16),
            pltpu.VMEM((2 * nb, own, D), bf16),
            pltpu.VMEM((nb, own, D), bf16),
            pltpu.VMEM((nb, own, D), bf16),
            pltpu.VMEM((own, D // CHUNKS), f32),
            pltpu.VMEM((nb, own, D), bf16),
            pltpu.VMEM((2, nb, own, D), bf16),
            pltpu.VMEM((n, 8, own), f32),
            pltpu.VMEM((n, 8, own), f32),
            dma((nf, PIECES)),
            dma((nf, PIECES)),
            dma((kinds, 2 * nb)),
            dma((kinds, 2 * nb)),
            dma((2,)),
            dma((2 * nb,)),
            dma((2 * nb,)),
            dma((nb, CHUNKS)),
            dma((nb, CHUNKS)),
            dma((nb, CHUNKS)),
            dma((2, nb, CHUNKS)),
            dma((n,)),
            dma((n,)),
        ],
        compiler_params=pltpu.CompilerParams(
            collective_id=2, has_side_effects=True, vmem_limit_bytes=58 * 2**20
        ),
        name="fused",
    )(allow, embeddings, centroids)


def body(embeddings, centroids, pair_list):
    nb, nf = lax.axis_size("blk"), lax.axis_size("feat")
    local_rows = embeddings.shape[0] // nf
    local_blocks = local_rows // RB
    device_index = lax.axis_index("blk") * nf + lax.axis_index("feat")
    mine = device_index * local_blocks + jnp.arange(local_blocks, dtype=jnp.int32)
    row_ids, col_ids = pair_list[:, 0], pair_list[:, 1]
    same = row_ids[None, :] == mine[:, None]
    if K // nb == 2 * CB and nf == 4 and local_blocks == 2:
        blocks = jnp.arange(NCB, dtype=jnp.int32)
        allow = jnp.sum(
            (same[:, None, :] & (col_ids[None, None, :] == blocks[None, :, None])).astype(jnp.int32),
            axis=2,
        )
        numerator, denominator, log_norm = fused(allow, embeddings, centroids, nb, nf)
    else:
        before = jnp.sum((row_ids[None, :] < mine[:, None]).astype(jnp.int32), axis=1)
        counts = jnp.sum(same.astype(jnp.int32), axis=1)
        rank = jnp.arange(row_ids.shape[0], dtype=jnp.int32)[None, :] - before[:, None]
        slots = jnp.arange(SLOTS, dtype=jnp.int32)
        picked = same[:, None, :] & (rank[:, None, :] == slots[None, :, None])
        chosen = jnp.sum(jnp.where(picked, col_ids[None, None, :], 0), axis=2)
        table = jnp.concatenate([counts[:, None], chosen], axis=1)
        row_data, panels = fetch(embeddings, centroids, nb, nf)
        num, mass, log_norm = terms(table, row_data, panels, nb, nf)
        numerator, denominator = reduce_sums(num, mass, nb, nf)

    own_count = centroids.shape[0] // nf
    own_rows = lax.dynamic_slice_in_dim(
        centroids, lax.axis_index("feat") * own_count, own_count, 0
    ).astype(jnp.float32)
    new_centroids = (numerator + prior_mass * own_rows) / (denominator[0][:, None] + prior_mass)
    return (new_centroids, log_norm.reshape(local_rows))


def solution(mesh):
    return jax.shard_map(
        body,
        mesh=mesh,
        in_specs=(P(("groups", "blk"), "feat"), P(("groups", "blk"), None), P("groups", None)),
        out_specs=(P(("groups", "blk", "feat"), None), P(("groups", "blk", "feat"))),
        check_vma=False,
    )
```

```python
import functools
import math

import jax
import jax.numpy as jnp
from jax import lax
from jax.experimental import pallas as pl
from jax.experimental.pallas import tpu as pltpu
from jax.sharding import PartitionSpec as P

D = 2048
K = 2048
RB = 512
CB = 256
NCB = K // CB
SLOTS = 4
PARTS = 8
PIECES = 8
CHUNKS = 8

neg_big = -1e30
prior_mass = 16.0
MESH = pl.DeviceIdType.MESH


def meet(peers):
    barrier = pltpu.get_barrier_semaphore()
    for peer in peers:
        pl.semaphore_signal(barrier, inc=1, device_id=peer, device_id_type=MESH)
    pl.semaphore_wait(barrier, len(peers))


def fetch_kernel(
    nb, nf, emb_ref, cen_ref, rows_ref, all_ref, row_send, row_recv, send, recv, own_sem,
    emb_hold, cen_hold,
):
    z = lax.axis_index("blk")
    f = lax.axis_index("feat")
    nx = nf // 2
    c = lax.rem(f, 2)
    x = f // 2
    rows, width = rows_ref.shape[0], emb_ref.shape[1]
    half = cen_ref.shape[0] // 2
    thin = D * 3 // 8 // nx // 128 * 128
    wide = D - nx * thin
    sibling = x * 2 + 1 - c

    def across(dx):
        return lax.rem(x + dx, nx)

    meet(
        [{"blk": z, "feat": lax.rem(f + d, nf)} for d in range(1, nf)]
        + [{"blk": lax.rem(z + d, nb), "feat": f} for d in range(1, nb)]
    )

    def spot(zz, cc, col, size):
        return all_ref.at[
            pl.ds(pl.multiple_of(zz * 2 * half + cc * half, half), half),
            pl.ds(pl.multiple_of(col, 128), size),
        ]

    def remote(src, dst, kind, d, blk, feat):
        return pltpu.make_async_remote_copy(
            src_ref=src,
            dst_ref=dst,
            send_sem=send.at[kind, d],
            recv_sem=recv.at[kind, d],
            device_id={"blk": blk, "feat": feat},
            device_id_type=MESH,
        )

    def own_part(col, size):
        return cen_ref.at[
            pl.ds(pl.multiple_of(c * half, half), half), pl.ds(pl.multiple_of(col, 128), size)
        ]

    thin_col = wide + x * thin
    started = []

    def go(cond, copy):
        pl.when(cond)(copy.start)
        started.append((cond, copy))

    def row_copy(d, piece):
        to = lax.rem(f + d, nf)
        size = rows // PIECES
        return pltpu.make_async_remote_copy(
            src_ref=emb_ref.at[pl.ds(pl.multiple_of(to * rows + piece * size, size), size), :],
            dst_ref=rows_ref.at[
                pl.ds(piece * size, size), pl.ds(pl.multiple_of(f * width, width), width)
            ],
            send_sem=row_send.at[d, piece],
            recv_sem=row_recv.at[d, piece],
            device_id={"blk": z, "feat": to},
            device_id_type=MESH,
        )

    def step(way):
        return jnp.clip(z + 1 - 2 * way, 0, nb - 1)

    def onward(way):
        return (z + 1 < nb) if way == 0 else (z > 0)

    for way in range(2):
        go(
            onward(way),
            remote(own_part(thin_col, thin), spot(z, c, thin_col, thin), 1, way * nb + 1, step(way), f),
        )
    for way in range(2):
        go(onward(way), remote(own_part(0, wide), spot(z, c, 0, wide), 0, way * nb + 1, step(way), f))
    row_copies = [row_copy(d, piece) for piece in range(PIECES) for d in range(1, nf)]
    for copy in row_copies:
        copy.start()
    holds = [
        (
            emb_ref.at[pl.ds(pl.multiple_of(f * rows, rows), rows), :],
            emb_hold,
            rows_ref.at[:, pl.ds(pl.multiple_of(f * width, width), width)],
        ),
        (
            cen_ref,
            cen_hold,
            all_ref.at[pl.ds(pl.multiple_of(z * 2 * half, half), 2 * half), :],
        ),
    ]
    loads = [pltpu.make_async_copy(src, hold, own_sem.at[i]) for i, (src, hold, _) in enumerate(holds)]
    stores = [
        pltpu.make_async_copy(hold, dst, own_sem.at[2 + i]) for i, (_, hold, dst) in enumerate(holds)
    ]
    for copy in loads:
        copy.start()
    for load, store in zip(loads, stores):
        load.wait()
        store.start()

    def source(way, hop):
        zz = z - hop if way == 0 else z + hop
        return (zz >= 0) if way == 0 else (zz < nb), jnp.clip(zz, 0, nb - 1)

    def arrived(cond, kind, d, zz, cc, col, size):
        here = spot(zz, cc, col, size)
        pl.when(cond)(remote(here, here, kind, d, z, sibling).wait_recv)
        return here

    turns = [(way, hop) for hop in range(1, nb) for way in range(2)]

    def pass_thin(way, hop):
        cond, zz = source(way, hop)
        d = way * nb + hop
        here = arrived(cond, 1, d, zz, c, thin_col, thin)
        if hop + 1 < nb:
            go(jnp.logical_and(cond, onward(way)), remote(here, here, 1, d + 1, step(way), f))
        for dx in range(1, nx):
            go(cond, remote(here, here, 4 + dx, d, z, across(dx) * 2 + c))
        go(cond, remote(here, here, 3, d, z, sibling))

    def pass_wide(way, hop):
        cond, zz = source(way, hop)
        d = way * nb + hop
        here = arrived(cond, 0, d, zz, c, 0, wide)
        if hop + 1 < nb:
            go(jnp.logical_and(cond, onward(way)), remote(here, here, 0, d + 1, step(way), f))
        go(cond, remote(here, here, 2, d, z, sibling))

    def pass_across(way, hop):
        cond, zz = source(way, hop)
        d = way * nb + hop
        for dx in range(1, nx):
            col = wide + lax.rem(x + nx - dx, nx) * thin
            here = arrived(cond, 4 + dx, d, zz, c, col, thin)
            go(cond, remote(here, here, 4 + nx + dx, d, z, sibling))

    for hop in range(1, nb):
        for way in range(2):
            pass_thin(way, hop)
        for way in range(2):
            pass_wide(way, hop)
    for way, hop in turns:
        pass_across(way, hop)
    for way, hop in turns:
        cond, zz = source(way, hop)
        d = way * nb + hop
        arrived(cond, 2, d, zz, 1 - c, 0, wide)
        arrived(cond, 3, d, zz, 1 - c, thin_col, thin)
        for dx in range(1, nx):
            col = wide + lax.rem(x + nx - dx, nx) * thin
            arrived(cond, 4 + nx + dx, d, zz, 1 - c, col, thin)
    for copy in stores:
        copy.wait()
    for copy in row_copies:
        copy.wait()
    for cond, copy in started:
        pl.when(cond)(copy.wait_send)


def fetch(embeddings, centroids, nb, nf):
    rows = embeddings.shape[0] // nf
    kinds = 4 + 2 * (nf // 2) + 1
    return pl.pallas_call(
        functools.partial(fetch_kernel, nb, nf),
        out_shape=(
            jax.ShapeDtypeStruct((rows, D), jnp.bfloat16),
            jax.ShapeDtypeStruct((K, D), jnp.bfloat16),
        ),
        in_specs=[pl.BlockSpec(memory_space=pltpu.HBM)] * 2,
        out_specs=(pl.BlockSpec(memory_space=pl.ANY),) * 2,
        scratch_shapes=[
            pltpu.SemaphoreType.DMA((nf, PIECES)),
            pltpu.SemaphoreType.DMA((nf, PIECES)),
            pltpu.SemaphoreType.DMA((kinds, 2 * nb)),
            pltpu.SemaphoreType.DMA((kinds, 2 * nb)),
            pltpu.SemaphoreType.DMA((4,)),
            pltpu.VMEM((rows, D // nf), jnp.bfloat16),
            pltpu.VMEM((K // nb, D), jnp.bfloat16),
        ],
        compiler_params=pltpu.CompilerParams(
            collective_id=0, has_side_effects=True, vmem_limit_bytes=6 * 2**20
        ),
        name="fetch",
    )(embeddings, centroids)


def term_kernel(nb, nf, tab_ref, rows_ref, all_ref, num_ref, mass_ref, norm_ref, score_ref, weight_ref, acc_ref, row_mass):
    local = rows_ref.shape[0] // RB
    scale = 1.0 / math.sqrt(D)
    own = K // (nb * nf)
    nx = nf // 2
    transposed = (((1,), (1,)), ((), ()))

    for r in range(local):
        part = rows_ref[r * RB : (r + 1) * RB, :]
        count = tab_ref[r, 0]

        def score_turn(slot, top):
            col = tab_ref[r, 1 + slot]
            panel = all_ref[pl.ds(pl.multiple_of(col * CB, CB), CB), :]
            wide = panel.astype(jnp.float32)
            offs = 0.5 * jnp.sum(wide * wide, axis=1, keepdims=True)
            raw = lax.dot_general(panel, part, transposed, preferred_element_type=jnp.float32)
            scores = (raw - offs) * scale
            score_ref[slot] = scores
            return jnp.maximum(top, jnp.max(scores, axis=0, keepdims=True))

        top = lax.fori_loop(0, count, score_turn, jnp.full((1, RB), neg_big, jnp.float32))

        def sum_turn(slot, total):
            return total + jnp.sum(jnp.exp(score_ref[slot] - top), axis=0, keepdims=True)

        total = lax.fori_loop(0, count, sum_turn, jnp.zeros((1, RB), jnp.float32))
        norm = top + jnp.log(total)
        norm_ref[r] = norm

        def weight_turn(slot, carry):
            col = tab_ref[r, 1 + slot]
            weight_ref[r, col] = jnp.exp(score_ref[slot] - norm).astype(jnp.bfloat16)
            return carry

        lax.fori_loop(0, count, weight_turn, 0)

    def col_turn(col, carry):
        acc_ref[...] = jnp.zeros_like(acc_ref)
        row_mass[...] = jnp.zeros_like(row_mass)
        for r in range(local):
            hit = jnp.int32(0)
            for slot in range(SLOTS):
                found = jnp.logical_and(tab_ref[r, 1 + slot] == col, slot < tab_ref[r, 0])
                hit = hit + found.astype(jnp.int32)

            @pl.when(hit > 0)
            def _():
                weights = weight_ref[r, col]
                acc_ref[...] += jnp.dot(
                    weights, rows_ref[r * RB : (r + 1) * RB, :], preferred_element_type=jnp.float32
                )
                row_mass[...] += lax.dot_general(
                    jnp.ones((8, RB), jnp.bfloat16),
                    weights,
                    transposed,
                    preferred_element_type=jnp.float32,
                )

        for j in range(CB // own):
            owner = col * (CB // own) + j
            zz, ff = owner // nf, lax.rem(owner, nf)
            num_ref[lax.rem(ff, 2), ff // 2, zz] = acc_ref[j * own : (j + 1) * own, :].astype(
                jnp.bfloat16
            )
            mass_ref[owner] = row_mass[:, j * own : (j + 1) * own]
        return carry

    lax.fori_loop(0, NCB, col_turn, 0)


def terms(table, row_data, panels, nb, nf):
    local = row_data.shape[0] // RB
    own = K // (nb * nf)
    vmem = pl.BlockSpec(memory_space=pltpu.VMEM)
    return pl.pallas_call(
        functools.partial(term_kernel, nb, nf),
        out_shape=(
            jax.ShapeDtypeStruct((2, nf // 2, nb, own, D), jnp.bfloat16),
            jax.ShapeDtypeStruct((nb * nf, 8, own), jnp.float32),
            jax.ShapeDtypeStruct((local, 1, RB), jnp.float32),
        ),
        in_specs=[pl.BlockSpec(memory_space=pltpu.SMEM), vmem, vmem],
        out_specs=(vmem,) * 3,
        scratch_shapes=[
            pltpu.VMEM((SLOTS, CB, RB), jnp.float32),
            pltpu.VMEM((local, NCB, CB, RB), jnp.bfloat16),
            pltpu.VMEM((CB, D), jnp.float32),
            pltpu.VMEM((8, CB), jnp.float32),
        ],
        compiler_params=pltpu.CompilerParams(vmem_limit_bytes=32 * 2**20),
        name="terms",
    )(table, row_data, panels)


def reduce_kernel(
    nb, nf, num_ref, mass_ref, out_ref, out_mass,
    from_sib, to_x, from_x, to_z, from_z, from_mass,
    a_send, a_recv, b_send, b_recv, c_send, c_recv, m_send, m_recv,
):
    z = lax.axis_index("blk")
    f = lax.axis_index("feat")
    nx = nf // 2
    n = nb * nf
    me = z * nf + f
    c = lax.rem(f, 2)
    x = f // 2
    sibling = x * 2 + 1 - c
    size = D // PARTS

    def at_offset(d):
        other = lax.rem(me + d, n)
        return {"blk": other // nf, "feat": lax.rem(other, nf)}

    barrier = pltpu.get_barrier_semaphore()

    def greet(d, carry):
        pl.semaphore_signal(barrier, inc=1, device_id=at_offset(d), device_id_type=MESH)
        return carry

    lax.fori_loop(1, n, greet, 0)
    pl.semaphore_wait(barrier, n - 1)

    def cols(t):
        return pl.ds(t * size, size)

    def a_copy(dx, t):
        xx = lax.rem(x + dx, nx)
        return pltpu.make_async_remote_copy(
            src_ref=num_ref.at[1 - c, xx, :, :, cols(t)],
            dst_ref=from_sib.at[xx, :, :, cols(t)],
            send_sem=a_send.at[dx, t],
            recv_sem=a_recv.at[dx, t],
            device_id={"blk": z, "feat": sibling},
            device_id_type=MESH,
        )

    def b_copy(dx, t):
        return pltpu.make_async_remote_copy(
            src_ref=to_x.at[dx - 1, :, :, cols(t)],
            dst_ref=from_x.at[dx - 1, :, :, cols(t)],
            send_sem=b_send.at[dx, t],
            recv_sem=b_recv.at[dx, t],
            device_id={"blk": z, "feat": lax.rem(x + dx, nx) * 2 + c},
            device_id_type=MESH,
        )

    def c_copy(d, t):
        return pltpu.make_async_remote_copy(
            src_ref=to_z.at[d - 1, :, cols(t)],
            dst_ref=from_z.at[d - 1, :, cols(t)],
            send_sem=c_send.at[d, t],
            recv_sem=c_recv.at[d, t],
            device_id={"blk": lax.rem(z + d, nb), "feat": f},
            device_id_type=MESH,
        )

    def m_copy(d):
        return pltpu.make_async_remote_copy(
            src_ref=mass_ref.at[lax.rem(me + d, n)],
            dst_ref=from_mass.at[d],
            send_sem=m_send.at[d],
            recv_sem=m_recv.at[d],
            device_id=at_offset(d),
            device_id_type=MESH,
        )

    def wide(value):
        return value.astype(jnp.float32)

    for t in range(PARTS):
        for dx in range(1, nx):
            a_copy(dx, t).start()
    for t in range(PARTS):
        a_copy(0, t).start()

    def mass_start(d, carry):
        m_copy(d).start()
        return carry

    lax.fori_loop(1, n, mass_start, 0)

    for t in range(PARTS):
        for dx in range(1, nx):
            xx = lax.rem(x + dx, nx)
            a_copy(dx, t).wait()
            for zz in range(nb):
                to_x[dx - 1, zz, :, cols(t)] = (
                    wide(num_ref[c, xx, zz, :, cols(t)]) + wide(from_sib[xx, zz, :, cols(t)])
                ).astype(jnp.bfloat16)
            b_copy(dx, t).start()

    def blk_sum(zz, t):
        total = wide(num_ref[c, x, zz, :, cols(t)]) + wide(from_sib[x, zz, :, cols(t)])
        for dx in range(1, nx):
            total = total + wide(from_x[dx - 1, zz, :, cols(t)])
        return total

    for t in range(PARTS):
        a_copy(0, t).wait()
        for dx in range(1, nx):
            b_copy(dx, t).wait()
        for d in range(1, nb):
            to_z[d - 1, :, cols(t)] = blk_sum(lax.rem(z + d, nb), t).astype(jnp.bfloat16)
            c_copy(d, t).start()
        out_ref[:, cols(t)] = blk_sum(z, t)

    def mass_end(d, total):
        m_copy(d).wait()
        return total + from_mass[d]

    out_mass[...] = lax.fori_loop(1, n, mass_end, mass_ref[me])

    for t in range(PARTS):
        total = out_ref[:, cols(t)]
        for d in range(1, nb):
            c_copy(d, t).wait()
            total = total + wide(from_z[d - 1, :, cols(t)])
        out_ref[:, cols(t)] = total


def reduce_sums(num, mass, nb, nf):
    own = K // (nb * nf)
    nx = nf // 2
    n = nb * nf
    vmem = pl.BlockSpec(memory_space=pltpu.VMEM)
    dma = pltpu.SemaphoreType.DMA
    return pl.pallas_call(
        functools.partial(reduce_kernel, nb, nf),
        out_shape=(
            jax.ShapeDtypeStruct((own, D), jnp.float32),
            jax.ShapeDtypeStruct((8, own), jnp.float32),
        ),
        in_specs=[vmem] * 2,
        out_specs=(vmem,) * 2,
        scratch_shapes=[
            pltpu.VMEM((nx, nb, own, D), jnp.bfloat16),
            pltpu.VMEM((nx - 1, nb, own, D), jnp.bfloat16),
            pltpu.VMEM((nx - 1, nb, own, D), jnp.bfloat16),
            pltpu.VMEM((nb - 1, own, D), jnp.bfloat16),
            pltpu.VMEM((nb - 1, own, D), jnp.bfloat16),
            pltpu.VMEM((n, 8, own), jnp.float32),
        ]
        + [dma((nx, PARTS))] * 4
        + [dma((nb, PARTS))] * 2
        + [dma((n,))] * 2,
        compiler_params=pltpu.CompilerParams(
            collective_id=1, has_side_effects=True, vmem_limit_bytes=24 * 2**20
        ),
        name="reduce_sums",
    )(num, mass)


def fused_kernel(
    nb, nf, allow_ref, emb_ref, cen_ref, num_ref, mass_ref, norm_ref,
    rows_ref, all_ref, offs_ref, score_ref, top_ref, sum_ref, weight_ref, keep_ref,
    to_sib, from_sib, to_x, from_x, part_ref, to_z, from_z, pair_ref, to_line, from_line,
    swap_out, swap_in, to_mass, from_mass,
    row_send, row_recv, send, recv, own_sem, a_send, a_recv, b_send, b_recv, z_send, z_recv,
    m_send, m_recv, swap_sem,
):
    z = lax.axis_index("blk")
    f = lax.axis_index("feat")
    nx = nf // 2
    n = nb * nf
    me = z * nf + f
    c = lax.rem(f, 2)
    x = f // 2
    rows, width = rows_ref.shape[0], emb_ref.shape[1]
    local = rows // RB
    per = K // nb // CB
    half = cen_ref.shape[0] // 2
    own = K // n
    thin = D * 3 // 8 // nx // 128 * 128
    wide = D - nx * thin
    sibling = x * 2 + 1 - c
    size = D // CHUNKS
    scale = 1.0 / math.sqrt(D)
    transposed = (((1,), (1,)), ((), ()))

    def at_offset(d):
        other = lax.rem(me + d, n)
        return {"blk": other // nf, "feat": lax.rem(other, nf)}

    barrier = pltpu.get_barrier_semaphore()

    def greet(d, carry):
        pl.semaphore_signal(barrier, inc=1, device_id=at_offset(d), device_id_type=MESH)
        return carry

    lax.fori_loop(1, n, greet, 0)
    pl.semaphore_wait(barrier, n - 1)

    def across(dx):
        return lax.rem(x + dx, nx)

    def spot(zz, cc, col, count):
        return all_ref.at[
            pl.ds(pl.multiple_of(zz * 2 * half + cc * half, half), half),
            pl.ds(pl.multiple_of(col, 128), count),
        ]

    def remote(src, dst, kind, d, blk, feat):
        return pltpu.make_async_remote_copy(
            src_ref=src,
            dst_ref=dst,
            send_sem=send.at[kind, d],
            recv_sem=recv.at[kind, d],
            device_id={"blk": blk, "feat": feat},
            device_id_type=MESH,
        )

    def own_part(col, count):
        return cen_ref.at[
            pl.ds(pl.multiple_of(c * half, half), half), pl.ds(pl.multiple_of(col, 128), count)
        ]

    thin_col = wide + x * thin
    started = []

    def go(cond, copy):
        pl.when(cond)(copy.start)
        started.append((cond, copy))

    piece_rows = rows // PIECES

    def row_copy(d, piece):
        to = lax.rem(f + d, nf)
        return pltpu.make_async_remote_copy(
            src_ref=emb_ref.at[
                pl.ds(pl.multiple_of(to * rows + piece * piece_rows, piece_rows), piece_rows), :
            ],
            dst_ref=rows_ref.at[
                pl.ds(piece * piece_rows, piece_rows),
                pl.ds(pl.multiple_of(f * width, width), width),
            ],
            send_sem=row_send.at[d, piece],
            recv_sem=row_recv.at[d, piece],
            device_id={"blk": z, "feat": to},
            device_id_type=MESH,
        )

    def step(way):
        return jnp.clip(z + 1 - 2 * way, 0, nb - 1)

    def onward(way):
        return (z + 1 < nb) if way == 0 else (z > 0)

    def source(way, hop):
        zz = z - hop if way == 0 else z + hop
        return (zz >= 0) if way == 0 else (zz < nb), jnp.clip(zz, 0, nb - 1)

    def arrived(cond, kind, d, zz, cc, col, count):
        here = spot(zz, cc, col, count)
        pl.when(cond)(remote(here, here, kind, d, z, sibling).wait_recv)
        return here

    def pass_thin(way, hop):
        cond, zz = source(way, hop)
        d = way * nb + hop
        here = arrived(cond, 1, d, zz, c, thin_col, thin)
        if hop + 1 < nb:
            go(jnp.logical_and(cond, onward(way)), remote(here, here, 1, d + 1, step(way), f))
        for dx in range(1, nx):
            go(cond, remote(here, here, 4 + dx, d, z, across(dx) * 2 + c))
        go(cond, remote(here, here, 3, d, z, sibling))

    def pass_wide(way, hop):
        cond, zz = source(way, hop)
        d = way * nb + hop
        here = arrived(cond, 0, d, zz, c, 0, wide)
        if hop + 1 < nb:
            go(jnp.logical_and(cond, onward(way)), remote(here, here, 0, d + 1, step(way), f))
        go(cond, remote(here, here, 2, d, z, sibling))

    def pass_across(way, hop):
        cond, zz = source(way, hop)
        d = way * nb + hop
        for dx in range(1, nx):
            col = wide + lax.rem(x + nx - dx, nx) * thin
            here = arrived(cond, 4 + dx, d, zz, c, col, thin)
            go(cond, remote(here, here, 4 + nx + dx, d, z, sibling))

    def complete(way, hop):
        cond, zz = source(way, hop)
        d = way * nb + hop
        arrived(cond, 2, d, zz, 1 - c, 0, wide)
        arrived(cond, 3, d, zz, 1 - c, thin_col, thin)
        for dx in range(1, nx):
            col = wide + lax.rem(x + nx - dx, nx) * thin
            arrived(cond, 4 + nx + dx, d, zz, 1 - c, col, thin)

    def both(turn, hop):
        for way in range(2):
            turn(way, hop)

    def block_turns(hop_first, hop_last, turn):
        def one(t, carry):
            hop, rest = t // (2 * per), lax.rem(t, 2 * per)
            way, j = rest // per, lax.rem(rest, per)
            zz = z + (2 * way - 1) * hop
            fits = jnp.logical_and(zz >= 0, zz < nb)
            fits = jnp.logical_and(fits, jnp.logical_or(hop > 0, way == 0))

            @pl.when(fits)
            def _():
                turn(zz * per + j)

            return carry

        lax.fori_loop(hop_first * 2 * per, hop_last * 2 * per, one, 0)

    def offsets(hop):
        def turn(col):
            panel = all_ref[pl.ds(pl.multiple_of(col * CB, CB), CB), :].astype(jnp.float32)
            offs_ref[col] = 0.5 * jnp.sum(panel * panel, axis=1, keepdims=True)

        block_turns(hop, hop + 1, turn)

    def scores(hop_first, hop_last, row_first, row_last):
        def turn(col):
            def row_turn(r, carry):
                raw = lax.dot_general(
                    all_ref[pl.ds(pl.multiple_of(col * CB, CB), CB), :],
                    rows_ref[pl.ds(pl.multiple_of(r * RB, RB), RB), :],
                    transposed,
                    preferred_element_type=jnp.float32,
                )
                value = jnp.where(allow_ref[r, col] > 0, (raw - offs_ref[col]) * scale, neg_big)
                score_ref[r, col] = value
                old = top_ref[r]
                top = jnp.maximum(old, jnp.max(value, axis=0, keepdims=True))
                sum_ref[r] = sum_ref[r] * jnp.exp(old - top) + jnp.sum(
                    jnp.exp(value - top), axis=0, keepdims=True
                )
                top_ref[r] = top
                return carry

            lax.fori_loop(row_first, row_last, row_turn, 0)

        block_turns(hop_first, hop_last, turn)

    first_pieces = PIECES // local
    for way in range(2):
        go(
            onward(way),
            remote(own_part(thin_col, thin), spot(z, c, thin_col, thin), 1, way * nb + 1, step(way), f),
        )
    for way in range(2):
        go(onward(way), remote(own_part(0, wide), spot(z, c, 0, wide), 0, way * nb + 1, step(way), f))
    row_copies = [[row_copy(d, piece) for d in range(1, nf)] for piece in range(PIECES)]
    for piece in range(first_pieces):
        for copy in row_copies[piece]:
            copy.start()
    loads = [
        pltpu.make_async_copy(
            emb_ref.at[pl.ds(pl.multiple_of(f * rows, rows), rows), :],
            rows_ref.at[:, pl.ds(pl.multiple_of(f * width, width), width)],
            own_sem.at[0],
        ),
        pltpu.make_async_copy(
            cen_ref, all_ref.at[pl.ds(pl.multiple_of(z * 2 * half, half), 2 * half), :], own_sem.at[1]
        ),
    ]
    for copy in loads:
        copy.start()
    top_ref[...] = jnp.full_like(top_ref, neg_big)
    sum_ref[...] = jnp.zeros_like(sum_ref)
    both(pass_thin, 1)
    for piece in range(first_pieces, PIECES):
        for copy in row_copies[piece]:
            copy.start()
    for copy in loads:
        copy.wait()
    offsets(0)
    both(pass_wide, 1)
    both(pass_thin, 2)
    for piece in range(first_pieces):
        for copy in row_copies[piece]:
            copy.wait_recv()
    scores(0, 1, 0, 1)
    both(pass_across, 1)
    both(complete, 1)
    offsets(1)
    scores(1, 2, 0, 1)
    both(pass_wide, 2)
    for hop in range(3, nb):
        both(pass_thin, hop)
    for piece in range(first_pieces, PIECES):
        for copy in row_copies[piece]:
            copy.wait_recv()
    scores(0, 2, 1, local)
    for hop in range(2, nb):
        if hop > 2:
            both(pass_wide, hop)
        both(pass_across, hop)
        both(complete, hop)
        offsets(hop)
        scores(hop, hop + 1, 0, local)

    for r in range(local):
        norm = top_ref[r] + jnp.log(sum_ref[r])
        norm_ref[r] = norm
        top_ref[r] = norm

    over_x = CHUNKS - 1

    def cols(t):
        return pl.ds(pl.multiple_of(t * size, size), size)

    left, right = jnp.int32(0), jnp.int32(nb - 1)
    turns = []
    for _ in range(nb):
        pick = (z - left) >= (right - z)
        turns.append(jnp.where(pick, left, right))
        left, right = jnp.where(pick, left + 1, left), jnp.where(pick, right, right - 1)

    def a_copy(q, t):
        return pltpu.make_async_remote_copy(
            src_ref=to_sib.at[q, :, cols(t)],
            dst_ref=from_sib.at[q, :, cols(t)],
            send_sem=a_send.at[q, t],
            recv_sem=a_recv.at[q, t],
            device_id={"blk": z, "feat": sibling},
            device_id_type=MESH,
        )

    def b_copy(i, t):
        return pltpu.make_async_remote_copy(
            src_ref=to_x.at[i, :, cols(t)],
            dst_ref=from_x.at[i, :, cols(t)],
            send_sem=b_send.at[i, t],
            recv_sem=b_recv.at[i, t],
            device_id={"blk": z, "feat": (1 - x) * 2 + c},
            device_id_type=MESH,
        )

    def z_copy(zz, way, t):
        return pltpu.make_async_remote_copy(
            src_ref=to_z.at[zz, :, cols(t)],
            dst_ref=from_z.at[way, zz, :, cols(t)],
            send_sem=z_send.at[zz, t],
            recv_sem=z_recv.at[way, zz, t],
            device_id={"blk": jnp.clip(z + 1 - 2 * way, 0, nb - 1), "feat": f},
            device_id_type=MESH,
        )

    def line_copy(zz, way):
        return pltpu.make_async_remote_copy(
            src_ref=to_line.at[zz],
            dst_ref=from_line.at[way, zz],
            send_sem=z_send.at[zz, over_x],
            recv_sem=z_recv.at[way, zz, over_x],
            device_id={"blk": jnp.clip(z + 1 - 2 * way, 0, nb - 1), "feat": f},
            device_id_type=MESH,
        )

    def swap_copy():
        return pltpu.make_async_remote_copy(
            src_ref=swap_out,
            dst_ref=swap_in,
            send_sem=swap_sem.at[0],
            recv_sem=swap_sem.at[1],
            device_id={"blk": z, "feat": (1 - x) * 2 + c},
            device_id_type=MESH,
        )

    def m_copy(d):
        return pltpu.make_async_remote_copy(
            src_ref=to_mass.at[lax.rem(me + d, n)],
            dst_ref=from_mass.at[d],
            send_sem=m_send.at[d],
            recv_sem=m_recv.at[d],
            device_id=at_offset(d),
            device_id_type=MESH,
        )

    def wide_of(value):
        return value.astype(jnp.float32)

    def place(i):
        zz = turns[nb - 1]
        for t in range(nb - 1):
            zz = jnp.where(i == t, turns[t], zz)
        return zz

    def sums(i, side):
        zz = place(i)
        xx = jnp.where(side == 0, 1 - x, x)
        q = side * nb + i
        col = zz * per + xx
        for cc in range(2):
            at = jnp.where(cc == 0, c, 1 - c)
            for r in range(local):
                value = score_ref[r, col, pl.ds(pl.multiple_of(at * own, own), own), :]
                weight_ref[cc * own : (cc + 1) * own, r * RB : (r + 1) * RB] = jnp.exp(
                    value - top_ref[r]
                ).astype(jnp.bfloat16)
        mass = lax.dot_general(
            jnp.ones((8, rows), jnp.bfloat16),
            weight_ref[...],
            transposed,
            preferred_element_type=jnp.float32,
        )
        to_mass[zz * nf + xx * 2 + c] = mass[:, :own]
        to_mass[zz * nf + xx * 2 + 1 - c] = mass[:, own:]

        def chunk(t, carry):
            total = jnp.dot(
                weight_ref[...], rows_ref[:, cols(t)], preferred_element_type=jnp.float32
            )
            keep_ref[q, :, cols(t)] = total[:own]
            to_sib[q, :, cols(t)] = total[own:].astype(jnp.bfloat16)
            a_copy(q, t).start()

            @pl.when(jnp.logical_and(side == 0, t > 0))
            def _():
                send_x(i, t - 1)

            return carry

        lax.fori_loop(0, CHUNKS, chunk, 0)

    def send_x(i, t):
        a_copy(i, t).wait()
        to_x[i, :, cols(t)] = (
            keep_ref[i, :, cols(t)] + wide_of(from_sib[i, :, cols(t)])
        ).astype(jnp.bfloat16)
        b_copy(i, t).start()

    def course(i):
        zz = place(i)
        fed = jnp.logical_or(
            jnp.logical_and(zz > z, z > 0), jnp.logical_and(zz < z, z < nb - 1)
        )
        return zz, (zz < z).astype(jnp.int32), fed

    def send_line(i):
        zz, way, fed = course(i)
        for side in range(2):
            q = side * nb + i
            a_copy(q, over_x).wait()
            pair_ref[side] = keep_ref[q, :, cols(over_x)] + wide_of(from_sib[q, :, cols(over_x)])

        @pl.when(fed)
        def _():
            line_copy(zz, way).wait_recv()
            pair_ref[...] += wide_of(from_line[way, zz])

        @pl.when(zz != z)
        def _():
            to_line[zz] = pair_ref[...].astype(jnp.bfloat16)
            line_copy(zz, way).start()

        @pl.when(zz == z)
        def _():
            for back in range(2):

                @pl.when((z > 0) if back == 0 else (z < nb - 1))
                def _():
                    line_copy(z, back).wait_recv()
                    pair_ref[...] += wide_of(from_line[back, z])

            swap_out[...] = pair_ref[0].astype(jnp.bfloat16)
            swap_copy().start()
            num_ref[:, cols(over_x)] = pair_ref[1]

    def send_z(i):
        zz, way, fed = course(i)
        q = nb + i

        def chunk(t, carry):
            a_copy(q, t).wait()
            b_copy(i, t).wait()
            part_ref[...] = (
                keep_ref[q, :, cols(t)]
                + wide_of(from_sib[q, :, cols(t)])
                + wide_of(from_x[i, :, cols(t)])
            )

            @pl.when(fed)
            def _():
                z_copy(zz, way, t).wait_recv()
                part_ref[...] += wide_of(from_z[way, zz, :, cols(t)])

            @pl.when(zz != z)
            def _():
                to_z[zz, :, cols(t)] = part_ref[...].astype(jnp.bfloat16)
                z_copy(zz, way, t).start()

            @pl.when(zz == z)
            def _():
                num_ref[:, cols(t)] = part_ref[...]

            return carry

        lax.fori_loop(0, over_x, chunk, 0)

    def turn(i, carry):
        @pl.when(i < nb)
        def _():
            def one(side, carry):
                sums(i, side)
                return carry

            lax.fori_loop(0, 2, one, 0)
            send_line(i)

        @pl.when(i == nb - 1)
        def _():
            def mass_start(d, carry):
                m_copy(d).start()
                return carry

            lax.fori_loop(1, n, mass_start, 0)

        @pl.when(i > 0)
        def _():
            send_z(i - 1)

        return carry

    lax.fori_loop(0, nb + 1, turn, 0)

    def mass_end(d, total):
        m_copy(d).wait()
        return total + from_mass[d]

    mass_ref[...] = lax.fori_loop(1, n, mass_end, to_mass[me])

    def last(t, carry):
        for way in range(2):

            @pl.when((z > 0) if way == 0 else (z < nb - 1))
            def _():
                z_copy(z, way, t).wait_recv()
                num_ref[:, cols(t)] += wide_of(from_z[way, z, :, cols(t)])

        for zz in range(nb):

            @pl.when(z != zz)
            def _():
                z_copy(zz, 0, t).wait_send()

        return carry

    lax.fori_loop(0, over_x, last, 0)
    for zz in range(nb):

        @pl.when(z != zz)
        def _():
            line_copy(zz, 0).wait_send()

    swap_copy().wait()
    num_ref[:, cols(over_x)] += wide_of(swap_in[...])
    for group in row_copies:
        for copy in group:
            copy.wait_send()
    for cond, copy in started:
        pl.when(cond)(copy.wait_send)


def fused(allow, embeddings, centroids, nb, nf):
    rows = embeddings.shape[0] // nf
    local = rows // RB
    nx = nf // 2
    n = nb * nf
    own = K // n
    kinds = 4 + 2 * nx + 1
    vmem = pl.BlockSpec(memory_space=pltpu.VMEM)
    hbm = pl.BlockSpec(memory_space=pltpu.HBM)
    dma = pltpu.SemaphoreType.DMA
    bf16, f32 = jnp.bfloat16, jnp.float32
    return pl.pallas_call(
        functools.partial(fused_kernel, nb, nf),
        out_shape=(
            jax.ShapeDtypeStruct((own, D), f32),
            jax.ShapeDtypeStruct((8, own), f32),
            jax.ShapeDtypeStruct((local, 1, RB), f32),
        ),
        in_specs=[pl.BlockSpec(memory_space=pltpu.SMEM), hbm, hbm],
        out_specs=(vmem,) * 3,
        scratch_shapes=[
            pltpu.VMEM((rows, D), bf16),
            pltpu.VMEM((K, D), bf16),
            pltpu.VMEM((NCB, CB, 1), f32),
            pltpu.VMEM((local, NCB, CB, RB), f32),
            pltpu.VMEM((local, 1, RB), f32),
            pltpu.VMEM((local, 1, RB), f32),
            pltpu.VMEM((CB, rows), bf16),
            pltpu.VMEM((2 * nb, own, D), f32),
            pltpu.VMEM((2 * nb, own, D), bf16),
            pltpu.VMEM((2 * nb, own, D), bf16),
            pltpu.VMEM((nb, own, D), bf16),
            pltpu.VMEM((nb, own, D), bf16),
            pltpu.VMEM((own, D // CHUNKS), f32),
            pltpu.VMEM((nb, own, D), bf16),
            pltpu.VMEM((2, nb, own, D), bf16),
            pltpu.VMEM((2, own, D // CHUNKS), f32),
            pltpu.VMEM((nb, 2, own, D // CHUNKS), bf16),
            pltpu.VMEM((2, nb, 2, own, D // CHUNKS), bf16),
            pltpu.VMEM((own, D // CHUNKS), bf16),
            pltpu.VMEM((own, D // CHUNKS), bf16),
            pltpu.VMEM((n, 8, own), f32),
            pltpu.VMEM((n, 8, own), f32),
            dma((nf, PIECES)),
            dma((nf, PIECES)),
            dma((kinds, 2 * nb)),
            dma((kinds, 2 * nb)),
            dma((2,)),
            dma((2 * nb, CHUNKS)),
            dma((2 * nb, CHUNKS)),
            dma((nb, CHUNKS)),
            dma((nb, CHUNKS)),
            dma((nb, CHUNKS)),
            dma((2, nb, CHUNKS)),
            dma((n,)),
            dma((n,)),
            dma((2,)),
        ],
        compiler_params=pltpu.CompilerParams(
            collective_id=2, has_side_effects=True, vmem_limit_bytes=58 * 2**20
        ),
        name="fused",
    )(allow, embeddings, centroids)


def body(embeddings, centroids, pair_list):
    nb, nf = lax.axis_size("blk"), lax.axis_size("feat")
    local_rows = embeddings.shape[0] // nf
    local_blocks = local_rows // RB
    device_index = lax.axis_index("blk") * nf + lax.axis_index("feat")
    mine = device_index * local_blocks + jnp.arange(local_blocks, dtype=jnp.int32)
    row_ids, col_ids = pair_list[:, 0], pair_list[:, 1]
    same = row_ids[None, :] == mine[:, None]
    if K // nb == 2 * CB and nf == 4 and local_blocks == 2:
        blocks = jnp.arange(NCB, dtype=jnp.int32)
        allow = jnp.sum(
            (same[:, None, :] & (col_ids[None, None, :] == blocks[None, :, None])).astype(jnp.int32),
            axis=2,
        )
        numerator, denominator, log_norm = fused(allow, embeddings, centroids, nb, nf)
    else:
        before = jnp.sum((row_ids[None, :] < mine[:, None]).astype(jnp.int32), axis=1)
        counts = jnp.sum(same.astype(jnp.int32), axis=1)
        rank = jnp.arange(row_ids.shape[0], dtype=jnp.int32)[None, :] - before[:, None]
        slots = jnp.arange(SLOTS, dtype=jnp.int32)
        picked = same[:, None, :] & (rank[:, None, :] == slots[None, :, None])
        chosen = jnp.sum(jnp.where(picked, col_ids[None, None, :], 0), axis=2)
        table = jnp.concatenate([counts[:, None], chosen], axis=1)
        row_data, panels = fetch(embeddings, centroids, nb, nf)
        num, mass, log_norm = terms(table, row_data, panels, nb, nf)
        numerator, denominator = reduce_sums(num, mass, nb, nf)

    own_count = centroids.shape[0] // nf
    own_rows = lax.dynamic_slice_in_dim(
        centroids, lax.axis_index("feat") * own_count, own_count, 0
    ).astype(jnp.float32)
    new_centroids = (numerator + prior_mass * own_rows) / (denominator[0][:, None] + prior_mass)
    return (new_centroids, log_norm.reshape(local_rows))


def solution(mesh):
    return jax.shard_map(
        body,
        mesh=mesh,
        in_specs=(P(("groups", "blk"), "feat"), P(("groups", "blk"), None), P("groups", None)),
        out_specs=(P(("groups", "blk", "feat"), None), P(("groups", "blk", "feat"))),
        check_vma=False,
    )
```

```python
import functools
import math

import jax
import jax.numpy as jnp
from jax import lax
from jax.experimental import pallas as pl
from jax.experimental.pallas import tpu as pltpu
from jax.sharding import PartitionSpec as P

D = 2048
K = 2048
RB = 512
CB = 256
NCB = K // CB
SLOTS = 4
PARTS = 8
PIECES = 8
CHUNKS = 8
SPANS = 4

neg_big = -1e30
prior_mass = 16.0
MESH = pl.DeviceIdType.MESH


def meet(peers):
    barrier = pltpu.get_barrier_semaphore()
    for peer in peers:
        pl.semaphore_signal(barrier, inc=1, device_id=peer, device_id_type=MESH)
    pl.semaphore_wait(barrier, len(peers))


def fetch_kernel(
    nb, nf, emb_ref, cen_ref, rows_ref, all_ref, row_send, row_recv, send, recv, own_sem,
    emb_hold, cen_hold,
):
    z = lax.axis_index("blk")
    f = lax.axis_index("feat")
    nx = nf // 2
    c = lax.rem(f, 2)
    x = f // 2
    rows, width = rows_ref.shape[0], emb_ref.shape[1]
    half = cen_ref.shape[0] // 2
    thin = D * 3 // 8 // nx // 128 * 128
    wide = D - nx * thin
    sibling = x * 2 + 1 - c

    def across(dx):
        return lax.rem(x + dx, nx)

    meet(
        [{"blk": z, "feat": lax.rem(f + d, nf)} for d in range(1, nf)]
        + [{"blk": lax.rem(z + d, nb), "feat": f} for d in range(1, nb)]
    )

    def spot(zz, cc, col, size):
        return all_ref.at[
            pl.ds(pl.multiple_of(zz * 2 * half + cc * half, half), half),
            pl.ds(pl.multiple_of(col, 128), size),
        ]

    def remote(src, dst, kind, d, blk, feat):
        return pltpu.make_async_remote_copy(
            src_ref=src,
            dst_ref=dst,
            send_sem=send.at[kind, d],
            recv_sem=recv.at[kind, d],
            device_id={"blk": blk, "feat": feat},
            device_id_type=MESH,
        )

    def own_part(col, size):
        return cen_ref.at[
            pl.ds(pl.multiple_of(c * half, half), half), pl.ds(pl.multiple_of(col, 128), size)
        ]

    thin_col = wide + x * thin
    started = []

    def go(cond, copy):
        pl.when(cond)(copy.start)
        started.append((cond, copy))

    def row_copy(d, piece):
        to = lax.rem(f + d, nf)
        size = rows // PIECES
        return pltpu.make_async_remote_copy(
            src_ref=emb_ref.at[pl.ds(pl.multiple_of(to * rows + piece * size, size), size), :],
            dst_ref=rows_ref.at[
                pl.ds(piece * size, size), pl.ds(pl.multiple_of(f * width, width), width)
            ],
            send_sem=row_send.at[d, piece],
            recv_sem=row_recv.at[d, piece],
            device_id={"blk": z, "feat": to},
            device_id_type=MESH,
        )

    def step(way):
        return jnp.clip(z + 1 - 2 * way, 0, nb - 1)

    def onward(way):
        return (z + 1 < nb) if way == 0 else (z > 0)

    for way in range(2):
        go(
            onward(way),
            remote(own_part(thin_col, thin), spot(z, c, thin_col, thin), 1, way * nb + 1, step(way), f),
        )
    for way in range(2):
        go(onward(way), remote(own_part(0, wide), spot(z, c, 0, wide), 0, way * nb + 1, step(way), f))
    row_copies = [row_copy(d, piece) for piece in range(PIECES) for d in range(1, nf)]
    for copy in row_copies:
        copy.start()
    holds = [
        (
            emb_ref.at[pl.ds(pl.multiple_of(f * rows, rows), rows), :],
            emb_hold,
            rows_ref.at[:, pl.ds(pl.multiple_of(f * width, width), width)],
        ),
        (
            cen_ref,
            cen_hold,
            all_ref.at[pl.ds(pl.multiple_of(z * 2 * half, half), 2 * half), :],
        ),
    ]
    loads = [pltpu.make_async_copy(src, hold, own_sem.at[i]) for i, (src, hold, _) in enumerate(holds)]
    stores = [
        pltpu.make_async_copy(hold, dst, own_sem.at[2 + i]) for i, (_, hold, dst) in enumerate(holds)
    ]
    for copy in loads:
        copy.start()
    for load, store in zip(loads, stores):
        load.wait()
        store.start()

    def source(way, hop):
        zz = z - hop if way == 0 else z + hop
        return (zz >= 0) if way == 0 else (zz < nb), jnp.clip(zz, 0, nb - 1)

    def arrived(cond, kind, d, zz, cc, col, size):
        here = spot(zz, cc, col, size)
        pl.when(cond)(remote(here, here, kind, d, z, sibling).wait_recv)
        return here

    turns = [(way, hop) for hop in range(1, nb) for way in range(2)]

    def pass_thin(way, hop):
        cond, zz = source(way, hop)
        d = way * nb + hop
        here = arrived(cond, 1, d, zz, c, thin_col, thin)
        if hop + 1 < nb:
            go(jnp.logical_and(cond, onward(way)), remote(here, here, 1, d + 1, step(way), f))
        for dx in range(1, nx):
            go(cond, remote(here, here, 4 + dx, d, z, across(dx) * 2 + c))
        go(cond, remote(here, here, 3, d, z, sibling))

    def pass_wide(way, hop):
        cond, zz = source(way, hop)
        d = way * nb + hop
        here = arrived(cond, 0, d, zz, c, 0, wide)
        if hop + 1 < nb:
            go(jnp.logical_and(cond, onward(way)), remote(here, here, 0, d + 1, step(way), f))
        go(cond, remote(here, here, 2, d, z, sibling))

    def pass_across(way, hop):
        cond, zz = source(way, hop)
        d = way * nb + hop
        for dx in range(1, nx):
            col = wide + lax.rem(x + nx - dx, nx) * thin
            here = arrived(cond, 4 + dx, d, zz, c, col, thin)
            go(cond, remote(here, here, 4 + nx + dx, d, z, sibling))

    for hop in range(1, nb):
        for way in range(2):
            pass_thin(way, hop)
        for way in range(2):
            pass_wide(way, hop)
    for way, hop in turns:
        pass_across(way, hop)
    for way, hop in turns:
        cond, zz = source(way, hop)
        d = way * nb + hop
        arrived(cond, 2, d, zz, 1 - c, 0, wide)
        arrived(cond, 3, d, zz, 1 - c, thin_col, thin)
        for dx in range(1, nx):
            col = wide + lax.rem(x + nx - dx, nx) * thin
            arrived(cond, 4 + nx + dx, d, zz, 1 - c, col, thin)
    for copy in stores:
        copy.wait()
    for copy in row_copies:
        copy.wait()
    for cond, copy in started:
        pl.when(cond)(copy.wait_send)


def fetch(embeddings, centroids, nb, nf):
    rows = embeddings.shape[0] // nf
    kinds = 4 + 2 * (nf // 2) + 1
    return pl.pallas_call(
        functools.partial(fetch_kernel, nb, nf),
        out_shape=(
            jax.ShapeDtypeStruct((rows, D), jnp.bfloat16),
            jax.ShapeDtypeStruct((K, D), jnp.bfloat16),
        ),
        in_specs=[pl.BlockSpec(memory_space=pltpu.HBM)] * 2,
        out_specs=(pl.BlockSpec(memory_space=pl.ANY),) * 2,
        scratch_shapes=[
            pltpu.SemaphoreType.DMA((nf, PIECES)),
            pltpu.SemaphoreType.DMA((nf, PIECES)),
            pltpu.SemaphoreType.DMA((kinds, 2 * nb)),
            pltpu.SemaphoreType.DMA((kinds, 2 * nb)),
            pltpu.SemaphoreType.DMA((4,)),
            pltpu.VMEM((rows, D // nf), jnp.bfloat16),
            pltpu.VMEM((K // nb, D), jnp.bfloat16),
        ],
        compiler_params=pltpu.CompilerParams(
            collective_id=0, has_side_effects=True, vmem_limit_bytes=6 * 2**20
        ),
        name="fetch",
    )(embeddings, centroids)


def term_kernel(nb, nf, tab_ref, rows_ref, all_ref, num_ref, mass_ref, norm_ref, score_ref, weight_ref, acc_ref, row_mass):
    local = rows_ref.shape[0] // RB
    scale = 1.0 / math.sqrt(D)
    own = K // (nb * nf)
    nx = nf // 2
    transposed = (((1,), (1,)), ((), ()))

    for r in range(local):
        part = rows_ref[r * RB : (r + 1) * RB, :]
        count = tab_ref[r, 0]

        def score_turn(slot, top):
            col = tab_ref[r, 1 + slot]
            panel = all_ref[pl.ds(pl.multiple_of(col * CB, CB), CB), :]
            wide = panel.astype(jnp.float32)
            offs = 0.5 * jnp.sum(wide * wide, axis=1, keepdims=True)
            raw = lax.dot_general(panel, part, transposed, preferred_element_type=jnp.float32)
            scores = (raw - offs) * scale
            score_ref[slot] = scores
            return jnp.maximum(top, jnp.max(scores, axis=0, keepdims=True))

        top = lax.fori_loop(0, count, score_turn, jnp.full((1, RB), neg_big, jnp.float32))

        def sum_turn(slot, total):
            return total + jnp.sum(jnp.exp(score_ref[slot] - top), axis=0, keepdims=True)

        total = lax.fori_loop(0, count, sum_turn, jnp.zeros((1, RB), jnp.float32))
        norm = top + jnp.log(total)
        norm_ref[r] = norm

        def weight_turn(slot, carry):
            col = tab_ref[r, 1 + slot]
            weight_ref[r, col] = jnp.exp(score_ref[slot] - norm).astype(jnp.bfloat16)
            return carry

        lax.fori_loop(0, count, weight_turn, 0)

    def col_turn(col, carry):
        acc_ref[...] = jnp.zeros_like(acc_ref)
        row_mass[...] = jnp.zeros_like(row_mass)
        for r in range(local):
            hit = jnp.int32(0)
            for slot in range(SLOTS):
                found = jnp.logical_and(tab_ref[r, 1 + slot] == col, slot < tab_ref[r, 0])
                hit = hit + found.astype(jnp.int32)

            @pl.when(hit > 0)
            def _():
                weights = weight_ref[r, col]
                acc_ref[...] += jnp.dot(
                    weights, rows_ref[r * RB : (r + 1) * RB, :], preferred_element_type=jnp.float32
                )
                row_mass[...] += lax.dot_general(
                    jnp.ones((8, RB), jnp.bfloat16),
                    weights,
                    transposed,
                    preferred_element_type=jnp.float32,
                )

        for j in range(CB // own):
            owner = col * (CB // own) + j
            zz, ff = owner // nf, lax.rem(owner, nf)
            num_ref[lax.rem(ff, 2), ff // 2, zz] = acc_ref[j * own : (j + 1) * own, :].astype(
                jnp.bfloat16
            )
            mass_ref[owner] = row_mass[:, j * own : (j + 1) * own]
        return carry

    lax.fori_loop(0, NCB, col_turn, 0)


def terms(table, row_data, panels, nb, nf):
    local = row_data.shape[0] // RB
    own = K // (nb * nf)
    vmem = pl.BlockSpec(memory_space=pltpu.VMEM)
    return pl.pallas_call(
        functools.partial(term_kernel, nb, nf),
        out_shape=(
            jax.ShapeDtypeStruct((2, nf // 2, nb, own, D), jnp.bfloat16),
            jax.ShapeDtypeStruct((nb * nf, 8, own), jnp.float32),
            jax.ShapeDtypeStruct((local, 1, RB), jnp.float32),
        ),
        in_specs=[pl.BlockSpec(memory_space=pltpu.SMEM), vmem, vmem],
        out_specs=(vmem,) * 3,
        scratch_shapes=[
            pltpu.VMEM((SLOTS, CB, RB), jnp.float32),
            pltpu.VMEM((local, NCB, CB, RB), jnp.bfloat16),
            pltpu.VMEM((CB, D), jnp.float32),
            pltpu.VMEM((8, CB), jnp.float32),
        ],
        compiler_params=pltpu.CompilerParams(vmem_limit_bytes=32 * 2**20),
        name="terms",
    )(table, row_data, panels)


def reduce_kernel(
    nb, nf, num_ref, mass_ref, out_ref, out_mass,
    from_sib, to_x, from_x, to_z, from_z, from_mass,
    a_send, a_recv, b_send, b_recv, c_send, c_recv, m_send, m_recv,
):
    z = lax.axis_index("blk")
    f = lax.axis_index("feat")
    nx = nf // 2
    n = nb * nf
    me = z * nf + f
    c = lax.rem(f, 2)
    x = f // 2
    sibling = x * 2 + 1 - c
    size = D // PARTS

    def at_offset(d):
        other = lax.rem(me + d, n)
        return {"blk": other // nf, "feat": lax.rem(other, nf)}

    barrier = pltpu.get_barrier_semaphore()

    def greet(d, carry):
        pl.semaphore_signal(barrier, inc=1, device_id=at_offset(d), device_id_type=MESH)
        return carry

    lax.fori_loop(1, n, greet, 0)
    pl.semaphore_wait(barrier, n - 1)

    def cols(t):
        return pl.ds(t * size, size)

    def a_copy(dx, t):
        xx = lax.rem(x + dx, nx)
        return pltpu.make_async_remote_copy(
            src_ref=num_ref.at[1 - c, xx, :, :, cols(t)],
            dst_ref=from_sib.at[xx, :, :, cols(t)],
            send_sem=a_send.at[dx, t],
            recv_sem=a_recv.at[dx, t],
            device_id={"blk": z, "feat": sibling},
            device_id_type=MESH,
        )

    def b_copy(dx, t):
        return pltpu.make_async_remote_copy(
            src_ref=to_x.at[dx - 1, :, :, cols(t)],
            dst_ref=from_x.at[dx - 1, :, :, cols(t)],
            send_sem=b_send.at[dx, t],
            recv_sem=b_recv.at[dx, t],
            device_id={"blk": z, "feat": lax.rem(x + dx, nx) * 2 + c},
            device_id_type=MESH,
        )

    def c_copy(d, t):
        return pltpu.make_async_remote_copy(
            src_ref=to_z.at[d - 1, :, cols(t)],
            dst_ref=from_z.at[d - 1, :, cols(t)],
            send_sem=c_send.at[d, t],
            recv_sem=c_recv.at[d, t],
            device_id={"blk": lax.rem(z + d, nb), "feat": f},
            device_id_type=MESH,
        )

    def m_copy(d):
        return pltpu.make_async_remote_copy(
            src_ref=mass_ref.at[lax.rem(me + d, n)],
            dst_ref=from_mass.at[d],
            send_sem=m_send.at[d],
            recv_sem=m_recv.at[d],
            device_id=at_offset(d),
            device_id_type=MESH,
        )

    def wide(value):
        return value.astype(jnp.float32)

    for t in range(PARTS):
        for dx in range(1, nx):
            a_copy(dx, t).start()
    for t in range(PARTS):
        a_copy(0, t).start()

    def mass_start(d, carry):
        m_copy(d).start()
        return carry

    lax.fori_loop(1, n, mass_start, 0)

    for t in range(PARTS):
        for dx in range(1, nx):
            xx = lax.rem(x + dx, nx)
            a_copy(dx, t).wait()
            for zz in range(nb):
                to_x[dx - 1, zz, :, cols(t)] = (
                    wide(num_ref[c, xx, zz, :, cols(t)]) + wide(from_sib[xx, zz, :, cols(t)])
                ).astype(jnp.bfloat16)
            b_copy(dx, t).start()

    def blk_sum(zz, t):
        total = wide(num_ref[c, x, zz, :, cols(t)]) + wide(from_sib[x, zz, :, cols(t)])
        for dx in range(1, nx):
            total = total + wide(from_x[dx - 1, zz, :, cols(t)])
        return total

    for t in range(PARTS):
        a_copy(0, t).wait()
        for dx in range(1, nx):
            b_copy(dx, t).wait()
        for d in range(1, nb):
            to_z[d - 1, :, cols(t)] = blk_sum(lax.rem(z + d, nb), t).astype(jnp.bfloat16)
            c_copy(d, t).start()
        out_ref[:, cols(t)] = blk_sum(z, t)

    def mass_end(d, total):
        m_copy(d).wait()
        return total + from_mass[d]

    out_mass[...] = lax.fori_loop(1, n, mass_end, mass_ref[me])

    for t in range(PARTS):
        total = out_ref[:, cols(t)]
        for d in range(1, nb):
            c_copy(d, t).wait()
            total = total + wide(from_z[d - 1, :, cols(t)])
        out_ref[:, cols(t)] = total


def reduce_sums(num, mass, nb, nf):
    own = K // (nb * nf)
    nx = nf // 2
    n = nb * nf
    vmem = pl.BlockSpec(memory_space=pltpu.VMEM)
    dma = pltpu.SemaphoreType.DMA
    return pl.pallas_call(
        functools.partial(reduce_kernel, nb, nf),
        out_shape=(
            jax.ShapeDtypeStruct((own, D), jnp.float32),
            jax.ShapeDtypeStruct((8, own), jnp.float32),
        ),
        in_specs=[vmem] * 2,
        out_specs=(vmem,) * 2,
        scratch_shapes=[
            pltpu.VMEM((nx, nb, own, D), jnp.bfloat16),
            pltpu.VMEM((nx - 1, nb, own, D), jnp.bfloat16),
            pltpu.VMEM((nx - 1, nb, own, D), jnp.bfloat16),
            pltpu.VMEM((nb - 1, own, D), jnp.bfloat16),
            pltpu.VMEM((nb - 1, own, D), jnp.bfloat16),
            pltpu.VMEM((n, 8, own), jnp.float32),
        ]
        + [dma((nx, PARTS))] * 4
        + [dma((nb, PARTS))] * 2
        + [dma((n,))] * 2,
        compiler_params=pltpu.CompilerParams(
            collective_id=1, has_side_effects=True, vmem_limit_bytes=24 * 2**20
        ),
        name="reduce_sums",
    )(num, mass)


def fused_kernel(
    nb, nf, allow_ref, emb_ref, cen_ref, num_ref, mass_ref, norm_ref,
    rows_ref, all_ref, offs_ref, score_ref, top_ref, sum_ref, weight_ref, keep_ref,
    to_sib, from_sib, to_x, from_x, part_ref, to_z, from_z, pair_ref, to_line, from_line,
    swap_out, swap_in, to_mass, from_mass,
    row_send, row_recv, send, recv, own_sem, a_send, a_recv, b_send, b_recv, z_send, z_recv,
    m_send, m_recv, line_send, line_recv, swap_sem,
):
    z = lax.axis_index("blk")
    f = lax.axis_index("feat")
    nx = nf // 2
    n = nb * nf
    me = z * nf + f
    c = lax.rem(f, 2)
    x = f // 2
    rows, width = rows_ref.shape[0], emb_ref.shape[1]
    local = rows // RB
    per = K // nb // CB
    half = cen_ref.shape[0] // 2
    own = K // n
    thin = D * 3 // 8 // nx // 128 * 128
    wide = D - nx * thin
    sibling = x * 2 + 1 - c
    size = D // CHUNKS
    scale = 1.0 / math.sqrt(D)
    transposed = (((1,), (1,)), ((), ()))

    def at_offset(d):
        other = lax.rem(me + d, n)
        return {"blk": other // nf, "feat": lax.rem(other, nf)}

    barrier = pltpu.get_barrier_semaphore()

    def greet(d, carry):
        pl.semaphore_signal(barrier, inc=1, device_id=at_offset(d), device_id_type=MESH)
        return carry

    lax.fori_loop(1, n, greet, 0)
    pl.semaphore_wait(barrier, n - 1)

    def across(dx):
        return lax.rem(x + dx, nx)

    def spot(zz, cc, col, count):
        return all_ref.at[
            pl.ds(pl.multiple_of(zz * 2 * half + cc * half, half), half),
            pl.ds(pl.multiple_of(col, 128), count),
        ]

    def remote(src, dst, kind, d, blk, feat):
        return pltpu.make_async_remote_copy(
            src_ref=src,
            dst_ref=dst,
            send_sem=send.at[kind, d],
            recv_sem=recv.at[kind, d],
            device_id={"blk": blk, "feat": feat},
            device_id_type=MESH,
        )

    def own_part(col, count):
        return cen_ref.at[
            pl.ds(pl.multiple_of(c * half, half), half), pl.ds(pl.multiple_of(col, 128), count)
        ]

    thin_col = wide + x * thin
    started = []

    def go(cond, copy):
        pl.when(cond)(copy.start)
        started.append((cond, copy))

    piece_rows = rows // PIECES

    def row_copy(d, piece):
        to = lax.rem(f + d, nf)
        return pltpu.make_async_remote_copy(
            src_ref=emb_ref.at[
                pl.ds(pl.multiple_of(to * rows + piece * piece_rows, piece_rows), piece_rows), :
            ],
            dst_ref=rows_ref.at[
                pl.ds(piece * piece_rows, piece_rows),
                pl.ds(pl.multiple_of(f * width, width), width),
            ],
            send_sem=row_send.at[d, piece],
            recv_sem=row_recv.at[d, piece],
            device_id={"blk": z, "feat": to},
            device_id_type=MESH,
        )

    def step(way):
        return jnp.clip(z + 1 - 2 * way, 0, nb - 1)

    def onward(way):
        return (z + 1 < nb) if way == 0 else (z > 0)

    def source(way, hop):
        zz = z - hop if way == 0 else z + hop
        return (zz >= 0) if way == 0 else (zz < nb), jnp.clip(zz, 0, nb - 1)

    def arrived(cond, kind, d, zz, cc, col, count):
        here = spot(zz, cc, col, count)
        pl.when(cond)(remote(here, here, kind, d, z, sibling).wait_recv)
        return here

    def pass_thin(way, hop):
        cond, zz = source(way, hop)
        d = way * nb + hop
        here = arrived(cond, 1, d, zz, c, thin_col, thin)
        if hop + 1 < nb:
            go(jnp.logical_and(cond, onward(way)), remote(here, here, 1, d + 1, step(way), f))
        for dx in range(1, nx):
            go(cond, remote(here, here, 4 + dx, d, z, across(dx) * 2 + c))
        go(cond, remote(here, here, 3, d, z, sibling))

    def pass_wide(way, hop):
        cond, zz = source(way, hop)
        d = way * nb + hop
        here = arrived(cond, 0, d, zz, c, 0, wide)
        if hop + 1 < nb:
            go(jnp.logical_and(cond, onward(way)), remote(here, here, 0, d + 1, step(way), f))
        go(cond, remote(here, here, 2, d, z, sibling))

    def pass_across(way, hop):
        cond, zz = source(way, hop)
        d = way * nb + hop
        for dx in range(1, nx):
            col = wide + lax.rem(x + nx - dx, nx) * thin
            here = arrived(cond, 4 + dx, d, zz, c, col, thin)
            go(cond, remote(here, here, 4 + nx + dx, d, z, sibling))

    def complete(way, hop):
        cond, zz = source(way, hop)
        d = way * nb + hop
        arrived(cond, 2, d, zz, 1 - c, 0, wide)
        arrived(cond, 3, d, zz, 1 - c, thin_col, thin)
        for dx in range(1, nx):
            col = wide + lax.rem(x + nx - dx, nx) * thin
            arrived(cond, 4 + nx + dx, d, zz, 1 - c, col, thin)

    def both(turn, hop):
        for way in range(2):
            turn(way, hop)

    def block_turns(hop_first, hop_last, turn):
        def one(t, carry):
            hop, rest = t // (2 * per), lax.rem(t, 2 * per)
            way, j = rest // per, lax.rem(rest, per)
            zz = z + (2 * way - 1) * hop
            fits = jnp.logical_and(zz >= 0, zz < nb)
            fits = jnp.logical_and(fits, jnp.logical_or(hop > 0, way == 0))

            @pl.when(fits)
            def _():
                turn(zz * per + j)

            return carry

        lax.fori_loop(hop_first * 2 * per, hop_last * 2 * per, one, 0)

    def offsets(hop):
        def turn(col):
            panel = all_ref[pl.ds(pl.multiple_of(col * CB, CB), CB), :].astype(jnp.float32)
            offs_ref[col] = 0.5 * jnp.sum(panel * panel, axis=1, keepdims=True)

        block_turns(hop, hop + 1, turn)

    def scores(hop_first, hop_last, row_first, row_last):
        def turn(col):
            def row_turn(r, carry):
                raw = lax.dot_general(
                    all_ref[pl.ds(pl.multiple_of(col * CB, CB), CB), :],
                    rows_ref[pl.ds(pl.multiple_of(r * RB, RB), RB), :],
                    transposed,
                    preferred_element_type=jnp.float32,
                )
                value = jnp.where(allow_ref[r, col] > 0, (raw - offs_ref[col]) * scale, neg_big)
                score_ref[r, col] = value
                old = top_ref[r]
                top = jnp.maximum(old, jnp.max(value, axis=0, keepdims=True))
                sum_ref[r] = sum_ref[r] * jnp.exp(old - top) + jnp.sum(
                    jnp.exp(value - top), axis=0, keepdims=True
                )
                top_ref[r] = top
                return carry

            lax.fori_loop(row_first, row_last, row_turn, 0)

        block_turns(hop_first, hop_last, turn)

    first_pieces = PIECES // local
    for way in range(2):
        go(
            onward(way),
            remote(own_part(thin_col, thin), spot(z, c, thin_col, thin), 1, way * nb + 1, step(way), f),
        )
    for way in range(2):
        go(onward(way), remote(own_part(0, wide), spot(z, c, 0, wide), 0, way * nb + 1, step(way), f))
    row_copies = [[row_copy(d, piece) for d in range(1, nf)] for piece in range(PIECES)]
    for piece in range(first_pieces):
        for copy in row_copies[piece]:
            copy.start()
    loads = [
        pltpu.make_async_copy(
            emb_ref.at[pl.ds(pl.multiple_of(f * rows, rows), rows), :],
            rows_ref.at[:, pl.ds(pl.multiple_of(f * width, width), width)],
            own_sem.at[0],
        ),
        pltpu.make_async_copy(
            cen_ref, all_ref.at[pl.ds(pl.multiple_of(z * 2 * half, half), 2 * half), :], own_sem.at[1]
        ),
    ]
    for copy in loads:
        copy.start()
    top_ref[...] = jnp.full_like(top_ref, neg_big)
    sum_ref[...] = jnp.zeros_like(sum_ref)
    both(pass_thin, 1)
    for piece in range(first_pieces, PIECES):
        for copy in row_copies[piece]:
            copy.start()
    for copy in loads:
        copy.wait()
    offsets(0)
    both(pass_wide, 1)
    both(pass_thin, 2)
    for piece in range(first_pieces):
        for copy in row_copies[piece]:
            copy.wait_recv()
    scores(0, 1, 0, 1)
    both(pass_across, 1)
    both(complete, 1)
    offsets(1)
    scores(1, 2, 0, 1)
    both(pass_wide, 2)
    for hop in range(3, nb):
        both(pass_thin, hop)
    for piece in range(first_pieces, PIECES):
        for copy in row_copies[piece]:
            copy.wait_recv()
    scores(0, 2, 1, local)
    for hop in range(2, nb):
        if hop > 2:
            both(pass_wide, hop)
        both(pass_across, hop)
        both(complete, hop)
        offsets(hop)
        scores(hop, hop + 1, 0, local)

    for r in range(local):
        norm = top_ref[r] + jnp.log(sum_ref[r])
        norm_ref[r] = norm
        top_ref[r] = norm

    lead = 0

    def cols(t):
        return pl.ds(pl.multiple_of(t * size, size), size)

    left, right = jnp.int32(0), jnp.int32(nb - 1)
    turns = []
    for _ in range(nb):
        pick = (z - left) >= (right - z)
        turns.append(jnp.where(pick, left, right))
        left, right = jnp.where(pick, left + 1, left), jnp.where(pick, right, right - 1)

    def a_copy(q, t):
        return pltpu.make_async_remote_copy(
            src_ref=to_sib.at[q, :, cols(t)],
            dst_ref=from_sib.at[q, :, cols(t)],
            send_sem=a_send.at[q, t],
            recv_sem=a_recv.at[q, t],
            device_id={"blk": z, "feat": sibling},
            device_id_type=MESH,
        )

    def b_copy(i, t):
        return pltpu.make_async_remote_copy(
            src_ref=to_x.at[i, :, cols(t)],
            dst_ref=from_x.at[i, :, cols(t)],
            send_sem=b_send.at[i, t],
            recv_sem=b_recv.at[i, t],
            device_id={"blk": z, "feat": (1 - x) * 2 + c},
            device_id_type=MESH,
        )

    def z_copy(zz, way, t):
        return pltpu.make_async_remote_copy(
            src_ref=to_z.at[zz, :, cols(t)],
            dst_ref=from_z.at[way, zz, :, cols(t)],
            send_sem=z_send.at[zz, t],
            recv_sem=z_recv.at[way, zz, t],
            device_id={"blk": jnp.clip(z + 1 - 2 * way, 0, nb - 1), "feat": f},
            device_id_type=MESH,
        )

    def line_copy(d):
        zz = lax.rem(z + d, nb)
        return pltpu.make_async_remote_copy(
            src_ref=to_line.at[zz],
            dst_ref=from_line.at[d - 1],
            send_sem=line_send.at[d],
            recv_sem=line_recv.at[d],
            device_id={"blk": zz, "feat": f},
            device_id_type=MESH,
        )

    def swap_copy():
        return pltpu.make_async_remote_copy(
            src_ref=swap_out,
            dst_ref=swap_in,
            send_sem=swap_sem.at[0],
            recv_sem=swap_sem.at[1],
            device_id={"blk": z, "feat": (1 - x) * 2 + c},
            device_id_type=MESH,
        )

    def m_copy(d):
        return pltpu.make_async_remote_copy(
            src_ref=to_mass.at[lax.rem(me + d, n)],
            dst_ref=from_mass.at[d],
            send_sem=m_send.at[d],
            recv_sem=m_recv.at[d],
            device_id=at_offset(d),
            device_id_type=MESH,
        )

    def wide_of(value):
        return value.astype(jnp.float32)

    def place(i):
        zz = turns[nb - 1]
        for t in range(nb - 1):
            zz = jnp.where(i == t, turns[t], zz)
        return zz

    group = CHUNKS // SPANS

    def weights(i, side):
        zz = place(i)
        xx = 1 - x if side == 0 else x
        col = zz * per + xx
        part = slice(side * CB, (side + 1) * CB)
        for cc in range(2):
            at = c if cc == 0 else 1 - c
            first = side * CB + cc * own
            for r in range(local):
                value = score_ref[r, col, pl.ds(pl.multiple_of(at * own, own), own), :]
                weight_ref[first : first + own, r * RB : (r + 1) * RB] = jnp.exp(
                    value - top_ref[r]
                ).astype(jnp.bfloat16)
        mass = lax.dot_general(
            jnp.ones((8, rows), jnp.bfloat16),
            weight_ref[part, :],
            transposed,
            preferred_element_type=jnp.float32,
        )
        to_mass[zz * nf + xx * 2 + c] = mass[:, :own]
        to_mass[zz * nf + xx * 2 + 1 - c] = mass[:, own:]

    def sums(i):
        for side in range(2):
            weights(i, side)

        def span(u, carry):
            @pl.when(u < SPANS)
            def _():
                at = pl.ds(pl.multiple_of(u * group * size, group * size), group * size)
                total = jnp.dot(
                    weight_ref[...], rows_ref[:, at], preferred_element_type=jnp.float32
                )
                for side in range(2):
                    first = side * CB
                    keep_ref[side * nb + i, :, at] = total[first : first + own]
                    to_sib[side * nb + i, :, at] = total[first + own : first + CB].astype(jnp.bfloat16)
                for side in range(2):
                    for t in range(group):
                        a_copy(side * nb + i, u * group + t).start()

            @pl.when(u == 1)
            def _():
                send_line(i)

            @pl.when(u > 0)
            def _():
                for t in range(group):
                    at = (u - 1) * group + t
                    pl.when(at > lead)(functools.partial(send_x, i, at))

            return carry

        lax.fori_loop(0, SPANS + 1, span, 0)

    def send_x(i, t):
        a_copy(i, t).wait()
        to_x[i, :, cols(t)] = (
            keep_ref[i, :, cols(t)] + wide_of(from_sib[i, :, cols(t)])
        ).astype(jnp.bfloat16)
        b_copy(i, t).start()

    def course(i):
        zz = place(i)
        fed = jnp.logical_or(
            jnp.logical_and(zz > z, z > 0), jnp.logical_and(zz < z, z < nb - 1)
        )
        return zz, (zz < z).astype(jnp.int32), fed

    def send_line(i):
        zz = place(i)
        for side in range(2):
            q = side * nb + i
            a_copy(q, lead).wait()
            pair_ref[side] = keep_ref[q, :, cols(lead)] + wide_of(from_sib[q, :, cols(lead)])

        @pl.when(zz != z)
        def _():
            to_line[zz] = pair_ref[...].astype(jnp.bfloat16)
            line_copy(lax.rem(zz - z + nb, nb)).start()

    def swap():
        def one(d, carry):
            line_copy(d).wait()
            pair_ref[...] += wide_of(from_line[d - 1])
            return carry

        lax.fori_loop(1, nb, one, 0)
        swap_out[...] = pair_ref[0].astype(jnp.bfloat16)
        swap_copy().start()
        num_ref[:, cols(lead)] = pair_ref[1]

    def send_z(i):
        zz, way, fed = course(i)
        q = nb + i

        def chunk(t, carry):
            a_copy(q, t).wait()
            b_copy(i, t).wait()
            part_ref[...] = (
                keep_ref[q, :, cols(t)]
                + wide_of(from_sib[q, :, cols(t)])
                + wide_of(from_x[i, :, cols(t)])
            )

            @pl.when(fed)
            def _():
                z_copy(zz, way, t).wait_recv()
                part_ref[...] += wide_of(from_z[way, zz, :, cols(t)])

            @pl.when(zz != z)
            def _():
                to_z[zz, :, cols(t)] = part_ref[...].astype(jnp.bfloat16)
                z_copy(zz, way, t).start()

            @pl.when(zz == z)
            def _():
                num_ref[:, cols(t)] = part_ref[...]

            return carry

        lax.fori_loop(lead + 1, CHUNKS, chunk, 0)

    def turn(i, carry):
        @pl.when(i < nb)
        def _():
            sums(i)

        @pl.when(i == nb - 1)
        def _():
            def mass_start(d, carry):
                m_copy(d).start()
                return carry

            lax.fori_loop(1, n, mass_start, 0)

        pl.when(i == nb)(swap)

        @pl.when(i > 0)
        def _():
            send_z(i - 1)

        return carry

    lax.fori_loop(0, nb + 1, turn, 0)

    def mass_end(d, total):
        m_copy(d).wait()
        return total + from_mass[d]

    mass_ref[...] = lax.fori_loop(1, n, mass_end, to_mass[me])

    def last(t, carry):
        for way in range(2):

            @pl.when((z > 0) if way == 0 else (z < nb - 1))
            def _():
                z_copy(z, way, t).wait_recv()
                num_ref[:, cols(t)] += wide_of(from_z[way, z, :, cols(t)])

        for zz in range(nb):

            @pl.when(z != zz)
            def _():
                z_copy(zz, 0, t).wait_send()

        return carry

    lax.fori_loop(lead + 1, CHUNKS, last, 0)
    swap_copy().wait()
    num_ref[:, cols(lead)] += wide_of(swap_in[...])
    for group in row_copies:
        for copy in group:
            copy.wait_send()
    for cond, copy in started:
        pl.when(cond)(copy.wait_send)


def fused(allow, embeddings, centroids, nb, nf):
    rows = embeddings.shape[0] // nf
    local = rows // RB
    nx = nf // 2
    n = nb * nf
    own = K // n
    kinds = 4 + 2 * nx + 1
    vmem = pl.BlockSpec(memory_space=pltpu.VMEM)
    hbm = pl.BlockSpec(memory_space=pltpu.HBM)
    dma = pltpu.SemaphoreType.DMA
    bf16, f32 = jnp.bfloat16, jnp.float32
    return pl.pallas_call(
        functools.partial(fused_kernel, nb, nf),
        out_shape=(
            jax.ShapeDtypeStruct((own, D), f32),
            jax.ShapeDtypeStruct((8, own), f32),
            jax.ShapeDtypeStruct((local, 1, RB), f32),
        ),
        in_specs=[pl.BlockSpec(memory_space=pltpu.SMEM), hbm, hbm],
        out_specs=(vmem,) * 3,
        scratch_shapes=[
            pltpu.VMEM((rows, D), bf16),
            pltpu.VMEM((K, D), bf16),
            pltpu.VMEM((NCB, CB, 1), f32),
            pltpu.VMEM((local, NCB, CB, RB), f32),
            pltpu.VMEM((local, 1, RB), f32),
            pltpu.VMEM((local, 1, RB), f32),
            pltpu.VMEM((2 * CB, rows), bf16),
            pltpu.VMEM((2 * nb, own, D), f32),
            pltpu.VMEM((2 * nb, own, D), bf16),
            pltpu.VMEM((2 * nb, own, D), bf16),
            pltpu.VMEM((nb, own, D), bf16),
            pltpu.VMEM((nb, own, D), bf16),
            pltpu.VMEM((own, D // CHUNKS), f32),
            pltpu.VMEM((nb, own, D), bf16),
            pltpu.VMEM((2, nb, own, D), bf16),
            pltpu.VMEM((2, own, D // CHUNKS), f32),
            pltpu.VMEM((nb, 2, own, D // CHUNKS), bf16),
            pltpu.VMEM((nb - 1, 2, own, D // CHUNKS), bf16),
            pltpu.VMEM((own, D // CHUNKS), bf16),
            pltpu.VMEM((own, D // CHUNKS), bf16),
            pltpu.VMEM((n, 8, own), f32),
            pltpu.VMEM((n, 8, own), f32),
            dma((nf, PIECES)),
            dma((nf, PIECES)),
            dma((kinds, 2 * nb)),
            dma((kinds, 2 * nb)),
            dma((2,)),
            dma((2 * nb, CHUNKS)),
            dma((2 * nb, CHUNKS)),
            dma((nb, CHUNKS)),
            dma((nb, CHUNKS)),
            dma((nb, CHUNKS)),
            dma((2, nb, CHUNKS)),
            dma((n,)),
            dma((n,)),
            dma((nb,)),
            dma((nb,)),
            dma((2,)),
        ],
        compiler_params=pltpu.CompilerParams(
            collective_id=2, has_side_effects=True, vmem_limit_bytes=58 * 2**20
        ),
        name="fused",
    )(allow, embeddings, centroids)


def body(embeddings, centroids, pair_list):
    nb, nf = lax.axis_size("blk"), lax.axis_size("feat")
    local_rows = embeddings.shape[0] // nf
    local_blocks = local_rows // RB
    device_index = lax.axis_index("blk") * nf + lax.axis_index("feat")
    mine = device_index * local_blocks + jnp.arange(local_blocks, dtype=jnp.int32)
    row_ids, col_ids = pair_list[:, 0], pair_list[:, 1]
    same = row_ids[None, :] == mine[:, None]
    if K // nb == 2 * CB and nf == 4 and local_blocks == 2:
        blocks = jnp.arange(NCB, dtype=jnp.int32)
        allow = jnp.sum(
            (same[:, None, :] & (col_ids[None, None, :] == blocks[None, :, None])).astype(jnp.int32),
            axis=2,
        )
        numerator, denominator, log_norm = fused(allow, embeddings, centroids, nb, nf)
    else:
        before = jnp.sum((row_ids[None, :] < mine[:, None]).astype(jnp.int32), axis=1)
        counts = jnp.sum(same.astype(jnp.int32), axis=1)
        rank = jnp.arange(row_ids.shape[0], dtype=jnp.int32)[None, :] - before[:, None]
        slots = jnp.arange(SLOTS, dtype=jnp.int32)
        picked = same[:, None, :] & (rank[:, None, :] == slots[None, :, None])
        chosen = jnp.sum(jnp.where(picked, col_ids[None, None, :], 0), axis=2)
        table = jnp.concatenate([counts[:, None], chosen], axis=1)
        row_data, panels = fetch(embeddings, centroids, nb, nf)
        num, mass, log_norm = terms(table, row_data, panels, nb, nf)
        numerator, denominator = reduce_sums(num, mass, nb, nf)

    own_count = centroids.shape[0] // nf
    own_rows = lax.dynamic_slice_in_dim(
        centroids, lax.axis_index("feat") * own_count, own_count, 0
    ).astype(jnp.float32)
    new_centroids = (numerator + prior_mass * own_rows) / (denominator[0][:, None] + prior_mass)
    return (new_centroids, log_norm.reshape(local_rows))


def solution(mesh):
    return jax.shard_map(
        body,
        mesh=mesh,
        in_specs=(P(("groups", "blk"), "feat"), P(("groups", "blk"), None), P("groups", None)),
        out_specs=(P(("groups", "blk", "feat"), None), P(("groups", "blk", "feat"))),
        check_vma=False,
    )
```

```python
import functools
import math

import jax
import jax.numpy as jnp
from jax import lax
from jax.experimental import pallas as pl
from jax.experimental.pallas import tpu as pltpu
from jax.sharding import PartitionSpec as P

D = 2048
K = 2048
RB = 512
CB = 256
NCB = K // CB
SLOTS = 4
PARTS = 8
PIECES = 8
CHUNKS = 8
SPANS = 4

neg_big = -1e30
prior_mass = 16.0
MESH = pl.DeviceIdType.MESH


def meet(peers):
    barrier = pltpu.get_barrier_semaphore()
    for peer in peers:
        pl.semaphore_signal(barrier, inc=1, device_id=peer, device_id_type=MESH)
    pl.semaphore_wait(barrier, len(peers))


def fetch_kernel(
    nb, nf, emb_ref, cen_ref, rows_ref, all_ref, row_send, row_recv, send, recv, own_sem,
    emb_hold, cen_hold,
):
    z = lax.axis_index("blk")
    f = lax.axis_index("feat")
    nx = nf // 2
    c = lax.rem(f, 2)
    x = f // 2
    rows, width = rows_ref.shape[0], emb_ref.shape[1]
    half = cen_ref.shape[0] // 2
    thin = D * 3 // 8 // nx // 128 * 128
    wide = D - nx * thin
    sibling = x * 2 + 1 - c

    def across(dx):
        return lax.rem(x + dx, nx)

    meet(
        [{"blk": z, "feat": lax.rem(f + d, nf)} for d in range(1, nf)]
        + [{"blk": lax.rem(z + d, nb), "feat": f} for d in range(1, nb)]
    )

    def spot(zz, cc, col, size):
        return all_ref.at[
            pl.ds(pl.multiple_of(zz * 2 * half + cc * half, half), half),
            pl.ds(pl.multiple_of(col, 128), size),
        ]

    def remote(src, dst, kind, d, blk, feat):
        return pltpu.make_async_remote_copy(
            src_ref=src,
            dst_ref=dst,
            send_sem=send.at[kind, d],
            recv_sem=recv.at[kind, d],
            device_id={"blk": blk, "feat": feat},
            device_id_type=MESH,
        )

    def own_part(col, size):
        return cen_ref.at[
            pl.ds(pl.multiple_of(c * half, half), half), pl.ds(pl.multiple_of(col, 128), size)
        ]

    thin_col = wide + x * thin
    started = []

    def go(cond, copy):
        pl.when(cond)(copy.start)
        started.append((cond, copy))

    def row_copy(d, piece):
        to = lax.rem(f + d, nf)
        size = rows // PIECES
        return pltpu.make_async_remote_copy(
            src_ref=emb_ref.at[pl.ds(pl.multiple_of(to * rows + piece * size, size), size), :],
            dst_ref=rows_ref.at[
                pl.ds(piece * size, size), pl.ds(pl.multiple_of(f * width, width), width)
            ],
            send_sem=row_send.at[d, piece],
            recv_sem=row_recv.at[d, piece],
            device_id={"blk": z, "feat": to},
            device_id_type=MESH,
        )

    def step(way):
        return jnp.clip(z + 1 - 2 * way, 0, nb - 1)

    def onward(way):
        return (z + 1 < nb) if way == 0 else (z > 0)

    for way in range(2):
        go(
            onward(way),
            remote(own_part(thin_col, thin), spot(z, c, thin_col, thin), 1, way * nb + 1, step(way), f),
        )
    for way in range(2):
        go(onward(way), remote(own_part(0, wide), spot(z, c, 0, wide), 0, way * nb + 1, step(way), f))
    row_copies = [row_copy(d, piece) for piece in range(PIECES) for d in range(1, nf)]
    for copy in row_copies:
        copy.start()
    holds = [
        (
            emb_ref.at[pl.ds(pl.multiple_of(f * rows, rows), rows), :],
            emb_hold,
            rows_ref.at[:, pl.ds(pl.multiple_of(f * width, width), width)],
        ),
        (
            cen_ref,
            cen_hold,
            all_ref.at[pl.ds(pl.multiple_of(z * 2 * half, half), 2 * half), :],
        ),
    ]
    loads = [pltpu.make_async_copy(src, hold, own_sem.at[i]) for i, (src, hold, _) in enumerate(holds)]
    stores = [
        pltpu.make_async_copy(hold, dst, own_sem.at[2 + i]) for i, (_, hold, dst) in enumerate(holds)
    ]
    for copy in loads:
        copy.start()
    for load, store in zip(loads, stores):
        load.wait()
        store.start()

    def source(way, hop):
        zz = z - hop if way == 0 else z + hop
        return (zz >= 0) if way == 0 else (zz < nb), jnp.clip(zz, 0, nb - 1)

    def arrived(cond, kind, d, zz, cc, col, size):
        here = spot(zz, cc, col, size)
        pl.when(cond)(remote(here, here, kind, d, z, sibling).wait_recv)
        return here

    turns = [(way, hop) for hop in range(1, nb) for way in range(2)]

    def pass_thin(way, hop):
        cond, zz = source(way, hop)
        d = way * nb + hop
        here = arrived(cond, 1, d, zz, c, thin_col, thin)
        if hop + 1 < nb:
            go(jnp.logical_and(cond, onward(way)), remote(here, here, 1, d + 1, step(way), f))
        for dx in range(1, nx):
            go(cond, remote(here, here, 4 + dx, d, z, across(dx) * 2 + c))
        go(cond, remote(here, here, 3, d, z, sibling))

    def pass_wide(way, hop):
        cond, zz = source(way, hop)
        d = way * nb + hop
        here = arrived(cond, 0, d, zz, c, 0, wide)
        if hop + 1 < nb:
            go(jnp.logical_and(cond, onward(way)), remote(here, here, 0, d + 1, step(way), f))
        go(cond, remote(here, here, 2, d, z, sibling))

    def pass_across(way, hop):
        cond, zz = source(way, hop)
        d = way * nb + hop
        for dx in range(1, nx):
            col = wide + lax.rem(x + nx - dx, nx) * thin
            here = arrived(cond, 4 + dx, d, zz, c, col, thin)
            go(cond, remote(here, here, 4 + nx + dx, d, z, sibling))

    for hop in range(1, nb):
        for way in range(2):
            pass_thin(way, hop)
        for way in range(2):
            pass_wide(way, hop)
    for way, hop in turns:
        pass_across(way, hop)
    for way, hop in turns:
        cond, zz = source(way, hop)
        d = way * nb + hop
        arrived(cond, 2, d, zz, 1 - c, 0, wide)
        arrived(cond, 3, d, zz, 1 - c, thin_col, thin)
        for dx in range(1, nx):
            col = wide + lax.rem(x + nx - dx, nx) * thin
            arrived(cond, 4 + nx + dx, d, zz, 1 - c, col, thin)
    for copy in stores:
        copy.wait()
    for copy in row_copies:
        copy.wait()
    for cond, copy in started:
        pl.when(cond)(copy.wait_send)


def fetch(embeddings, centroids, nb, nf):
    rows = embeddings.shape[0] // nf
    kinds = 4 + 2 * (nf // 2) + 1
    return pl.pallas_call(
        functools.partial(fetch_kernel, nb, nf),
        out_shape=(
            jax.ShapeDtypeStruct((rows, D), jnp.bfloat16),
            jax.ShapeDtypeStruct((K, D), jnp.bfloat16),
        ),
        in_specs=[pl.BlockSpec(memory_space=pltpu.HBM)] * 2,
        out_specs=(pl.BlockSpec(memory_space=pl.ANY),) * 2,
        scratch_shapes=[
            pltpu.SemaphoreType.DMA((nf, PIECES)),
            pltpu.SemaphoreType.DMA((nf, PIECES)),
            pltpu.SemaphoreType.DMA((kinds, 2 * nb)),
            pltpu.SemaphoreType.DMA((kinds, 2 * nb)),
            pltpu.SemaphoreType.DMA((4,)),
            pltpu.VMEM((rows, D // nf), jnp.bfloat16),
            pltpu.VMEM((K // nb, D), jnp.bfloat16),
        ],
        compiler_params=pltpu.CompilerParams(
            collective_id=0, has_side_effects=True, vmem_limit_bytes=6 * 2**20
        ),
        name="fetch",
    )(embeddings, centroids)


def term_kernel(nb, nf, tab_ref, rows_ref, all_ref, num_ref, mass_ref, norm_ref, score_ref, weight_ref, acc_ref, row_mass):
    local = rows_ref.shape[0] // RB
    scale = 1.0 / math.sqrt(D)
    own = K // (nb * nf)
    nx = nf // 2
    transposed = (((1,), (1,)), ((), ()))

    for r in range(local):
        part = rows_ref[r * RB : (r + 1) * RB, :]
        count = tab_ref[r, 0]

        def score_turn(slot, top):
            col = tab_ref[r, 1 + slot]
            panel = all_ref[pl.ds(pl.multiple_of(col * CB, CB), CB), :]
            wide = panel.astype(jnp.float32)
            offs = 0.5 * jnp.sum(wide * wide, axis=1, keepdims=True)
            raw = lax.dot_general(panel, part, transposed, preferred_element_type=jnp.float32)
            scores = (raw - offs) * scale
            score_ref[slot] = scores
            return jnp.maximum(top, jnp.max(scores, axis=0, keepdims=True))

        top = lax.fori_loop(0, count, score_turn, jnp.full((1, RB), neg_big, jnp.float32))

        def sum_turn(slot, total):
            return total + jnp.sum(jnp.exp(score_ref[slot] - top), axis=0, keepdims=True)

        total = lax.fori_loop(0, count, sum_turn, jnp.zeros((1, RB), jnp.float32))
        norm = top + jnp.log(total)
        norm_ref[r] = norm

        def weight_turn(slot, carry):
            col = tab_ref[r, 1 + slot]
            weight_ref[r, col] = jnp.exp(score_ref[slot] - norm).astype(jnp.bfloat16)
            return carry

        lax.fori_loop(0, count, weight_turn, 0)

    def col_turn(col, carry):
        acc_ref[...] = jnp.zeros_like(acc_ref)
        row_mass[...] = jnp.zeros_like(row_mass)
        for r in range(local):
            hit = jnp.int32(0)
            for slot in range(SLOTS):
                found = jnp.logical_and(tab_ref[r, 1 + slot] == col, slot < tab_ref[r, 0])
                hit = hit + found.astype(jnp.int32)

            @pl.when(hit > 0)
            def _():
                weights = weight_ref[r, col]
                acc_ref[...] += jnp.dot(
                    weights, rows_ref[r * RB : (r + 1) * RB, :], preferred_element_type=jnp.float32
                )
                row_mass[...] += lax.dot_general(
                    jnp.ones((8, RB), jnp.bfloat16),
                    weights,
                    transposed,
                    preferred_element_type=jnp.float32,
                )

        for j in range(CB // own):
            owner = col * (CB // own) + j
            zz, ff = owner // nf, lax.rem(owner, nf)
            num_ref[lax.rem(ff, 2), ff // 2, zz] = acc_ref[j * own : (j + 1) * own, :].astype(
                jnp.bfloat16
            )
            mass_ref[owner] = row_mass[:, j * own : (j + 1) * own]
        return carry

    lax.fori_loop(0, NCB, col_turn, 0)


def terms(table, row_data, panels, nb, nf):
    local = row_data.shape[0] // RB
    own = K // (nb * nf)
    vmem = pl.BlockSpec(memory_space=pltpu.VMEM)
    return pl.pallas_call(
        functools.partial(term_kernel, nb, nf),
        out_shape=(
            jax.ShapeDtypeStruct((2, nf // 2, nb, own, D), jnp.bfloat16),
            jax.ShapeDtypeStruct((nb * nf, 8, own), jnp.float32),
            jax.ShapeDtypeStruct((local, 1, RB), jnp.float32),
        ),
        in_specs=[pl.BlockSpec(memory_space=pltpu.SMEM), vmem, vmem],
        out_specs=(vmem,) * 3,
        scratch_shapes=[
            pltpu.VMEM((SLOTS, CB, RB), jnp.float32),
            pltpu.VMEM((local, NCB, CB, RB), jnp.bfloat16),
            pltpu.VMEM((CB, D), jnp.float32),
            pltpu.VMEM((8, CB), jnp.float32),
        ],
        compiler_params=pltpu.CompilerParams(vmem_limit_bytes=32 * 2**20),
        name="terms",
    )(table, row_data, panels)


def reduce_kernel(
    nb, nf, num_ref, mass_ref, out_ref, out_mass,
    from_sib, to_x, from_x, to_z, from_z, from_mass,
    a_send, a_recv, b_send, b_recv, c_send, c_recv, m_send, m_recv,
):
    z = lax.axis_index("blk")
    f = lax.axis_index("feat")
    nx = nf // 2
    n = nb * nf
    me = z * nf + f
    c = lax.rem(f, 2)
    x = f // 2
    sibling = x * 2 + 1 - c
    size = D // PARTS

    def at_offset(d):
        other = lax.rem(me + d, n)
        return {"blk": other // nf, "feat": lax.rem(other, nf)}

    barrier = pltpu.get_barrier_semaphore()

    def greet(d, carry):
        pl.semaphore_signal(barrier, inc=1, device_id=at_offset(d), device_id_type=MESH)
        return carry

    lax.fori_loop(1, n, greet, 0)
    pl.semaphore_wait(barrier, n - 1)

    def cols(t):
        return pl.ds(t * size, size)

    def a_copy(dx, t):
        xx = lax.rem(x + dx, nx)
        return pltpu.make_async_remote_copy(
            src_ref=num_ref.at[1 - c, xx, :, :, cols(t)],
            dst_ref=from_sib.at[xx, :, :, cols(t)],
            send_sem=a_send.at[dx, t],
            recv_sem=a_recv.at[dx, t],
            device_id={"blk": z, "feat": sibling},
            device_id_type=MESH,
        )

    def b_copy(dx, t):
        return pltpu.make_async_remote_copy(
            src_ref=to_x.at[dx - 1, :, :, cols(t)],
            dst_ref=from_x.at[dx - 1, :, :, cols(t)],
            send_sem=b_send.at[dx, t],
            recv_sem=b_recv.at[dx, t],
            device_id={"blk": z, "feat": lax.rem(x + dx, nx) * 2 + c},
            device_id_type=MESH,
        )

    def c_copy(d, t):
        return pltpu.make_async_remote_copy(
            src_ref=to_z.at[d - 1, :, cols(t)],
            dst_ref=from_z.at[d - 1, :, cols(t)],
            send_sem=c_send.at[d, t],
            recv_sem=c_recv.at[d, t],
            device_id={"blk": lax.rem(z + d, nb), "feat": f},
            device_id_type=MESH,
        )

    def m_copy(d):
        return pltpu.make_async_remote_copy(
            src_ref=mass_ref.at[lax.rem(me + d, n)],
            dst_ref=from_mass.at[d],
            send_sem=m_send.at[d],
            recv_sem=m_recv.at[d],
            device_id=at_offset(d),
            device_id_type=MESH,
        )

    def wide(value):
        return value.astype(jnp.float32)

    for t in range(PARTS):
        for dx in range(1, nx):
            a_copy(dx, t).start()
    for t in range(PARTS):
        a_copy(0, t).start()

    def mass_start(d, carry):
        m_copy(d).start()
        return carry

    lax.fori_loop(1, n, mass_start, 0)

    for t in range(PARTS):
        for dx in range(1, nx):
            xx = lax.rem(x + dx, nx)
            a_copy(dx, t).wait()
            for zz in range(nb):
                to_x[dx - 1, zz, :, cols(t)] = (
                    wide(num_ref[c, xx, zz, :, cols(t)]) + wide(from_sib[xx, zz, :, cols(t)])
                ).astype(jnp.bfloat16)
            b_copy(dx, t).start()

    def blk_sum(zz, t):
        total = wide(num_ref[c, x, zz, :, cols(t)]) + wide(from_sib[x, zz, :, cols(t)])
        for dx in range(1, nx):
            total = total + wide(from_x[dx - 1, zz, :, cols(t)])
        return total

    for t in range(PARTS):
        a_copy(0, t).wait()
        for dx in range(1, nx):
            b_copy(dx, t).wait()
        for d in range(1, nb):
            to_z[d - 1, :, cols(t)] = blk_sum(lax.rem(z + d, nb), t).astype(jnp.bfloat16)
            c_copy(d, t).start()
        out_ref[:, cols(t)] = blk_sum(z, t)

    def mass_end(d, total):
        m_copy(d).wait()
        return total + from_mass[d]

    out_mass[...] = lax.fori_loop(1, n, mass_end, mass_ref[me])

    for t in range(PARTS):
        total = out_ref[:, cols(t)]
        for d in range(1, nb):
            c_copy(d, t).wait()
            total = total + wide(from_z[d - 1, :, cols(t)])
        out_ref[:, cols(t)] = total


def reduce_sums(num, mass, nb, nf):
    own = K // (nb * nf)
    nx = nf // 2
    n = nb * nf
    vmem = pl.BlockSpec(memory_space=pltpu.VMEM)
    dma = pltpu.SemaphoreType.DMA
    return pl.pallas_call(
        functools.partial(reduce_kernel, nb, nf),
        out_shape=(
            jax.ShapeDtypeStruct((own, D), jnp.float32),
            jax.ShapeDtypeStruct((8, own), jnp.float32),
        ),
        in_specs=[vmem] * 2,
        out_specs=(vmem,) * 2,
        scratch_shapes=[
            pltpu.VMEM((nx, nb, own, D), jnp.bfloat16),
            pltpu.VMEM((nx - 1, nb, own, D), jnp.bfloat16),
            pltpu.VMEM((nx - 1, nb, own, D), jnp.bfloat16),
            pltpu.VMEM((nb - 1, own, D), jnp.bfloat16),
            pltpu.VMEM((nb - 1, own, D), jnp.bfloat16),
            pltpu.VMEM((n, 8, own), jnp.float32),
        ]
        + [dma((nx, PARTS))] * 4
        + [dma((nb, PARTS))] * 2
        + [dma((n,))] * 2,
        compiler_params=pltpu.CompilerParams(
            collective_id=1, has_side_effects=True, vmem_limit_bytes=24 * 2**20
        ),
        name="reduce_sums",
    )(num, mass)


def fused_kernel(
    nb, nf, allow_ref, emb_ref, cen_ref, num_ref, mass_ref, norm_ref,
    rows_ref, all_ref, offs_ref, score_ref, top_ref, sum_ref, weight_ref, keep_ref,
    to_sib, from_sib, to_x, from_x, part_ref, to_z, from_z, pair_ref, to_line, from_line,
    swap_out, swap_in, to_mass, from_mass,
    row_send, row_recv, send, recv, own_sem, a_send, a_recv, b_send, b_recv, z_send, z_recv,
    m_send, m_recv, line_send, line_recv, swap_sem,
):
    z = lax.axis_index("blk")
    f = lax.axis_index("feat")
    n = nb * nf
    me = z * nf + f
    c = lax.rem(f, 2)
    x = f // 2
    rows, width = rows_ref.shape[0], emb_ref.shape[1]
    local = rows // RB
    per = K // nb // CB
    half = CB // 2
    own = K // n
    thin = D * 3 // 16
    wide = D - 2 * thin
    sibling = x * 2 + 1 - c
    size = D // CHUNKS
    scale = 1.0 / math.sqrt(D)
    transposed = (((1,), (1,)), ((), ()))

    def at_offset(d):
        other = lax.rem(me + d, n)
        return {"blk": other // nf, "feat": lax.rem(other, nf)}

    barrier = pltpu.get_barrier_semaphore()

    def greet(d, carry):
        pl.semaphore_signal(barrier, inc=1, device_id=at_offset(d), device_id_type=MESH)
        return carry

    lax.fori_loop(1, n, greet, 0)
    pl.semaphore_wait(barrier, n - 1)

    def wide_spot(ref, block, p, cc):
        first = (block * per + p) * CB + cc * half
        return ref.at[pl.ds(pl.multiple_of(first, half), half), pl.ds(0, wide)]

    def thin_spot(ref, block, cc, xx):
        count = per * half
        return ref.at[
            pl.ds(pl.multiple_of((block * 2 + cc) * count, count), count),
            pl.ds(pl.multiple_of(wide + xx * thin, 128), thin),
        ]

    def remote(src, dst, kind, d, blk, feat):
        return pltpu.make_async_remote_copy(
            src_ref=src,
            dst_ref=dst,
            send_sem=send.at[kind, d],
            recv_sem=recv.at[kind, d],
            device_id={"blk": blk, "feat": feat},
            device_id_type=MESH,
        )

    started = []

    def go(cond, copy):
        pl.when(cond)(copy.start)
        started.append((cond, copy))

    piece_rows = rows // PIECES

    def row_copy(d, piece):
        to = lax.rem(f + d, nf)
        return pltpu.make_async_remote_copy(
            src_ref=emb_ref.at[
                pl.ds(pl.multiple_of(to * rows + piece * piece_rows, piece_rows), piece_rows), :
            ],
            dst_ref=rows_ref.at[
                pl.ds(piece * piece_rows, piece_rows),
                pl.ds(pl.multiple_of(f * width, width), width),
            ],
            send_sem=row_send.at[d, piece],
            recv_sem=row_recv.at[d, piece],
            device_id={"blk": z, "feat": to},
            device_id_type=MESH,
        )

    def step(way):
        return jnp.clip(z + 1 - 2 * way, 0, nb - 1)

    def onward(way):
        return (z + 1 < nb) if way == 0 else (z > 0)

    def source(way, hop):
        zz = z - hop if way == 0 else z + hop
        return (zz >= 0) if way == 0 else (zz < nb), jnp.clip(zz, 0, nb - 1)

    def arrived(cond, kind, d, here):
        pl.when(cond)(remote(here, here, kind, d, z, sibling).wait_recv)
        return here

    def pass_thin(way, hop):
        cond, zz = source(way, hop)
        d = (way * nb + hop) * per
        here = arrived(cond, 0, d, thin_spot(all_ref, zz, c, x))
        if hop + 1 < nb:
            go(jnp.logical_and(cond, onward(way)), remote(here, here, 0, d + per, step(way), f))
        go(cond, remote(here, here, 1, d, z, (1 - x) * 2 + c))
        go(cond, remote(here, here, 2, d, z, sibling))

    def pass_wide(way, hop, p):
        cond, zz = source(way, hop)
        d = (way * nb + hop) * per + p
        here = arrived(cond, 4, d, wide_spot(all_ref, zz, p, c))
        if hop + 1 < nb:
            go(jnp.logical_and(cond, onward(way)), remote(here, here, 4, d + per, step(way), f))
        go(cond, remote(here, here, 5, d, z, sibling))

    def pass_across(way, hop):
        cond, zz = source(way, hop)
        d = (way * nb + hop) * per
        here = arrived(cond, 1, d, thin_spot(all_ref, zz, c, 1 - x))
        go(cond, remote(here, here, 3, d, z, sibling))

    def have_thin(way, hop):
        cond, zz = source(way, hop)
        d = (way * nb + hop) * per
        arrived(cond, 2, d, thin_spot(all_ref, zz, 1 - c, x))
        arrived(cond, 3, d, thin_spot(all_ref, zz, 1 - c, 1 - x))

    def have_wide(way, hop, p):
        cond, zz = source(way, hop)
        arrived(cond, 5, (way * nb + hop) * per + p, wide_spot(all_ref, zz, p, 1 - c))

    def both(turn, *where):
        for way in range(2):
            turn(way, *where)

    def panel_turns(hop, first, last, turn):
        def one(t, carry):
            way, p = lax.rem(t, 2), t // 2
            zz = z + (2 * way - 1) * hop
            fits = jnp.logical_and(zz >= 0, zz < nb)
            fits = jnp.logical_and(fits, jnp.logical_or(hop > 0, way == 0))

            @pl.when(fits)
            def _():
                turn(zz * per + p)

            return carry

        lax.fori_loop(first * 2, last * 2, one, 0)

    def scores(hop, first, last, row_blocks):
        span = len(row_blocks) * RB
        low = row_blocks[0]

        def turn(col):
            panel = all_ref[pl.ds(pl.multiple_of(col * CB, CB), CB), :]
            if low == 0:
                wider = panel.astype(jnp.float32)
                offs = 0.5 * jnp.sum(wider * wider, axis=1, keepdims=True)
                if len(row_blocks) < local:
                    offs_ref[col] = offs
            else:
                offs = offs_ref[col]
            raw = lax.dot_general(
                panel,
                rows_ref[low * RB : low * RB + span, :],
                transposed,
                preferred_element_type=jnp.float32,
            )
            for r in row_blocks:
                part = raw[:, (r - low) * RB : (r - low + 1) * RB]
                value = jnp.where(allow_ref[r, col] > 0, (part - offs) * scale, neg_big)
                score_ref[r, col] = value
                old = top_ref[r]
                top = jnp.maximum(old, jnp.max(value, axis=0, keepdims=True))
                sum_ref[r] = sum_ref[r] * jnp.exp(old - top) + jnp.sum(
                    jnp.exp(value - top), axis=0, keepdims=True
                )
                top_ref[r] = top

        panel_turns(hop, first, last, turn)

    first_pieces = PIECES // local
    for way in range(2):
        d = (way * nb + 1) * per
        mine = thin_spot(cen_ref, 0, c, x)
        go(onward(way), remote(mine, thin_spot(all_ref, z, c, x), 0, d, step(way), f))
    for p in range(per):
        for way in range(2):
            d = (way * nb + 1) * per + p
            mine = wide_spot(cen_ref, 0, p, c)
            go(onward(way), remote(mine, wide_spot(all_ref, z, p, c), 4, d, step(way), f))
    row_copies = [[row_copy(d, piece) for d in range(1, nf)] for piece in range(PIECES)]
    for piece in range(first_pieces):
        for copy in row_copies[piece]:
            copy.start()
    loads = [
        pltpu.make_async_copy(
            emb_ref.at[pl.ds(pl.multiple_of(f * rows, rows), rows), :],
            rows_ref.at[:, pl.ds(pl.multiple_of(f * width, width), width)],
            own_sem.at[0],
        ),
        pltpu.make_async_copy(
            cen_ref, all_ref.at[pl.ds(pl.multiple_of(z * per * CB, CB), per * CB), :], own_sem.at[1]
        ),
    ]
    for copy in loads:
        copy.start()
    top_ref[...] = jnp.full_like(top_ref, neg_big)
    sum_ref[...] = jnp.zeros_like(sum_ref)
    early = list(range(1))
    late = list(range(1, local))
    both(pass_thin, 1)
    for piece in range(first_pieces, PIECES):
        for copy in row_copies[piece]:
            copy.start()
    for copy in loads:
        copy.wait()
    for p in range(per):
        both(pass_wide, 1, p)
    both(pass_thin, 2)
    for piece in range(first_pieces):
        for copy in row_copies[piece]:
            copy.wait_recv()
    scores(0, 0, per, early)
    both(pass_across, 1)
    both(have_thin, 1)
    for p in range(per):
        both(have_wide, 1, p)
    scores(1, 0, per, early)
    for p in range(per):
        both(pass_wide, 2, p)
    for hop in range(3, nb):
        both(pass_thin, hop)
        for p in range(per):
            if hop < nb - 1 or p < per - 1:
                both(pass_wide, hop, p)
    for piece in range(first_pieces, PIECES):
        for copy in row_copies[piece]:
            copy.wait_recv()
    scores(0, 0, per, late)
    scores(1, 0, per, late)
    for hop in range(2, nb):
        both(pass_across, hop)
        both(have_thin, hop)
        for p in range(per):
            both(have_wide, hop, p)
            scores(hop, p, p + 1, early + late)
            if hop == nb - 2 and p == per - 2:
                both(pass_wide, nb - 1, per - 1)

    for r in range(local):
        norm = top_ref[r] + jnp.log(sum_ref[r])
        norm_ref[r] = norm
        top_ref[r] = norm

    lead = 0

    def cols(t):
        return pl.ds(pl.multiple_of(t * size, size), size)

    left, right = jnp.int32(0), jnp.int32(nb - 1)
    turns = []
    for _ in range(nb):
        pick = (z - left) >= (right - z)
        turns.append(jnp.where(pick, left, right))
        left, right = jnp.where(pick, left + 1, left), jnp.where(pick, right, right - 1)

    def a_copy(q, t):
        return pltpu.make_async_remote_copy(
            src_ref=to_sib.at[q, :, cols(t)],
            dst_ref=from_sib.at[q, :, cols(t)],
            send_sem=a_send.at[q, t],
            recv_sem=a_recv.at[q, t],
            device_id={"blk": z, "feat": sibling},
            device_id_type=MESH,
        )

    def b_copy(i, t):
        return pltpu.make_async_remote_copy(
            src_ref=to_x.at[i, :, cols(t)],
            dst_ref=from_x.at[i, :, cols(t)],
            send_sem=b_send.at[i, t],
            recv_sem=b_recv.at[i, t],
            device_id={"blk": z, "feat": (1 - x) * 2 + c},
            device_id_type=MESH,
        )

    def z_copy(zz, way, t):
        return pltpu.make_async_remote_copy(
            src_ref=to_z.at[zz, :, cols(t)],
            dst_ref=from_z.at[way, zz, :, cols(t)],
            send_sem=z_send.at[zz, t],
            recv_sem=z_recv.at[way, zz, t],
            device_id={"blk": jnp.clip(z + 1 - 2 * way, 0, nb - 1), "feat": f},
            device_id_type=MESH,
        )

    def line_copy(d):
        zz = lax.rem(z + d, nb)
        return pltpu.make_async_remote_copy(
            src_ref=to_line.at[zz],
            dst_ref=from_line.at[d - 1],
            send_sem=line_send.at[d],
            recv_sem=line_recv.at[d],
            device_id={"blk": zz, "feat": f},
            device_id_type=MESH,
        )

    def swap_copy():
        return pltpu.make_async_remote_copy(
            src_ref=swap_out,
            dst_ref=swap_in,
            send_sem=swap_sem.at[0],
            recv_sem=swap_sem.at[1],
            device_id={"blk": z, "feat": (1 - x) * 2 + c},
            device_id_type=MESH,
        )

    def m_copy(d):
        return pltpu.make_async_remote_copy(
            src_ref=to_mass.at[lax.rem(me + d, n)],
            dst_ref=from_mass.at[d],
            send_sem=m_send.at[d],
            recv_sem=m_recv.at[d],
            device_id=at_offset(d),
            device_id_type=MESH,
        )

    def wide_of(value):
        return value.astype(jnp.float32)

    def place(i):
        zz = turns[nb - 1]
        for t in range(nb - 1):
            zz = jnp.where(i == t, turns[t], zz)
        return zz

    group = CHUNKS // SPANS

    def weights(i, side):
        zz = place(i)
        xx = 1 - x if side == 0 else x
        col = zz * per + xx
        part = slice(side * CB, (side + 1) * CB)
        for cc in range(2):
            at = c if cc == 0 else 1 - c
            first = side * CB + cc * own
            for r in range(local):
                value = score_ref[r, col, pl.ds(pl.multiple_of(at * own, own), own), :]
                weight_ref[first : first + own, r * RB : (r + 1) * RB] = jnp.exp(
                    value - top_ref[r]
                ).astype(jnp.bfloat16)
        mass = lax.dot_general(
            jnp.ones((8, rows), jnp.bfloat16),
            weight_ref[part, :],
            transposed,
            preferred_element_type=jnp.float32,
        )
        to_mass[zz * nf + xx * 2 + c] = mass[:, :own]
        to_mass[zz * nf + xx * 2 + 1 - c] = mass[:, own:]

    def sums(i):
        for side in range(2):
            weights(i, side)

        def span(u, carry):
            @pl.when(u < SPANS)
            def _():
                at = pl.ds(pl.multiple_of(u * group * size, group * size), group * size)
                total = jnp.dot(
                    weight_ref[...], rows_ref[:, at], preferred_element_type=jnp.float32
                )
                for side in range(2):
                    first = side * CB
                    keep_ref[side * nb + i, :, at] = total[first : first + own]
                    to_sib[side * nb + i, :, at] = total[first + own : first + CB].astype(jnp.bfloat16)
                for side in range(2):
                    for t in range(group):
                        a_copy(side * nb + i, u * group + t).start()

            @pl.when(u == 1)
            def _():
                send_line(i)

            @pl.when(u > 0)
            def _():
                for t in range(group):
                    at = (u - 1) * group + t
                    pl.when(at > lead)(functools.partial(send_x, i, at))

            return carry

        lax.fori_loop(0, SPANS + 1, span, 0)

    def send_x(i, t):
        a_copy(i, t).wait()
        to_x[i, :, cols(t)] = (
            keep_ref[i, :, cols(t)] + wide_of(from_sib[i, :, cols(t)])
        ).astype(jnp.bfloat16)
        b_copy(i, t).start()

    def course(i):
        zz = place(i)
        fed = jnp.logical_or(
            jnp.logical_and(zz > z, z > 0), jnp.logical_and(zz < z, z < nb - 1)
        )
        return zz, (zz < z).astype(jnp.int32), fed

    def send_line(i):
        zz = place(i)
        for side in range(2):
            q = side * nb + i
            a_copy(q, lead).wait()
            pair_ref[side] = keep_ref[q, :, cols(lead)] + wide_of(from_sib[q, :, cols(lead)])

        @pl.when(zz != z)
        def _():
            to_line[zz] = pair_ref[...].astype(jnp.bfloat16)
            line_copy(lax.rem(zz - z + nb, nb)).start()

    def swap():
        def one(d, carry):
            line_copy(d).wait()
            pair_ref[...] += wide_of(from_line[d - 1])
            return carry

        lax.fori_loop(1, nb, one, 0)
        swap_out[...] = pair_ref[0].astype(jnp.bfloat16)
        swap_copy().start()
        num_ref[:, cols(lead)] = pair_ref[1]

    def send_z(i):
        zz, way, fed = course(i)
        q = nb + i

        def chunk(t, carry):
            a_copy(q, t).wait()
            b_copy(i, t).wait()
            part_ref[...] = (
                keep_ref[q, :, cols(t)]
                + wide_of(from_sib[q, :, cols(t)])
                + wide_of(from_x[i, :, cols(t)])
            )

            @pl.when(fed)
            def _():
                z_copy(zz, way, t).wait_recv()
                part_ref[...] += wide_of(from_z[way, zz, :, cols(t)])

            @pl.when(zz != z)
            def _():
                to_z[zz, :, cols(t)] = part_ref[...].astype(jnp.bfloat16)
                z_copy(zz, way, t).start()

            @pl.when(zz == z)
            def _():
                num_ref[:, cols(t)] = part_ref[...]

            return carry

        lax.fori_loop(lead + 1, CHUNKS, chunk, 0)

    def turn(i, carry):
        @pl.when(i < nb)
        def _():
            sums(i)

        @pl.when(i == nb - 1)
        def _():
            def mass_start(d, carry):
                m_copy(d).start()
                return carry

            lax.fori_loop(1, n, mass_start, 0)

        pl.when(i == nb)(swap)

        @pl.when(i > 0)
        def _():
            send_z(i - 1)

        return carry

    lax.fori_loop(0, nb + 1, turn, 0)

    def mass_end(d, total):
        m_copy(d).wait()
        return total + from_mass[d]

    mass_ref[...] = lax.fori_loop(1, n, mass_end, to_mass[me])

    def last(t, carry):
        for way in range(2):

            @pl.when((z > 0) if way == 0 else (z < nb - 1))
            def _():
                z_copy(z, way, t).wait_recv()
                num_ref[:, cols(t)] += wide_of(from_z[way, z, :, cols(t)])

        for zz in range(nb):

            @pl.when(z != zz)
            def _():
                z_copy(zz, 0, t).wait_send()

        return carry

    lax.fori_loop(lead + 1, CHUNKS, last, 0)
    swap_copy().wait()
    num_ref[:, cols(lead)] += wide_of(swap_in[...])
    for group in row_copies:
        for copy in group:
            copy.wait_send()
    for cond, copy in started:
        pl.when(cond)(copy.wait_send)


def fused(allow, embeddings, centroids, nb, nf):
    rows = embeddings.shape[0] // nf
    local = rows // RB
    n = nb * nf
    own = K // n
    per = K // nb // CB
    kinds = 6
    vmem = pl.BlockSpec(memory_space=pltpu.VMEM)
    hbm = pl.BlockSpec(memory_space=pltpu.HBM)
    dma = pltpu.SemaphoreType.DMA
    bf16, f32 = jnp.bfloat16, jnp.float32
    return pl.pallas_call(
        functools.partial(fused_kernel, nb, nf),
        out_shape=(
            jax.ShapeDtypeStruct((own, D), f32),
            jax.ShapeDtypeStruct((8, own), f32),
            jax.ShapeDtypeStruct((local, 1, RB), f32),
        ),
        in_specs=[pl.BlockSpec(memory_space=pltpu.SMEM), hbm, hbm],
        out_specs=(vmem,) * 3,
        scratch_shapes=[
            pltpu.VMEM((rows, D), bf16),
            pltpu.VMEM((K, D), bf16),
            pltpu.VMEM((NCB, CB, 1), f32),
            pltpu.VMEM((local, NCB, CB, RB), f32),
            pltpu.VMEM((local, 1, RB), f32),
            pltpu.VMEM((local, 1, RB), f32),
            pltpu.VMEM((2 * CB, rows), bf16),
            pltpu.VMEM((2 * nb, own, D), f32),
            pltpu.VMEM((2 * nb, own, D), bf16),
            pltpu.VMEM((2 * nb, own, D), bf16),
            pltpu.VMEM((nb, own, D), bf16),
            pltpu.VMEM((nb, own, D), bf16),
            pltpu.VMEM((own, D // CHUNKS), f32),
            pltpu.VMEM((nb, own, D), bf16),
            pltpu.VMEM((2, nb, own, D), bf16),
            pltpu.VMEM((2, own, D // CHUNKS), f32),
            pltpu.VMEM((nb, 2, own, D // CHUNKS), bf16),
            pltpu.VMEM((nb - 1, 2, own, D // CHUNKS), bf16),
            pltpu.VMEM((own, D // CHUNKS), bf16),
            pltpu.VMEM((own, D // CHUNKS), bf16),
            pltpu.VMEM((n, 8, own), f32),
            pltpu.VMEM((n, 8, own), f32),
            dma((nf, PIECES)),
            dma((nf, PIECES)),
            dma((kinds, 2 * nb * per)),
            dma((kinds, 2 * nb * per)),
            dma((2,)),
            dma((2 * nb, CHUNKS)),
            dma((2 * nb, CHUNKS)),
            dma((nb, CHUNKS)),
            dma((nb, CHUNKS)),
            dma((nb, CHUNKS)),
            dma((2, nb, CHUNKS)),
            dma((n,)),
            dma((n,)),
            dma((nb,)),
            dma((nb,)),
            dma((2,)),
        ],
        compiler_params=pltpu.CompilerParams(
            collective_id=2, has_side_effects=True, vmem_limit_bytes=58 * 2**20
        ),
        name="fused",
    )(allow, embeddings, centroids)


def body(embeddings, centroids, pair_list):
    nb, nf = lax.axis_size("blk"), lax.axis_size("feat")
    local_rows = embeddings.shape[0] // nf
    local_blocks = local_rows // RB
    device_index = lax.axis_index("blk") * nf + lax.axis_index("feat")
    mine = device_index * local_blocks + jnp.arange(local_blocks, dtype=jnp.int32)
    row_ids, col_ids = pair_list[:, 0], pair_list[:, 1]
    same = row_ids[None, :] == mine[:, None]
    if K // nb == 2 * CB and nf == 4 and local_blocks == 2:
        blocks = jnp.arange(NCB, dtype=jnp.int32)
        allow = jnp.sum(
            (same[:, None, :] & (col_ids[None, None, :] == blocks[None, :, None])).astype(jnp.int32),
            axis=2,
        )
        numerator, denominator, log_norm = fused(allow, embeddings, centroids, nb, nf)
    else:
        before = jnp.sum((row_ids[None, :] < mine[:, None]).astype(jnp.int32), axis=1)
        counts = jnp.sum(same.astype(jnp.int32), axis=1)
        rank = jnp.arange(row_ids.shape[0], dtype=jnp.int32)[None, :] - before[:, None]
        slots = jnp.arange(SLOTS, dtype=jnp.int32)
        picked = same[:, None, :] & (rank[:, None, :] == slots[None, :, None])
        chosen = jnp.sum(jnp.where(picked, col_ids[None, None, :], 0), axis=2)
        table = jnp.concatenate([counts[:, None], chosen], axis=1)
        row_data, panels = fetch(embeddings, centroids, nb, nf)
        num, mass, log_norm = terms(table, row_data, panels, nb, nf)
        numerator, denominator = reduce_sums(num, mass, nb, nf)

    own_count = centroids.shape[0] // nf
    own_rows = lax.dynamic_slice_in_dim(
        centroids, lax.axis_index("feat") * own_count, own_count, 0
    ).astype(jnp.float32)
    new_centroids = (numerator + prior_mass * own_rows) / (denominator[0][:, None] + prior_mass)
    return (new_centroids, log_norm.reshape(local_rows))


def solution(mesh):
    return jax.shard_map(
        body,
        mesh=mesh,
        in_specs=(P(("groups", "blk"), "feat"), P(("groups", "blk"), None), P("groups", None)),
        out_specs=(P(("groups", "blk", "feat"), None), P(("groups", "blk", "feat"))),
        check_vma=False,
    )
```

```python
import functools
import math

import jax
import jax.numpy as jnp
from jax import lax
from jax.experimental import pallas as pl
from jax.experimental.pallas import tpu as pltpu
from jax.sharding import PartitionSpec as P

D = 2048
K = 2048
RB = 512
CB = 256
NCB = K // CB
SLOTS = 4
PARTS = 8
PIECES = 8
CHUNKS = 8
SPANS = 4

neg_big = -1e30
prior_mass = 16.0
MESH = pl.DeviceIdType.MESH


def meet(peers):
    barrier = pltpu.get_barrier_semaphore()
    for peer in peers:
        pl.semaphore_signal(barrier, inc=1, device_id=peer, device_id_type=MESH)
    pl.semaphore_wait(barrier, len(peers))


def fetch_kernel(
    nb, nf, emb_ref, cen_ref, rows_ref, all_ref, row_send, row_recv, send, recv, own_sem,
    emb_hold, cen_hold,
):
    z = lax.axis_index("blk")
    f = lax.axis_index("feat")
    nx = nf // 2
    c = lax.rem(f, 2)
    x = f // 2
    rows, width = rows_ref.shape[0], emb_ref.shape[1]
    half = cen_ref.shape[0] // 2
    thin = D * 3 // 8 // nx // 128 * 128
    wide = D - nx * thin
    sibling = x * 2 + 1 - c

    def across(dx):
        return lax.rem(x + dx, nx)

    meet(
        [{"blk": z, "feat": lax.rem(f + d, nf)} for d in range(1, nf)]
        + [{"blk": lax.rem(z + d, nb), "feat": f} for d in range(1, nb)]
    )

    def spot(zz, cc, col, size):
        return all_ref.at[
            pl.ds(pl.multiple_of(zz * 2 * half + cc * half, half), half),
            pl.ds(pl.multiple_of(col, 128), size),
        ]

    def remote(src, dst, kind, d, blk, feat):
        return pltpu.make_async_remote_copy(
            src_ref=src,
            dst_ref=dst,
            send_sem=send.at[kind, d],
            recv_sem=recv.at[kind, d],
            device_id={"blk": blk, "feat": feat},
            device_id_type=MESH,
        )

    def own_part(col, size):
        return cen_ref.at[
            pl.ds(pl.multiple_of(c * half, half), half), pl.ds(pl.multiple_of(col, 128), size)
        ]

    thin_col = wide + x * thin
    started = []

    def go(cond, copy):
        pl.when(cond)(copy.start)
        started.append((cond, copy))

    def row_copy(d, piece):
        to = lax.rem(f + d, nf)
        size = rows // PIECES
        return pltpu.make_async_remote_copy(
            src_ref=emb_ref.at[pl.ds(pl.multiple_of(to * rows + piece * size, size), size), :],
            dst_ref=rows_ref.at[
                pl.ds(piece * size, size), pl.ds(pl.multiple_of(f * width, width), width)
            ],
            send_sem=row_send.at[d, piece],
            recv_sem=row_recv.at[d, piece],
            device_id={"blk": z, "feat": to},
            device_id_type=MESH,
        )

    def step(way):
        return jnp.clip(z + 1 - 2 * way, 0, nb - 1)

    def onward(way):
        return (z + 1 < nb) if way == 0 else (z > 0)

    for way in range(2):
        go(
            onward(way),
            remote(own_part(thin_col, thin), spot(z, c, thin_col, thin), 1, way * nb + 1, step(way), f),
        )
    for way in range(2):
        go(onward(way), remote(own_part(0, wide), spot(z, c, 0, wide), 0, way * nb + 1, step(way), f))
    row_copies = [row_copy(d, piece) for piece in range(PIECES) for d in range(1, nf)]
    for copy in row_copies:
        copy.start()
    holds = [
        (
            emb_ref.at[pl.ds(pl.multiple_of(f * rows, rows), rows), :],
            emb_hold,
            rows_ref.at[:, pl.ds(pl.multiple_of(f * width, width), width)],
        ),
        (
            cen_ref,
            cen_hold,
            all_ref.at[pl.ds(pl.multiple_of(z * 2 * half, half), 2 * half), :],
        ),
    ]
    loads = [pltpu.make_async_copy(src, hold, own_sem.at[i]) for i, (src, hold, _) in enumerate(holds)]
    stores = [
        pltpu.make_async_copy(hold, dst, own_sem.at[2 + i]) for i, (_, hold, dst) in enumerate(holds)
    ]
    for copy in loads:
        copy.start()
    for load, store in zip(loads, stores):
        load.wait()
        store.start()

    def source(way, hop):
        zz = z - hop if way == 0 else z + hop
        return (zz >= 0) if way == 0 else (zz < nb), jnp.clip(zz, 0, nb - 1)

    def arrived(cond, kind, d, zz, cc, col, size):
        here = spot(zz, cc, col, size)
        pl.when(cond)(remote(here, here, kind, d, z, sibling).wait_recv)
        return here

    turns = [(way, hop) for hop in range(1, nb) for way in range(2)]

    def pass_thin(way, hop):
        cond, zz = source(way, hop)
        d = way * nb + hop
        here = arrived(cond, 1, d, zz, c, thin_col, thin)
        if hop + 1 < nb:
            go(jnp.logical_and(cond, onward(way)), remote(here, here, 1, d + 1, step(way), f))
        for dx in range(1, nx):
            go(cond, remote(here, here, 4 + dx, d, z, across(dx) * 2 + c))
        go(cond, remote(here, here, 3, d, z, sibling))

    def pass_wide(way, hop):
        cond, zz = source(way, hop)
        d = way * nb + hop
        here = arrived(cond, 0, d, zz, c, 0, wide)
        if hop + 1 < nb:
            go(jnp.logical_and(cond, onward(way)), remote(here, here, 0, d + 1, step(way), f))
        go(cond, remote(here, here, 2, d, z, sibling))

    def pass_across(way, hop):
        cond, zz = source(way, hop)
        d = way * nb + hop
        for dx in range(1, nx):
            col = wide + lax.rem(x + nx - dx, nx) * thin
            here = arrived(cond, 4 + dx, d, zz, c, col, thin)
            go(cond, remote(here, here, 4 + nx + dx, d, z, sibling))

    for hop in range(1, nb):
        for way in range(2):
            pass_thin(way, hop)
        for way in range(2):
            pass_wide(way, hop)
    for way, hop in turns:
        pass_across(way, hop)
    for way, hop in turns:
        cond, zz = source(way, hop)
        d = way * nb + hop
        arrived(cond, 2, d, zz, 1 - c, 0, wide)
        arrived(cond, 3, d, zz, 1 - c, thin_col, thin)
        for dx in range(1, nx):
            col = wide + lax.rem(x + nx - dx, nx) * thin
            arrived(cond, 4 + nx + dx, d, zz, 1 - c, col, thin)
    for copy in stores:
        copy.wait()
    for copy in row_copies:
        copy.wait()
    for cond, copy in started:
        pl.when(cond)(copy.wait_send)


def fetch(embeddings, centroids, nb, nf):
    rows = embeddings.shape[0] // nf
    kinds = 4 + 2 * (nf // 2) + 1
    return pl.pallas_call(
        functools.partial(fetch_kernel, nb, nf),
        out_shape=(
            jax.ShapeDtypeStruct((rows, D), jnp.bfloat16),
            jax.ShapeDtypeStruct((K, D), jnp.bfloat16),
        ),
        in_specs=[pl.BlockSpec(memory_space=pltpu.HBM)] * 2,
        out_specs=(pl.BlockSpec(memory_space=pl.ANY),) * 2,
        scratch_shapes=[
            pltpu.SemaphoreType.DMA((nf, PIECES)),
            pltpu.SemaphoreType.DMA((nf, PIECES)),
            pltpu.SemaphoreType.DMA((kinds, 2 * nb)),
            pltpu.SemaphoreType.DMA((kinds, 2 * nb)),
            pltpu.SemaphoreType.DMA((4,)),
            pltpu.VMEM((rows, D // nf), jnp.bfloat16),
            pltpu.VMEM((K // nb, D), jnp.bfloat16),
        ],
        compiler_params=pltpu.CompilerParams(
            collective_id=0, has_side_effects=True, vmem_limit_bytes=6 * 2**20
        ),
        name="fetch",
    )(embeddings, centroids)


def term_kernel(nb, nf, tab_ref, rows_ref, all_ref, num_ref, mass_ref, norm_ref, score_ref, weight_ref, acc_ref, row_mass):
    local = rows_ref.shape[0] // RB
    scale = 1.0 / math.sqrt(D)
    own = K // (nb * nf)
    nx = nf // 2
    transposed = (((1,), (1,)), ((), ()))

    for r in range(local):
        part = rows_ref[r * RB : (r + 1) * RB, :]
        count = tab_ref[r, 0]

        def score_turn(slot, top):
            col = tab_ref[r, 1 + slot]
            panel = all_ref[pl.ds(pl.multiple_of(col * CB, CB), CB), :]
            wide = panel.astype(jnp.float32)
            offs = 0.5 * jnp.sum(wide * wide, axis=1, keepdims=True)
            raw = lax.dot_general(panel, part, transposed, preferred_element_type=jnp.float32)
            scores = (raw - offs) * scale
            score_ref[slot] = scores
            return jnp.maximum(top, jnp.max(scores, axis=0, keepdims=True))

        top = lax.fori_loop(0, count, score_turn, jnp.full((1, RB), neg_big, jnp.float32))

        def sum_turn(slot, total):
            return total + jnp.sum(jnp.exp(score_ref[slot] - top), axis=0, keepdims=True)

        total = lax.fori_loop(0, count, sum_turn, jnp.zeros((1, RB), jnp.float32))
        norm = top + jnp.log(total)
        norm_ref[r] = norm

        def weight_turn(slot, carry):
            col = tab_ref[r, 1 + slot]
            weight_ref[r, col] = jnp.exp(score_ref[slot] - norm).astype(jnp.bfloat16)
            return carry

        lax.fori_loop(0, count, weight_turn, 0)

    def col_turn(col, carry):
        acc_ref[...] = jnp.zeros_like(acc_ref)
        row_mass[...] = jnp.zeros_like(row_mass)
        for r in range(local):
            hit = jnp.int32(0)
            for slot in range(SLOTS):
                found = jnp.logical_and(tab_ref[r, 1 + slot] == col, slot < tab_ref[r, 0])
                hit = hit + found.astype(jnp.int32)

            @pl.when(hit > 0)
            def _():
                weights = weight_ref[r, col]
                acc_ref[...] += jnp.dot(
                    weights, rows_ref[r * RB : (r + 1) * RB, :], preferred_element_type=jnp.float32
                )
                row_mass[...] += lax.dot_general(
                    jnp.ones((8, RB), jnp.bfloat16),
                    weights,
                    transposed,
                    preferred_element_type=jnp.float32,
                )

        for j in range(CB // own):
            owner = col * (CB // own) + j
            zz, ff = owner // nf, lax.rem(owner, nf)
            num_ref[lax.rem(ff, 2), ff // 2, zz] = acc_ref[j * own : (j + 1) * own, :].astype(
                jnp.bfloat16
            )
            mass_ref[owner] = row_mass[:, j * own : (j + 1) * own]
        return carry

    lax.fori_loop(0, NCB, col_turn, 0)


def terms(table, row_data, panels, nb, nf):
    local = row_data.shape[0] // RB
    own = K // (nb * nf)
    vmem = pl.BlockSpec(memory_space=pltpu.VMEM)
    return pl.pallas_call(
        functools.partial(term_kernel, nb, nf),
        out_shape=(
            jax.ShapeDtypeStruct((2, nf // 2, nb, own, D), jnp.bfloat16),
            jax.ShapeDtypeStruct((nb * nf, 8, own), jnp.float32),
            jax.ShapeDtypeStruct((local, 1, RB), jnp.float32),
        ),
        in_specs=[pl.BlockSpec(memory_space=pltpu.SMEM), vmem, vmem],
        out_specs=(vmem,) * 3,
        scratch_shapes=[
            pltpu.VMEM((SLOTS, CB, RB), jnp.float32),
            pltpu.VMEM((local, NCB, CB, RB), jnp.bfloat16),
            pltpu.VMEM((CB, D), jnp.float32),
            pltpu.VMEM((8, CB), jnp.float32),
        ],
        compiler_params=pltpu.CompilerParams(vmem_limit_bytes=32 * 2**20),
        name="terms",
    )(table, row_data, panels)


def reduce_kernel(
    nb, nf, num_ref, mass_ref, out_ref, out_mass,
    from_sib, to_x, from_x, to_z, from_z, from_mass,
    a_send, a_recv, b_send, b_recv, c_send, c_recv, m_send, m_recv,
):
    z = lax.axis_index("blk")
    f = lax.axis_index("feat")
    nx = nf // 2
    n = nb * nf
    me = z * nf + f
    c = lax.rem(f, 2)
    x = f // 2
    sibling = x * 2 + 1 - c
    size = D // PARTS

    def at_offset(d):
        other = lax.rem(me + d, n)
        return {"blk": other // nf, "feat": lax.rem(other, nf)}

    barrier = pltpu.get_barrier_semaphore()

    def greet(d, carry):
        pl.semaphore_signal(barrier, inc=1, device_id=at_offset(d), device_id_type=MESH)
        return carry

    lax.fori_loop(1, n, greet, 0)
    pl.semaphore_wait(barrier, n - 1)

    def cols(t):
        return pl.ds(t * size, size)

    def a_copy(dx, t):
        xx = lax.rem(x + dx, nx)
        return pltpu.make_async_remote_copy(
            src_ref=num_ref.at[1 - c, xx, :, :, cols(t)],
            dst_ref=from_sib.at[xx, :, :, cols(t)],
            send_sem=a_send.at[dx, t],
            recv_sem=a_recv.at[dx, t],
            device_id={"blk": z, "feat": sibling},
            device_id_type=MESH,
        )

    def b_copy(dx, t):
        return pltpu.make_async_remote_copy(
            src_ref=to_x.at[dx - 1, :, :, cols(t)],
            dst_ref=from_x.at[dx - 1, :, :, cols(t)],
            send_sem=b_send.at[dx, t],
            recv_sem=b_recv.at[dx, t],
            device_id={"blk": z, "feat": lax.rem(x + dx, nx) * 2 + c},
            device_id_type=MESH,
        )

    def c_copy(d, t):
        return pltpu.make_async_remote_copy(
            src_ref=to_z.at[d - 1, :, cols(t)],
            dst_ref=from_z.at[d - 1, :, cols(t)],
            send_sem=c_send.at[d, t],
            recv_sem=c_recv.at[d, t],
            device_id={"blk": lax.rem(z + d, nb), "feat": f},
            device_id_type=MESH,
        )

    def m_copy(d):
        return pltpu.make_async_remote_copy(
            src_ref=mass_ref.at[lax.rem(me + d, n)],
            dst_ref=from_mass.at[d],
            send_sem=m_send.at[d],
            recv_sem=m_recv.at[d],
            device_id=at_offset(d),
            device_id_type=MESH,
        )

    def wide(value):
        return value.astype(jnp.float32)

    for t in range(PARTS):
        for dx in range(1, nx):
            a_copy(dx, t).start()
    for t in range(PARTS):
        a_copy(0, t).start()

    def mass_start(d, carry):
        m_copy(d).start()
        return carry

    lax.fori_loop(1, n, mass_start, 0)

    for t in range(PARTS):
        for dx in range(1, nx):
            xx = lax.rem(x + dx, nx)
            a_copy(dx, t).wait()
            for zz in range(nb):
                to_x[dx - 1, zz, :, cols(t)] = (
                    wide(num_ref[c, xx, zz, :, cols(t)]) + wide(from_sib[xx, zz, :, cols(t)])
                ).astype(jnp.bfloat16)
            b_copy(dx, t).start()

    def blk_sum(zz, t):
        total = wide(num_ref[c, x, zz, :, cols(t)]) + wide(from_sib[x, zz, :, cols(t)])
        for dx in range(1, nx):
            total = total + wide(from_x[dx - 1, zz, :, cols(t)])
        return total

    for t in range(PARTS):
        a_copy(0, t).wait()
        for dx in range(1, nx):
            b_copy(dx, t).wait()
        for d in range(1, nb):
            to_z[d - 1, :, cols(t)] = blk_sum(lax.rem(z + d, nb), t).astype(jnp.bfloat16)
            c_copy(d, t).start()
        out_ref[:, cols(t)] = blk_sum(z, t)

    def mass_end(d, total):
        m_copy(d).wait()
        return total + from_mass[d]

    out_mass[...] = lax.fori_loop(1, n, mass_end, mass_ref[me])

    for t in range(PARTS):
        total = out_ref[:, cols(t)]
        for d in range(1, nb):
            c_copy(d, t).wait()
            total = total + wide(from_z[d - 1, :, cols(t)])
        out_ref[:, cols(t)] = total


def reduce_sums(num, mass, nb, nf):
    own = K // (nb * nf)
    nx = nf // 2
    n = nb * nf
    vmem = pl.BlockSpec(memory_space=pltpu.VMEM)
    dma = pltpu.SemaphoreType.DMA
    return pl.pallas_call(
        functools.partial(reduce_kernel, nb, nf),
        out_shape=(
            jax.ShapeDtypeStruct((own, D), jnp.float32),
            jax.ShapeDtypeStruct((8, own), jnp.float32),
        ),
        in_specs=[vmem] * 2,
        out_specs=(vmem,) * 2,
        scratch_shapes=[
            pltpu.VMEM((nx, nb, own, D), jnp.bfloat16),
            pltpu.VMEM((nx - 1, nb, own, D), jnp.bfloat16),
            pltpu.VMEM((nx - 1, nb, own, D), jnp.bfloat16),
            pltpu.VMEM((nb - 1, own, D), jnp.bfloat16),
            pltpu.VMEM((nb - 1, own, D), jnp.bfloat16),
            pltpu.VMEM((n, 8, own), jnp.float32),
        ]
        + [dma((nx, PARTS))] * 4
        + [dma((nb, PARTS))] * 2
        + [dma((n,))] * 2,
        compiler_params=pltpu.CompilerParams(
            collective_id=1, has_side_effects=True, vmem_limit_bytes=24 * 2**20
        ),
        name="reduce_sums",
    )(num, mass)


def fused_kernel(
    nb, nf, allow_ref, emb_ref, cen_ref, num_ref, norm_ref,
    rows_ref, all_ref, offs_ref, score_ref, top_ref, sum_ref, weight_ref, keep_ref,
    to_sib, from_sib, to_x, from_x, part_ref, to_z, from_z, sides_ref, to_line, from_line,
    swap_out, swap_in, to_mass, from_mass,
    row_send, row_recv, send, recv, own_sem, a_send, a_recv, b_send, b_recv, z_send, z_recv,
    m_send, m_recv, line_send, line_recv, swap_sem,
):
    z = lax.axis_index("blk")
    f = lax.axis_index("feat")
    n = nb * nf
    me = z * nf + f
    c = lax.rem(f, 2)
    x = f // 2
    rows, width = rows_ref.shape[0], emb_ref.shape[1]
    local = rows // RB
    per = K // nb // CB
    half = CB // 2
    own = K // n
    thin = D * 3 // 16
    wide = D - 2 * thin
    sibling = x * 2 + 1 - c
    size = D // CHUNKS
    scale = 1.0 / math.sqrt(D)
    transposed = (((1,), (1,)), ((), ()))

    def at_offset(d):
        other = lax.rem(me + d, n)
        return {"blk": other // nf, "feat": lax.rem(other, nf)}

    barrier = pltpu.get_barrier_semaphore()

    def greet(d, carry):
        pl.semaphore_signal(barrier, inc=1, device_id=at_offset(d), device_id_type=MESH)
        return carry

    lax.fori_loop(1, n, greet, 0)
    pl.semaphore_wait(barrier, n - 1)

    def wide_spot(ref, block, p, cc):
        first = (block * per + p) * CB + cc * half
        return ref.at[pl.ds(pl.multiple_of(first, half), half), pl.ds(0, wide)]

    def thin_spot(ref, block, cc, xx):
        count = per * half
        return ref.at[
            pl.ds(pl.multiple_of((block * 2 + cc) * count, count), count),
            pl.ds(pl.multiple_of(wide + xx * thin, 128), thin),
        ]

    def remote(src, dst, kind, d, blk, feat):
        return pltpu.make_async_remote_copy(
            src_ref=src,
            dst_ref=dst,
            send_sem=send.at[kind, d],
            recv_sem=recv.at[kind, d],
            device_id={"blk": blk, "feat": feat},
            device_id_type=MESH,
        )

    started = []

    def go(cond, copy):
        pl.when(cond)(copy.start)
        started.append((cond, copy))

    piece_rows = rows // PIECES

    def row_copy(d, piece):
        to = lax.rem(f + d, nf)
        return pltpu.make_async_remote_copy(
            src_ref=emb_ref.at[
                pl.ds(pl.multiple_of(to * rows + piece * piece_rows, piece_rows), piece_rows), :
            ],
            dst_ref=rows_ref.at[
                pl.ds(piece * piece_rows, piece_rows),
                pl.ds(pl.multiple_of(f * width, width), width),
            ],
            send_sem=row_send.at[d, piece],
            recv_sem=row_recv.at[d, piece],
            device_id={"blk": z, "feat": to},
            device_id_type=MESH,
        )

    def step(way):
        return jnp.clip(z + 1 - 2 * way, 0, nb - 1)

    def onward(way):
        return (z + 1 < nb) if way == 0 else (z > 0)

    def source(way, hop):
        zz = z - hop if way == 0 else z + hop
        return (zz >= 0) if way == 0 else (zz < nb), jnp.clip(zz, 0, nb - 1)

    def arrived(cond, kind, d, here):
        pl.when(cond)(remote(here, here, kind, d, z, sibling).wait_recv)
        return here

    def pass_thin(way, hop):
        cond, zz = source(way, hop)
        d = (way * nb + hop) * per
        here = arrived(cond, 0, d, thin_spot(all_ref, zz, c, x))
        if hop + 1 < nb:
            go(jnp.logical_and(cond, onward(way)), remote(here, here, 0, d + per, step(way), f))
        go(cond, remote(here, here, 1, d, z, (1 - x) * 2 + c))
        go(cond, remote(here, here, 2, d, z, sibling))

    def pass_wide(way, hop, p):
        cond, zz = source(way, hop)
        d = (way * nb + hop) * per + p
        here = arrived(cond, 4, d, wide_spot(all_ref, zz, p, c))
        if hop + 1 < nb:
            go(jnp.logical_and(cond, onward(way)), remote(here, here, 4, d + per, step(way), f))
        go(cond, remote(here, here, 5, d, z, sibling))

    def pass_across(way, hop):
        cond, zz = source(way, hop)
        d = (way * nb + hop) * per
        here = arrived(cond, 1, d, thin_spot(all_ref, zz, c, 1 - x))
        go(cond, remote(here, here, 3, d, z, sibling))

    def have_thin(way, hop):
        cond, zz = source(way, hop)
        d = (way * nb + hop) * per
        arrived(cond, 2, d, thin_spot(all_ref, zz, 1 - c, x))
        arrived(cond, 3, d, thin_spot(all_ref, zz, 1 - c, 1 - x))

    def have_wide(way, hop, p):
        cond, zz = source(way, hop)
        arrived(cond, 5, (way * nb + hop) * per + p, wide_spot(all_ref, zz, p, 1 - c))

    def both(turn, *where):
        for way in range(2):
            turn(way, *where)

    def panel_turns(hop, first, last, turn):
        def one(t, carry):
            way, p = lax.rem(t, 2), t // 2
            zz = z + (2 * way - 1) * hop
            fits = jnp.logical_and(zz >= 0, zz < nb)
            fits = jnp.logical_and(fits, jnp.logical_or(hop > 0, way == 0))

            @pl.when(fits)
            def _():
                turn(zz * per + p)

            return carry

        lax.fori_loop(first * 2, last * 2, one, 0)

    def scores(hop, first, last, row_blocks):
        span = len(row_blocks) * RB
        low = row_blocks[0]

        def turn(col):
            panel = all_ref[pl.ds(pl.multiple_of(col * CB, CB), CB), :]
            if low == 0:
                wider = panel.astype(jnp.float32)
                offs = 0.5 * jnp.sum(wider * wider, axis=1, keepdims=True)
                if len(row_blocks) < local:
                    offs_ref[col] = offs
            else:
                offs = offs_ref[col]
            raw = lax.dot_general(
                panel,
                rows_ref[low * RB : low * RB + span, :],
                transposed,
                preferred_element_type=jnp.float32,
            )
            for r in row_blocks:
                part = raw[:, (r - low) * RB : (r - low + 1) * RB]
                value = jnp.where(
                    allow_ref[r, col] > 0, (part - offs) * scale, neg_big
                )
                score_ref[r, col] = value
                old = top_ref[r]
                top = jnp.maximum(old, jnp.max(value, axis=0, keepdims=True))
                sum_ref[r] = sum_ref[r] * jnp.exp(old - top) + jnp.sum(
                    jnp.exp(value - top), axis=0, keepdims=True
                )
                top_ref[r] = top

        panel_turns(hop, first, last, turn)

    first_pieces = PIECES // local
    for way in range(2):
        d = (way * nb + 1) * per
        mine = thin_spot(cen_ref, 0, c, x)
        go(onward(way), remote(mine, thin_spot(all_ref, z, c, x), 0, d, step(way), f))
    for p in range(per):
        for way in range(2):
            d = (way * nb + 1) * per + p
            mine = wide_spot(cen_ref, 0, p, c)
            go(onward(way), remote(mine, wide_spot(all_ref, z, p, c), 4, d, step(way), f))
    row_copies = [[row_copy(d, piece) for d in range(1, nf)] for piece in range(PIECES)]
    for piece in range(first_pieces):
        for copy in row_copies[piece]:
            copy.start()
    loads = [
        pltpu.make_async_copy(
            emb_ref.at[pl.ds(pl.multiple_of(f * rows, rows), rows), :],
            rows_ref.at[:, pl.ds(pl.multiple_of(f * width, width), width)],
            own_sem.at[0],
        ),
        pltpu.make_async_copy(
            cen_ref, all_ref.at[pl.ds(pl.multiple_of(z * per * CB, CB), per * CB), :], own_sem.at[1]
        ),
    ]
    for copy in loads:
        copy.start()
    top_ref[...] = jnp.full_like(top_ref, neg_big)
    sum_ref[...] = jnp.zeros_like(sum_ref)
    early = list(range(1))
    late = list(range(1, local))
    both(pass_thin, 1)
    for piece in range(first_pieces, PIECES):
        for copy in row_copies[piece]:
            copy.start()
    for copy in loads:
        copy.wait()
    for p in range(per):
        both(pass_wide, 1, p)
    both(pass_thin, 2)
    for piece in range(first_pieces):
        for copy in row_copies[piece]:
            copy.wait_recv()
    scores(0, 0, per, early)
    both(pass_across, 1)
    both(have_thin, 1)
    for p in range(per):
        both(have_wide, 1, p)
    scores(1, 0, per, early)
    for p in range(per):
        both(pass_wide, 2, p)
    for hop in range(3, nb):
        both(pass_thin, hop)
        for p in range(per):
            if hop < nb - 1 or p < per - 1:
                both(pass_wide, hop, p)
    for piece in range(first_pieces, PIECES):
        for copy in row_copies[piece]:
            copy.wait_recv()
    scores(0, 0, per, late)
    scores(1, 0, per, late)
    for hop in range(2, nb):
        both(pass_across, hop)
        both(have_thin, hop)
        for p in range(per):
            both(have_wide, hop, p)
            scores(hop, p, p + 1, early + late)
            if hop == nb - 2 and p == per - 2:
                both(pass_wide, nb - 1, per - 1)

    for r in range(local):
        norm = top_ref[r] + jnp.log(sum_ref[r])
        for j in range(RB // 128):
            norm_ref[r * (RB // 128) + j, :] = norm[0, j * 128 : (j + 1) * 128]
        top_ref[r] = norm

    lead = 0

    def cols(t):
        return pl.ds(pl.multiple_of(t * size, size), size)

    left, right = jnp.int32(0), jnp.int32(nb - 1)
    turns = []
    for _ in range(nb):
        pick = (z - left) >= (right - z)
        turns.append(jnp.where(pick, left, right))
        left, right = jnp.where(pick, left + 1, left), jnp.where(pick, right, right - 1)

    def a_copy(q, t):
        return pltpu.make_async_remote_copy(
            src_ref=to_sib.at[q, :, cols(t)],
            dst_ref=from_sib.at[q, :, cols(t)],
            send_sem=a_send.at[q, t],
            recv_sem=a_recv.at[q, t],
            device_id={"blk": z, "feat": sibling},
            device_id_type=MESH,
        )

    def b_copy(i, t):
        return pltpu.make_async_remote_copy(
            src_ref=to_x.at[i, :, cols(t)],
            dst_ref=from_x.at[i, :, cols(t)],
            send_sem=b_send.at[i, t],
            recv_sem=b_recv.at[i, t],
            device_id={"blk": z, "feat": (1 - x) * 2 + c},
            device_id_type=MESH,
        )

    def z_copy(zz, way, t):
        return pltpu.make_async_remote_copy(
            src_ref=to_z.at[zz, :, cols(t)],
            dst_ref=from_z.at[way, zz, :, cols(t)],
            send_sem=z_send.at[zz, t],
            recv_sem=z_recv.at[way, zz, t],
            device_id={"blk": jnp.clip(z + 1 - 2 * way, 0, nb - 1), "feat": f},
            device_id_type=MESH,
        )

    def line_copy(d):
        zz = lax.rem(z + d, nb)
        return pltpu.make_async_remote_copy(
            src_ref=to_line.at[zz],
            dst_ref=from_line.at[d - 1],
            send_sem=line_send.at[d],
            recv_sem=line_recv.at[d],
            device_id={"blk": zz, "feat": f},
            device_id_type=MESH,
        )

    def swap_copy():
        return pltpu.make_async_remote_copy(
            src_ref=swap_out,
            dst_ref=swap_in,
            send_sem=swap_sem.at[0],
            recv_sem=swap_sem.at[1],
            device_id={"blk": z, "feat": (1 - x) * 2 + c},
            device_id_type=MESH,
        )

    def m_copy(d):
        return pltpu.make_async_remote_copy(
            src_ref=to_mass.at[lax.rem(me + d, n)],
            dst_ref=from_mass.at[d],
            send_sem=m_send.at[d],
            recv_sem=m_recv.at[d],
            device_id=at_offset(d),
            device_id_type=MESH,
        )

    def wide_of(value):
        return value.astype(jnp.float32)

    def place(i):
        zz = turns[nb - 1]
        for t in range(nb - 1):
            zz = jnp.where(i == t, turns[t], zz)
        return zz

    group = CHUNKS // SPANS

    def weights(i, side):
        zz = place(i)
        xx = 1 - x if side == 0 else x
        col = zz * per + xx
        part = slice(side * CB, (side + 1) * CB)
        for cc in range(2):
            at = c if cc == 0 else 1 - c
            first = side * CB + cc * own
            for r in range(local):
                value = score_ref[r, col, pl.ds(pl.multiple_of(at * own, own), own), :]
                weight_ref[first : first + own, r * RB : (r + 1) * RB] = jnp.exp(
                    value - top_ref[r]
                ).astype(jnp.bfloat16)
        mass = lax.dot_general(
            jnp.ones((8, rows), jnp.bfloat16),
            weight_ref[part, :],
            transposed,
            preferred_element_type=jnp.float32,
        )
        to_mass[zz * nf + xx * 2 + c] = mass[:, :own]
        to_mass[zz * nf + xx * 2 + 1 - c] = mass[:, own:]

    def sums(i):
        for side in range(2):
            weights(i, side)

        def span(u, carry):
            @pl.when(u < SPANS)
            def _():
                at = pl.ds(pl.multiple_of(u * group * size, group * size), group * size)
                total = jnp.dot(
                    weight_ref[...], rows_ref[:, at], preferred_element_type=jnp.float32
                )
                for side in range(2):
                    first = side * CB
                    keep_ref[side * nb + i, :, at] = total[first : first + own]
                    to_sib[side * nb + i, :, at] = total[first + own : first + CB].astype(jnp.bfloat16)
                for side in range(2):
                    for t in range(group):
                        a_copy(side * nb + i, u * group + t).start()

            @pl.when(u == 1)
            def _():
                send_line(i)

            @pl.when(u > 0)
            def _():
                for t in range(group):
                    at = (u - 1) * group + t
                    pl.when(at > lead)(functools.partial(send_x, i, at))

            return carry

        lax.fori_loop(0, SPANS + 1, span, 0)

    def send_x(i, t):
        a_copy(i, t).wait()
        to_x[i, :, cols(t)] = (
            keep_ref[i, :, cols(t)] + wide_of(from_sib[i, :, cols(t)])
        ).astype(jnp.bfloat16)
        b_copy(i, t).start()

    def course(i):
        zz = place(i)
        fed = jnp.logical_or(
            jnp.logical_and(zz > z, z > 0), jnp.logical_and(zz < z, z < nb - 1)
        )
        return zz, (zz < z).astype(jnp.int32), fed

    def send_line(i):
        zz = place(i)
        for side in range(2):
            q = side * nb + i
            a_copy(q, lead).wait()
            sides_ref[side] = keep_ref[q, :, cols(lead)] + wide_of(from_sib[q, :, cols(lead)])

        @pl.when(zz != z)
        def _():
            to_line[zz] = sides_ref[...].astype(jnp.bfloat16)
            line_copy(lax.rem(zz - z + nb, nb)).start()

    def swap():
        def one(d, carry):
            line_copy(d).wait()
            sides_ref[...] += wide_of(from_line[d - 1])
            return carry

        lax.fori_loop(1, nb, one, 0)
        swap_out[...] = sides_ref[0].astype(jnp.bfloat16)
        swap_copy().start()
        num_ref[:, cols(lead)] = sides_ref[1]

    def send_z(i):
        zz, way, fed = course(i)
        q = nb + i

        def chunk(t, carry):
            a_copy(q, t).wait()
            b_copy(i, t).wait()
            part_ref[...] = (
                keep_ref[q, :, cols(t)]
                + wide_of(from_sib[q, :, cols(t)])
                + wide_of(from_x[i, :, cols(t)])
            )

            @pl.when(fed)
            def _():
                z_copy(zz, way, t).wait_recv()
                part_ref[...] += wide_of(from_z[way, zz, :, cols(t)])

            @pl.when(zz != z)
            def _():
                to_z[zz, :, cols(t)] = part_ref[...].astype(jnp.bfloat16)
                z_copy(zz, way, t).start()

            @pl.when(zz == z)
            def _():
                num_ref[:, cols(t)] = part_ref[...]

            return carry

        lax.fori_loop(lead + 1, CHUNKS, chunk, 0)

    def turn(i, carry):
        @pl.when(i < nb)
        def _():
            sums(i)

        @pl.when(i == nb - 1)
        def _():
            def mass_start(d, carry):
                m_copy(d).start()
                return carry

            lax.fori_loop(1, n, mass_start, 0)

        pl.when(i == nb)(swap)

        @pl.when(i > 0)
        def _():
            send_z(i - 1)

        return carry

    lax.fori_loop(0, nb + 1, turn, 0)

    def mass_end(d, total):
        m_copy(d).wait()
        return total + from_mass[d]

    mass = lax.fori_loop(1, n, mass_end, to_mass[me])[:1]
    spread = jnp.broadcast_to(mass, (own, own))
    diagonal = lax.broadcasted_iota(jnp.int32, (own, own), 0) == lax.broadcasted_iota(
        jnp.int32, (own, own), 1
    )
    inverse = 1.0 / (
        jnp.sum(jnp.where(diagonal, spread, 0.0), axis=1, keepdims=True) + prior_mass
    )

    def finish(t):
        old = all_ref[pl.ds(pl.multiple_of(me * own, own), own), cols(t)]
        num_ref[:, cols(t)] = (num_ref[:, cols(t)] + prior_mass * wide_of(old)) * inverse

    def last(t, carry):
        for way in range(2):

            @pl.when((z > 0) if way == 0 else (z < nb - 1))
            def _():
                z_copy(z, way, t).wait_recv()
                num_ref[:, cols(t)] += wide_of(from_z[way, z, :, cols(t)])

        for zz in range(nb):

            @pl.when(z != zz)
            def _():
                z_copy(zz, 0, t).wait_send()

        finish(t)
        return carry

    lax.fori_loop(lead + 1, CHUNKS, last, 0)
    swap_copy().wait()
    num_ref[:, cols(lead)] += wide_of(swap_in[...])
    finish(lead)
    for group in row_copies:
        for copy in group:
            copy.wait_send()
    for cond, copy in started:
        pl.when(cond)(copy.wait_send)


def fused(allow, embeddings, centroids, nb, nf):
    rows = embeddings.shape[0] // nf
    local = rows // RB
    n = nb * nf
    own = K // n
    per = K // nb // CB
    kinds = 6
    vmem = pl.BlockSpec(memory_space=pltpu.VMEM)
    hbm = pl.BlockSpec(memory_space=pltpu.HBM)
    dma = pltpu.SemaphoreType.DMA
    bf16, f32 = jnp.bfloat16, jnp.float32
    return pl.pallas_call(
        functools.partial(fused_kernel, nb, nf),
        out_shape=(
            jax.ShapeDtypeStruct((own, D), f32),
            jax.ShapeDtypeStruct((rows // 128, 128), f32),
        ),
        in_specs=[pl.BlockSpec(memory_space=pltpu.SMEM), hbm, hbm],
        out_specs=(vmem,) * 2,
        scratch_shapes=[
            pltpu.VMEM((rows, D), bf16),
            pltpu.VMEM((K, D), bf16),
            pltpu.VMEM((NCB, CB, 1), f32),
            pltpu.VMEM((local, NCB, CB, RB), f32),
            pltpu.VMEM((local, 1, RB), f32),
            pltpu.VMEM((local, 1, RB), f32),
            pltpu.VMEM((2 * CB, rows), bf16),
            pltpu.VMEM((2 * nb, own, D), f32),
            pltpu.VMEM((2 * nb, own, D), bf16),
            pltpu.VMEM((2 * nb, own, D), bf16),
            pltpu.VMEM((nb, own, D), bf16),
            pltpu.VMEM((nb, own, D), bf16),
            pltpu.VMEM((own, D // CHUNKS), f32),
            pltpu.VMEM((nb, own, D), bf16),
            pltpu.VMEM((2, nb, own, D), bf16),
            pltpu.VMEM((2, own, D // CHUNKS), f32),
            pltpu.VMEM((nb, 2, own, D // CHUNKS), bf16),
            pltpu.VMEM((nb - 1, 2, own, D // CHUNKS), bf16),
            pltpu.VMEM((own, D // CHUNKS), bf16),
            pltpu.VMEM((own, D // CHUNKS), bf16),
            pltpu.VMEM((n, 8, own), f32),
            pltpu.VMEM((n, 8, own), f32),
            dma((nf, PIECES)),
            dma((nf, PIECES)),
            dma((kinds, 2 * nb * per)),
            dma((kinds, 2 * nb * per)),
            dma((2,)),
            dma((2 * nb, CHUNKS)),
            dma((2 * nb, CHUNKS)),
            dma((nb, CHUNKS)),
            dma((nb, CHUNKS)),
            dma((nb, CHUNKS)),
            dma((2, nb, CHUNKS)),
            dma((n,)),
            dma((n,)),
            dma((nb,)),
            dma((nb,)),
            dma((2,)),
        ],
        compiler_params=pltpu.CompilerParams(
            collective_id=2, has_side_effects=True, vmem_limit_bytes=58 * 2**20
        ),
        name="fused",
    )(allow, embeddings, centroids)


def body(embeddings, centroids, pair_list):
    nb, nf = lax.axis_size("blk"), lax.axis_size("feat")
    local_rows = embeddings.shape[0] // nf
    local_blocks = local_rows // RB
    device_index = lax.axis_index("blk") * nf + lax.axis_index("feat")
    mine = device_index * local_blocks + jnp.arange(local_blocks, dtype=jnp.int32)
    row_ids, col_ids = pair_list[:, 0], pair_list[:, 1]
    same = row_ids[None, :] == mine[:, None]
    if K // nb == 2 * CB and nf == 4 and local_blocks == 2:
        blocks = jnp.arange(NCB, dtype=jnp.int32)
        listed = same[:, None, :] & (col_ids[None, None, :] == blocks[None, :, None])
        allow = jnp.sum(listed.astype(jnp.int32), axis=2)
        new_centroids, log_norm = fused(allow, embeddings, centroids, nb, nf)
        return (new_centroids, log_norm.reshape(local_rows))
    before = jnp.sum((row_ids[None, :] < mine[:, None]).astype(jnp.int32), axis=1)
    counts = jnp.sum(same.astype(jnp.int32), axis=1)
    rank = jnp.arange(row_ids.shape[0], dtype=jnp.int32)[None, :] - before[:, None]
    slots = jnp.arange(SLOTS, dtype=jnp.int32)
    picked = same[:, None, :] & (rank[:, None, :] == slots[None, :, None])
    chosen = jnp.sum(jnp.where(picked, col_ids[None, None, :], 0), axis=2)
    table = jnp.concatenate([counts[:, None], chosen], axis=1)

    row_data, panels = fetch(embeddings, centroids, nb, nf)
    num, mass, log_norm = terms(table, row_data, panels, nb, nf)
    numerator, denominator = reduce_sums(num, mass, nb, nf)

    own_count = centroids.shape[0] // nf
    own_rows = lax.dynamic_slice_in_dim(
        centroids, lax.axis_index("feat") * own_count, own_count, 0
    ).astype(jnp.float32)
    new_centroids = (numerator + prior_mass * own_rows) / (denominator[0][:, None] + prior_mass)
    return (new_centroids, log_norm.reshape(local_rows))


def solution(mesh):
    return jax.shard_map(
        body,
        mesh=mesh,
        in_specs=(P(("groups", "blk"), "feat"), P(("groups", "blk"), None), P("groups", None)),
        out_specs=(P(("groups", "blk", "feat"), None), P(("groups", "blk", "feat"))),
        check_vma=False,
    )
```

```python
import functools
import math

import jax
import jax.numpy as jnp
from jax import lax
from jax.experimental import pallas as pl
from jax.experimental.pallas import tpu as pltpu
from jax.sharding import PartitionSpec as P

D = 2048
K = 2048
RB = 512
CB = 256
NCB = K // CB
SLOTS = 4
PARTS = 8
PIECES = 8
CHUNKS = 8
SPANS = 4

neg_big = -1e30
prior_mass = 16.0
MESH = pl.DeviceIdType.MESH


def meet(peers):
    barrier = pltpu.get_barrier_semaphore()
    for peer in peers:
        pl.semaphore_signal(barrier, inc=1, device_id=peer, device_id_type=MESH)
    pl.semaphore_wait(barrier, len(peers))


def fetch_kernel(
    nb, nf, emb_ref, cen_ref, rows_ref, all_ref, row_send, row_recv, send, recv, own_sem,
    emb_hold, cen_hold,
):
    z = lax.axis_index("blk")
    f = lax.axis_index("feat")
    nx = nf // 2
    c = lax.rem(f, 2)
    x = f // 2
    rows, width = rows_ref.shape[0], emb_ref.shape[1]
    half = cen_ref.shape[0] // 2
    thin = D * 3 // 8 // nx // 128 * 128
    wide = D - nx * thin
    sibling = x * 2 + 1 - c

    def across(dx):
        return lax.rem(x + dx, nx)

    meet(
        [{"blk": z, "feat": lax.rem(f + d, nf)} for d in range(1, nf)]
        + [{"blk": lax.rem(z + d, nb), "feat": f} for d in range(1, nb)]
    )

    def spot(zz, cc, col, size):
        return all_ref.at[
            pl.ds(pl.multiple_of(zz * 2 * half + cc * half, half), half),
            pl.ds(pl.multiple_of(col, 128), size),
        ]

    def remote(src, dst, kind, d, blk, feat):
        return pltpu.make_async_remote_copy(
            src_ref=src,
            dst_ref=dst,
            send_sem=send.at[kind, d],
            recv_sem=recv.at[kind, d],
            device_id={"blk": blk, "feat": feat},
            device_id_type=MESH,
        )

    def own_part(col, size):
        return cen_ref.at[
            pl.ds(pl.multiple_of(c * half, half), half), pl.ds(pl.multiple_of(col, 128), size)
        ]

    thin_col = wide + x * thin
    started = []

    def go(cond, copy):
        pl.when(cond)(copy.start)
        started.append((cond, copy))

    def row_copy(d, piece):
        to = lax.rem(f + d, nf)
        size = rows // PIECES
        return pltpu.make_async_remote_copy(
            src_ref=emb_ref.at[pl.ds(pl.multiple_of(to * rows + piece * size, size), size), :],
            dst_ref=rows_ref.at[
                pl.ds(piece * size, size), pl.ds(pl.multiple_of(f * width, width), width)
            ],
            send_sem=row_send.at[d, piece],
            recv_sem=row_recv.at[d, piece],
            device_id={"blk": z, "feat": to},
            device_id_type=MESH,
        )

    def step(way):
        return jnp.clip(z + 1 - 2 * way, 0, nb - 1)

    def onward(way):
        return (z + 1 < nb) if way == 0 else (z > 0)

    for way in range(2):
        go(
            onward(way),
            remote(own_part(thin_col, thin), spot(z, c, thin_col, thin), 1, way * nb + 1, step(way), f),
        )
    for way in range(2):
        go(onward(way), remote(own_part(0, wide), spot(z, c, 0, wide), 0, way * nb + 1, step(way), f))
    row_copies = [row_copy(d, piece) for piece in range(PIECES) for d in range(1, nf)]
    for copy in row_copies:
        copy.start()
    holds = [
        (
            emb_ref.at[pl.ds(pl.multiple_of(f * rows, rows), rows), :],
            emb_hold,
            rows_ref.at[:, pl.ds(pl.multiple_of(f * width, width), width)],
        ),
        (
            cen_ref,
            cen_hold,
            all_ref.at[pl.ds(pl.multiple_of(z * 2 * half, half), 2 * half), :],
        ),
    ]
    loads = [pltpu.make_async_copy(src, hold, own_sem.at[i]) for i, (src, hold, _) in enumerate(holds)]
    stores = [
        pltpu.make_async_copy(hold, dst, own_sem.at[2 + i]) for i, (_, hold, dst) in enumerate(holds)
    ]
    for copy in loads:
        copy.start()
    for load, store in zip(loads, stores):
        load.wait()
        store.start()

    def source(way, hop):
        zz = z - hop if way == 0 else z + hop
        return (zz >= 0) if way == 0 else (zz < nb), jnp.clip(zz, 0, nb - 1)

    def arrived(cond, kind, d, zz, cc, col, size):
        here = spot(zz, cc, col, size)
        pl.when(cond)(remote(here, here, kind, d, z, sibling).wait_recv)
        return here

    turns = [(way, hop) for hop in range(1, nb) for way in range(2)]

    def pass_thin(way, hop):
        cond, zz = source(way, hop)
        d = way * nb + hop
        here = arrived(cond, 1, d, zz, c, thin_col, thin)
        if hop + 1 < nb:
            go(jnp.logical_and(cond, onward(way)), remote(here, here, 1, d + 1, step(way), f))
        for dx in range(1, nx):
            go(cond, remote(here, here, 4 + dx, d, z, across(dx) * 2 + c))
        go(cond, remote(here, here, 3, d, z, sibling))

    def pass_wide(way, hop):
        cond, zz = source(way, hop)
        d = way * nb + hop
        here = arrived(cond, 0, d, zz, c, 0, wide)
        if hop + 1 < nb:
            go(jnp.logical_and(cond, onward(way)), remote(here, here, 0, d + 1, step(way), f))
        go(cond, remote(here, here, 2, d, z, sibling))

    def pass_across(way, hop):
        cond, zz = source(way, hop)
        d = way * nb + hop
        for dx in range(1, nx):
            col = wide + lax.rem(x + nx - dx, nx) * thin
            here = arrived(cond, 4 + dx, d, zz, c, col, thin)
            go(cond, remote(here, here, 4 + nx + dx, d, z, sibling))

    for hop in range(1, nb):
        for way in range(2):
            pass_thin(way, hop)
        for way in range(2):
            pass_wide(way, hop)
    for way, hop in turns:
        pass_across(way, hop)
    for way, hop in turns:
        cond, zz = source(way, hop)
        d = way * nb + hop
        arrived(cond, 2, d, zz, 1 - c, 0, wide)
        arrived(cond, 3, d, zz, 1 - c, thin_col, thin)
        for dx in range(1, nx):
            col = wide + lax.rem(x + nx - dx, nx) * thin
            arrived(cond, 4 + nx + dx, d, zz, 1 - c, col, thin)
    for copy in stores:
        copy.wait()
    for copy in row_copies:
        copy.wait()
    for cond, copy in started:
        pl.when(cond)(copy.wait_send)


def fetch(embeddings, centroids, nb, nf):
    rows = embeddings.shape[0] // nf
    kinds = 4 + 2 * (nf // 2) + 1
    return pl.pallas_call(
        functools.partial(fetch_kernel, nb, nf),
        out_shape=(
            jax.ShapeDtypeStruct((rows, D), jnp.bfloat16),
            jax.ShapeDtypeStruct((K, D), jnp.bfloat16),
        ),
        in_specs=[pl.BlockSpec(memory_space=pltpu.HBM)] * 2,
        out_specs=(pl.BlockSpec(memory_space=pl.ANY),) * 2,
        scratch_shapes=[
            pltpu.SemaphoreType.DMA((nf, PIECES)),
            pltpu.SemaphoreType.DMA((nf, PIECES)),
            pltpu.SemaphoreType.DMA((kinds, 2 * nb)),
            pltpu.SemaphoreType.DMA((kinds, 2 * nb)),
            pltpu.SemaphoreType.DMA((4,)),
            pltpu.VMEM((rows, D // nf), jnp.bfloat16),
            pltpu.VMEM((K // nb, D), jnp.bfloat16),
        ],
        compiler_params=pltpu.CompilerParams(
            collective_id=0, has_side_effects=True, vmem_limit_bytes=6 * 2**20
        ),
        name="fetch",
    )(embeddings, centroids)


def term_kernel(nb, nf, tab_ref, rows_ref, all_ref, num_ref, mass_ref, norm_ref, score_ref, weight_ref, acc_ref, row_mass):
    local = rows_ref.shape[0] // RB
    scale = 1.0 / math.sqrt(D)
    own = K // (nb * nf)
    nx = nf // 2
    transposed = (((1,), (1,)), ((), ()))

    for r in range(local):
        part = rows_ref[r * RB : (r + 1) * RB, :]
        count = tab_ref[r, 0]

        def score_turn(slot, top):
            col = tab_ref[r, 1 + slot]
            panel = all_ref[pl.ds(pl.multiple_of(col * CB, CB), CB), :]
            wide = panel.astype(jnp.float32)
            offs = 0.5 * jnp.sum(wide * wide, axis=1, keepdims=True)
            raw = lax.dot_general(panel, part, transposed, preferred_element_type=jnp.float32)
            scores = (raw - offs) * scale
            score_ref[slot] = scores
            return jnp.maximum(top, jnp.max(scores, axis=0, keepdims=True))

        top = lax.fori_loop(0, count, score_turn, jnp.full((1, RB), neg_big, jnp.float32))

        def sum_turn(slot, total):
            return total + jnp.sum(jnp.exp(score_ref[slot] - top), axis=0, keepdims=True)

        total = lax.fori_loop(0, count, sum_turn, jnp.zeros((1, RB), jnp.float32))
        norm = top + jnp.log(total)
        norm_ref[r] = norm

        def weight_turn(slot, carry):
            col = tab_ref[r, 1 + slot]
            weight_ref[r, col] = jnp.exp(score_ref[slot] - norm).astype(jnp.bfloat16)
            return carry

        lax.fori_loop(0, count, weight_turn, 0)

    def col_turn(col, carry):
        acc_ref[...] = jnp.zeros_like(acc_ref)
        row_mass[...] = jnp.zeros_like(row_mass)
        for r in range(local):
            hit = jnp.int32(0)
            for slot in range(SLOTS):
                found = jnp.logical_and(tab_ref[r, 1 + slot] == col, slot < tab_ref[r, 0])
                hit = hit + found.astype(jnp.int32)

            @pl.when(hit > 0)
            def _():
                weights = weight_ref[r, col]
                acc_ref[...] += jnp.dot(
                    weights, rows_ref[r * RB : (r + 1) * RB, :], preferred_element_type=jnp.float32
                )
                row_mass[...] += lax.dot_general(
                    jnp.ones((8, RB), jnp.bfloat16),
                    weights,
                    transposed,
                    preferred_element_type=jnp.float32,
                )

        for j in range(CB // own):
            owner = col * (CB // own) + j
            zz, ff = owner // nf, lax.rem(owner, nf)
            num_ref[lax.rem(ff, 2), ff // 2, zz] = acc_ref[j * own : (j + 1) * own, :].astype(
                jnp.bfloat16
            )
            mass_ref[owner] = row_mass[:, j * own : (j + 1) * own]
        return carry

    lax.fori_loop(0, NCB, col_turn, 0)


def terms(table, row_data, panels, nb, nf):
    local = row_data.shape[0] // RB
    own = K // (nb * nf)
    vmem = pl.BlockSpec(memory_space=pltpu.VMEM)
    return pl.pallas_call(
        functools.partial(term_kernel, nb, nf),
        out_shape=(
            jax.ShapeDtypeStruct((2, nf // 2, nb, own, D), jnp.bfloat16),
            jax.ShapeDtypeStruct((nb * nf, 8, own), jnp.float32),
            jax.ShapeDtypeStruct((local, 1, RB), jnp.float32),
        ),
        in_specs=[pl.BlockSpec(memory_space=pltpu.SMEM), vmem, vmem],
        out_specs=(vmem,) * 3,
        scratch_shapes=[
            pltpu.VMEM((SLOTS, CB, RB), jnp.float32),
            pltpu.VMEM((local, NCB, CB, RB), jnp.bfloat16),
            pltpu.VMEM((CB, D), jnp.float32),
            pltpu.VMEM((8, CB), jnp.float32),
        ],
        compiler_params=pltpu.CompilerParams(vmem_limit_bytes=32 * 2**20),
        name="terms",
    )(table, row_data, panels)


def reduce_kernel(
    nb, nf, num_ref, mass_ref, out_ref, out_mass,
    from_sib, to_x, from_x, to_z, from_z, from_mass,
    a_send, a_recv, b_send, b_recv, c_send, c_recv, m_send, m_recv,
):
    z = lax.axis_index("blk")
    f = lax.axis_index("feat")
    nx = nf // 2
    n = nb * nf
    me = z * nf + f
    c = lax.rem(f, 2)
    x = f // 2
    sibling = x * 2 + 1 - c
    size = D // PARTS

    def at_offset(d):
        other = lax.rem(me + d, n)
        return {"blk": other // nf, "feat": lax.rem(other, nf)}

    barrier = pltpu.get_barrier_semaphore()

    def greet(d, carry):
        pl.semaphore_signal(barrier, inc=1, device_id=at_offset(d), device_id_type=MESH)
        return carry

    lax.fori_loop(1, n, greet, 0)
    pl.semaphore_wait(barrier, n - 1)

    def cols(t):
        return pl.ds(t * size, size)

    def a_copy(dx, t):
        xx = lax.rem(x + dx, nx)
        return pltpu.make_async_remote_copy(
            src_ref=num_ref.at[1 - c, xx, :, :, cols(t)],
            dst_ref=from_sib.at[xx, :, :, cols(t)],
            send_sem=a_send.at[dx, t],
            recv_sem=a_recv.at[dx, t],
            device_id={"blk": z, "feat": sibling},
            device_id_type=MESH,
        )

    def b_copy(dx, t):
        return pltpu.make_async_remote_copy(
            src_ref=to_x.at[dx - 1, :, :, cols(t)],
            dst_ref=from_x.at[dx - 1, :, :, cols(t)],
            send_sem=b_send.at[dx, t],
            recv_sem=b_recv.at[dx, t],
            device_id={"blk": z, "feat": lax.rem(x + dx, nx) * 2 + c},
            device_id_type=MESH,
        )

    def c_copy(d, t):
        return pltpu.make_async_remote_copy(
            src_ref=to_z.at[d - 1, :, cols(t)],
            dst_ref=from_z.at[d - 1, :, cols(t)],
            send_sem=c_send.at[d, t],
            recv_sem=c_recv.at[d, t],
            device_id={"blk": lax.rem(z + d, nb), "feat": f},
            device_id_type=MESH,
        )

    def m_copy(d):
        return pltpu.make_async_remote_copy(
            src_ref=mass_ref.at[lax.rem(me + d, n)],
            dst_ref=from_mass.at[d],
            send_sem=m_send.at[d],
            recv_sem=m_recv.at[d],
            device_id=at_offset(d),
            device_id_type=MESH,
        )

    def wide(value):
        return value.astype(jnp.float32)

    for t in range(PARTS):
        for dx in range(1, nx):
            a_copy(dx, t).start()
    for t in range(PARTS):
        a_copy(0, t).start()

    def mass_start(d, carry):
        m_copy(d).start()
        return carry

    lax.fori_loop(1, n, mass_start, 0)

    for t in range(PARTS):
        for dx in range(1, nx):
            xx = lax.rem(x + dx, nx)
            a_copy(dx, t).wait()
            for zz in range(nb):
                to_x[dx - 1, zz, :, cols(t)] = (
                    wide(num_ref[c, xx, zz, :, cols(t)]) + wide(from_sib[xx, zz, :, cols(t)])
                ).astype(jnp.bfloat16)
            b_copy(dx, t).start()

    def blk_sum(zz, t):
        total = wide(num_ref[c, x, zz, :, cols(t)]) + wide(from_sib[x, zz, :, cols(t)])
        for dx in range(1, nx):
            total = total + wide(from_x[dx - 1, zz, :, cols(t)])
        return total

    for t in range(PARTS):
        a_copy(0, t).wait()
        for dx in range(1, nx):
            b_copy(dx, t).wait()
        for d in range(1, nb):
            to_z[d - 1, :, cols(t)] = blk_sum(lax.rem(z + d, nb), t).astype(jnp.bfloat16)
            c_copy(d, t).start()
        out_ref[:, cols(t)] = blk_sum(z, t)

    def mass_end(d, total):
        m_copy(d).wait()
        return total + from_mass[d]

    out_mass[...] = lax.fori_loop(1, n, mass_end, mass_ref[me])

    for t in range(PARTS):
        total = out_ref[:, cols(t)]
        for d in range(1, nb):
            c_copy(d, t).wait()
            total = total + wide(from_z[d - 1, :, cols(t)])
        out_ref[:, cols(t)] = total


def reduce_sums(num, mass, nb, nf):
    own = K // (nb * nf)
    nx = nf // 2
    n = nb * nf
    vmem = pl.BlockSpec(memory_space=pltpu.VMEM)
    dma = pltpu.SemaphoreType.DMA
    return pl.pallas_call(
        functools.partial(reduce_kernel, nb, nf),
        out_shape=(
            jax.ShapeDtypeStruct((own, D), jnp.float32),
            jax.ShapeDtypeStruct((8, own), jnp.float32),
        ),
        in_specs=[vmem] * 2,
        out_specs=(vmem,) * 2,
        scratch_shapes=[
            pltpu.VMEM((nx, nb, own, D), jnp.bfloat16),
            pltpu.VMEM((nx - 1, nb, own, D), jnp.bfloat16),
            pltpu.VMEM((nx - 1, nb, own, D), jnp.bfloat16),
            pltpu.VMEM((nb - 1, own, D), jnp.bfloat16),
            pltpu.VMEM((nb - 1, own, D), jnp.bfloat16),
            pltpu.VMEM((n, 8, own), jnp.float32),
        ]
        + [dma((nx, PARTS))] * 4
        + [dma((nb, PARTS))] * 2
        + [dma((n,))] * 2,
        compiler_params=pltpu.CompilerParams(
            collective_id=1, has_side_effects=True, vmem_limit_bytes=24 * 2**20
        ),
        name="reduce_sums",
    )(num, mass)


def fused_kernel(
    nb, nf, allow_ref, emb_ref, cen_ref, num_ref, norm_ref,
    rows_ref, all_ref, offs_ref, score_ref, top_ref, sum_ref, weight_ref, keep_ref,
    to_sib, from_sib, to_x, from_x, part_ref, to_z, from_z, sides_ref, to_line, from_line,
    swap_out, swap_in, to_mass, from_mass, inverse_ref,
    row_send, row_recv, send, recv, own_sem, a_send, a_recv, b_send, b_recv, z_send, z_recv,
    m_send, m_recv, line_send, line_recv, swap_sem,
):
    z = lax.axis_index("blk")
    f = lax.axis_index("feat")
    n = nb * nf
    me = z * nf + f
    c = lax.rem(f, 2)
    x = f // 2
    rows, width = rows_ref.shape[0], emb_ref.shape[1]
    local = rows // RB
    per = K // nb // CB
    half = CB // 2
    own = K // n
    thin = D * 3 // 16
    wide = D - 2 * thin
    sibling = x * 2 + 1 - c
    size = D // CHUNKS
    scale = 1.0 / math.sqrt(D)
    transposed = (((1,), (1,)), ((), ()))

    def at_offset(d):
        other = lax.rem(me + d, n)
        return {"blk": other // nf, "feat": lax.rem(other, nf)}

    barrier = pltpu.get_barrier_semaphore()

    def greet(d, carry):
        pl.semaphore_signal(barrier, inc=1, device_id=at_offset(d), device_id_type=MESH)
        return carry

    lax.fori_loop(1, n, greet, 0)
    pl.semaphore_wait(barrier, n - 1)

    def wide_spot(ref, block, p, cc):
        first = (block * per + p) * CB + cc * half
        return ref.at[pl.ds(pl.multiple_of(first, half), half), pl.ds(0, wide)]

    def thin_spot(ref, block, cc, xx):
        count = per * half
        return ref.at[
            pl.ds(pl.multiple_of((block * 2 + cc) * count, count), count),
            pl.ds(pl.multiple_of(wide + xx * thin, 128), thin),
        ]

    def remote(src, dst, kind, d, blk, feat):
        return pltpu.make_async_remote_copy(
            src_ref=src,
            dst_ref=dst,
            send_sem=send.at[kind, d],
            recv_sem=recv.at[kind, d],
            device_id={"blk": blk, "feat": feat},
            device_id_type=MESH,
        )

    started = []

    def go(cond, copy):
        pl.when(cond)(copy.start)
        started.append((cond, copy))

    piece_rows = rows // PIECES

    def row_copy(d, piece):
        to = lax.rem(f + d, nf)
        return pltpu.make_async_remote_copy(
            src_ref=emb_ref.at[
                pl.ds(pl.multiple_of(to * rows + piece * piece_rows, piece_rows), piece_rows), :
            ],
            dst_ref=rows_ref.at[
                pl.ds(piece * piece_rows, piece_rows),
                pl.ds(pl.multiple_of(f * width, width), width),
            ],
            send_sem=row_send.at[d, piece],
            recv_sem=row_recv.at[d, piece],
            device_id={"blk": z, "feat": to},
            device_id_type=MESH,
        )

    def step(way):
        return jnp.clip(z + 1 - 2 * way, 0, nb - 1)

    def onward(way):
        return (z + 1 < nb) if way == 0 else (z > 0)

    def source(way, hop):
        zz = z - hop if way == 0 else z + hop
        return (zz >= 0) if way == 0 else (zz < nb), jnp.clip(zz, 0, nb - 1)

    def arrived(cond, kind, d, here):
        pl.when(cond)(remote(here, here, kind, d, z, sibling).wait_recv)
        return here

    def pass_thin(way, hop):
        cond, zz = source(way, hop)
        d = (way * nb + hop) * per
        here = arrived(cond, 0, d, thin_spot(all_ref, zz, c, x))
        if hop + 1 < nb:
            go(jnp.logical_and(cond, onward(way)), remote(here, here, 0, d + per, step(way), f))
        go(cond, remote(here, here, 1, d, z, (1 - x) * 2 + c))
        go(cond, remote(here, here, 2, d, z, sibling))

    def pass_wide(way, hop, p):
        cond, zz = source(way, hop)
        d = (way * nb + hop) * per + p
        here = arrived(cond, 4, d, wide_spot(all_ref, zz, p, c))
        if hop + 1 < nb:
            go(jnp.logical_and(cond, onward(way)), remote(here, here, 4, d + per, step(way), f))
        go(cond, remote(here, here, 5, d, z, sibling))

    def pass_across(way, hop):
        cond, zz = source(way, hop)
        d = (way * nb + hop) * per
        here = arrived(cond, 1, d, thin_spot(all_ref, zz, c, 1 - x))
        go(cond, remote(here, here, 3, d, z, sibling))

    def have_thin(way, hop):
        cond, zz = source(way, hop)
        d = (way * nb + hop) * per
        arrived(cond, 2, d, thin_spot(all_ref, zz, 1 - c, x))
        arrived(cond, 3, d, thin_spot(all_ref, zz, 1 - c, 1 - x))

    def have_wide(way, hop, p):
        cond, zz = source(way, hop)
        arrived(cond, 5, (way * nb + hop) * per + p, wide_spot(all_ref, zz, p, 1 - c))

    def both(turn, *where):
        for way in range(2):
            turn(way, *where)

    def panel_turns(hop, first, last, turn):
        def one(t, carry):
            way, p = lax.rem(t, 2), t // 2
            zz = z + (2 * way - 1) * hop
            fits = jnp.logical_and(zz >= 0, zz < nb)
            fits = jnp.logical_and(fits, jnp.logical_or(hop > 0, way == 0))

            @pl.when(fits)
            def _():
                turn(zz * per + p)

            return carry

        lax.fori_loop(first * 2, last * 2, one, 0)

    def scores(hop, first, last, row_blocks):
        span = len(row_blocks) * RB
        low = row_blocks[0]

        def turn(col):
            panel = all_ref[pl.ds(pl.multiple_of(col * CB, CB), CB), :]
            if low == 0:
                wider = panel.astype(jnp.float32)
                offs = 0.5 * jnp.sum(wider * wider, axis=1, keepdims=True)
                if len(row_blocks) < local:
                    offs_ref[col] = offs
            else:
                offs = offs_ref[col]
            raw = lax.dot_general(
                panel,
                rows_ref[low * RB : low * RB + span, :],
                transposed,
                preferred_element_type=jnp.float32,
            )
            for r in row_blocks:
                part = raw[:, (r - low) * RB : (r - low + 1) * RB]
                value = jnp.where(
                    allow_ref[r, col] > 0, (part - offs) * scale, neg_big
                )
                score_ref[r, col] = value
                old = top_ref[r]
                top = jnp.maximum(old, jnp.max(value, axis=0, keepdims=True))
                sum_ref[r] = sum_ref[r] * jnp.exp(old - top) + jnp.sum(
                    jnp.exp(value - top), axis=0, keepdims=True
                )
                top_ref[r] = top

        panel_turns(hop, first, last, turn)

    first_pieces = PIECES // local
    for way in range(2):
        d = (way * nb + 1) * per
        mine = thin_spot(cen_ref, 0, c, x)
        go(onward(way), remote(mine, thin_spot(all_ref, z, c, x), 0, d, step(way), f))
    for p in range(per):
        for way in range(2):
            d = (way * nb + 1) * per + p
            mine = wide_spot(cen_ref, 0, p, c)
            go(onward(way), remote(mine, wide_spot(all_ref, z, p, c), 4, d, step(way), f))
    row_copies = [[row_copy(d, piece) for d in range(1, nf)] for piece in range(PIECES)]
    for piece in range(first_pieces):
        for copy in row_copies[piece]:
            copy.start()
    loads = [
        pltpu.make_async_copy(
            emb_ref.at[pl.ds(pl.multiple_of(f * rows, rows), rows), :],
            rows_ref.at[:, pl.ds(pl.multiple_of(f * width, width), width)],
            own_sem.at[0],
        ),
        pltpu.make_async_copy(
            cen_ref, all_ref.at[pl.ds(pl.multiple_of(z * per * CB, CB), per * CB), :], own_sem.at[1]
        ),
    ]
    for copy in loads:
        copy.start()
    top_ref[...] = jnp.full_like(top_ref, neg_big)
    sum_ref[...] = jnp.zeros_like(sum_ref)
    early = list(range(1))
    late = list(range(1, local))
    both(pass_thin, 1)
    for piece in range(first_pieces, PIECES):
        for copy in row_copies[piece]:
            copy.start()
    for copy in loads:
        copy.wait()
    for p in range(per):
        both(pass_wide, 1, p)
    both(pass_thin, 2)
    for piece in range(first_pieces):
        for copy in row_copies[piece]:
            copy.wait_recv()
    scores(0, 0, per, early)
    both(pass_across, 1)
    both(have_thin, 1)
    for p in range(per):
        both(have_wide, 1, p)
    scores(1, 0, per, early)
    for p in range(per):
        both(pass_wide, 2, p)
    for hop in range(3, nb):
        both(pass_thin, hop)
        for p in range(per):
            if hop < nb - 1 or p < per - 1:
                both(pass_wide, hop, p)
    for piece in range(first_pieces, PIECES):
        for copy in row_copies[piece]:
            copy.wait_recv()
    scores(0, 0, per, late)
    scores(1, 0, per, late)
    for hop in range(2, nb):
        both(pass_across, hop)
        both(have_thin, hop)
        for p in range(per):
            both(have_wide, hop, p)
            scores(hop, p, p + 1, early + late)
            if hop == nb - 2 and p == per - 2:
                both(pass_wide, nb - 1, per - 1)

    for r in range(local):
        norm = top_ref[r] + jnp.log(sum_ref[r])
        for j in range(RB // 128):
            norm_ref[r * (RB // 128) + j, :] = norm[0, j * 128 : (j + 1) * 128]
        top_ref[r] = norm

    lead = 0

    def cols(t):
        return pl.ds(pl.multiple_of(t * size, size), size)

    left, right = jnp.int32(0), jnp.int32(nb - 1)
    turns = []
    for _ in range(nb):
        pick = (z - left) >= (right - z)
        turns.append(jnp.where(pick, left, right))
        left, right = jnp.where(pick, left + 1, left), jnp.where(pick, right, right - 1)

    def a_copy(q, t):
        return pltpu.make_async_remote_copy(
            src_ref=to_sib.at[q, :, cols(t)],
            dst_ref=from_sib.at[q, :, cols(t)],
            send_sem=a_send.at[q, t],
            recv_sem=a_recv.at[q, t],
            device_id={"blk": z, "feat": sibling},
            device_id_type=MESH,
        )

    def b_copy(i, t):
        return pltpu.make_async_remote_copy(
            src_ref=to_x.at[i, :, cols(t)],
            dst_ref=from_x.at[i, :, cols(t)],
            send_sem=b_send.at[i, t],
            recv_sem=b_recv.at[i, t],
            device_id={"blk": z, "feat": (1 - x) * 2 + c},
            device_id_type=MESH,
        )

    def z_copy(zz, way, t):
        return pltpu.make_async_remote_copy(
            src_ref=to_z.at[zz, :, cols(t)],
            dst_ref=from_z.at[way, zz, :, cols(t)],
            send_sem=z_send.at[zz, t],
            recv_sem=z_recv.at[way, zz, t],
            device_id={"blk": jnp.clip(z + 1 - 2 * way, 0, nb - 1), "feat": f},
            device_id_type=MESH,
        )

    def line_copy(d):
        zz = lax.rem(z + d, nb)
        return pltpu.make_async_remote_copy(
            src_ref=to_line.at[zz],
            dst_ref=from_line.at[d - 1],
            send_sem=line_send.at[d],
            recv_sem=line_recv.at[d],
            device_id={"blk": zz, "feat": f},
            device_id_type=MESH,
        )

    def swap_copy():
        return pltpu.make_async_remote_copy(
            src_ref=swap_out,
            dst_ref=swap_in,
            send_sem=swap_sem.at[0],
            recv_sem=swap_sem.at[1],
            device_id={"blk": z, "feat": (1 - x) * 2 + c},
            device_id_type=MESH,
        )

    def m_copy(d):
        return pltpu.make_async_remote_copy(
            src_ref=to_mass.at[lax.rem(me + d, n)],
            dst_ref=from_mass.at[d],
            send_sem=m_send.at[d],
            recv_sem=m_recv.at[d],
            device_id=at_offset(d),
            device_id_type=MESH,
        )

    def wide_of(value):
        return value.astype(jnp.float32)

    def place(i):
        zz = turns[nb - 1]
        for t in range(nb - 1):
            zz = jnp.where(i == t, turns[t], zz)
        return zz

    group = CHUNKS // SPANS

    def weights(i, side):
        zz = place(i)
        xx = 1 - x if side == 0 else x
        col = zz * per + xx
        for cc in range(2):
            at = c if cc == 0 else 1 - c
            first = side * CB + cc * own
            for r in range(local):
                value = score_ref[r, col, pl.ds(pl.multiple_of(at * own, own), own), :]
                weight_ref[first : first + own, r * RB : (r + 1) * RB] = jnp.exp(
                    value - top_ref[r]
                ).astype(jnp.bfloat16)

    def masses(i, side):
        zz = place(i)
        xx = 1 - x if side == 0 else x
        part = slice(side * CB, (side + 1) * CB)
        mass = lax.dot_general(
            jnp.ones((8, rows), jnp.bfloat16),
            weight_ref[part, :],
            transposed,
            preferred_element_type=jnp.float32,
        )
        to_mass[zz * nf + xx * 2 + c] = mass[:, :own]
        to_mass[zz * nf + xx * 2 + 1 - c] = mass[:, own:]

    def sums(i):
        for side in range(2):
            weights(i, side)

        def span(u, carry):
            @pl.when(u < SPANS)
            def _():
                at = pl.ds(pl.multiple_of(u * group * size, group * size), group * size)
                total = jnp.dot(
                    weight_ref[...], rows_ref[:, at], preferred_element_type=jnp.float32
                )
                for side in range(2):
                    first = side * CB
                    keep_ref[side * nb + i, :, at] = total[first : first + own]
                    to_sib[side * nb + i, :, at] = total[first + own : first + CB].astype(jnp.bfloat16)
                for side in range(2):
                    for t in range(group):
                        a_copy(side * nb + i, u * group + t).start()

            @pl.when(u == 2)
            def _():
                send_line(i)

            @pl.when(u > 1)
            def _():
                for t in range(group):
                    at = (u - 2) * group + t
                    pl.when(at > lead)(functools.partial(send_x, i, at))

            return carry

        lax.fori_loop(0, SPANS + 2, span, 0)
        for side in range(2):
            masses(i, side)

    def send_x(i, t):
        a_copy(i, t).wait()
        to_x[i, :, cols(t)] = (
            keep_ref[i, :, cols(t)] + wide_of(from_sib[i, :, cols(t)])
        ).astype(jnp.bfloat16)
        b_copy(i, t).start()

    def course(i):
        zz = place(i)
        fed = jnp.logical_or(
            jnp.logical_and(zz > z, z > 0), jnp.logical_and(zz < z, z < nb - 1)
        )
        return zz, (zz < z).astype(jnp.int32), fed

    def send_line(i):
        zz = place(i)
        for side in range(2):
            q = side * nb + i
            a_copy(q, lead).wait()
            sides_ref[side] = keep_ref[q, :, cols(lead)] + wide_of(from_sib[q, :, cols(lead)])

        @pl.when(zz != z)
        def _():
            to_line[zz] = sides_ref[...].astype(jnp.bfloat16)
            line_copy(lax.rem(zz - z + nb, nb)).start()

    def swap():
        def one(d, carry):
            line_copy(d).wait()
            sides_ref[...] += wide_of(from_line[d - 1])
            return carry

        lax.fori_loop(1, nb, one, 0)
        swap_out[...] = sides_ref[0].astype(jnp.bfloat16)
        swap_copy().start()

    def mass_end(d, total):
        m_copy(d).wait()
        return total + from_mass[d]

    def masses_in():
        mass = lax.fori_loop(1, n, mass_end, to_mass[me])[:1]
        spread = jnp.broadcast_to(mass, (own, own))
        diagonal = lax.broadcasted_iota(jnp.int32, (own, own), 0) == lax.broadcasted_iota(
            jnp.int32, (own, own), 1
        )
        inverse_ref[...] = 1.0 / (
            jnp.sum(jnp.where(diagonal, spread, 0.0), axis=1, keepdims=True) + prior_mass
        )

    def finish(t, total):
        old = all_ref[pl.ds(pl.multiple_of(me * own, own), own), cols(t)]
        num_ref[:, cols(t)] = (total + prior_mass * wide_of(old)) * inverse_ref[...]

    def send_z(i):
        zz, way, fed = course(i)
        q = nb + i

        def chunk(t, carry):
            a_copy(q, t).wait()
            b_copy(i, t).wait()
            part_ref[...] = (
                keep_ref[q, :, cols(t)]
                + wide_of(from_sib[q, :, cols(t)])
                + wide_of(from_x[i, :, cols(t)])
            )

            @pl.when(fed)
            def _():
                z_copy(zz, way, t).wait_recv()
                part_ref[...] += wide_of(from_z[way, zz, :, cols(t)])

            @pl.when(zz != z)
            def _():
                to_z[zz, :, cols(t)] = part_ref[...].astype(jnp.bfloat16)
                z_copy(zz, way, t).start()

            @pl.when(zz == z)
            def _():
                for back in range(2):

                    @pl.when((z > 0) if back == 0 else (z < nb - 1))
                    def _():
                        z_copy(z, back, t).wait_recv()
                        part_ref[...] += wide_of(from_z[back, z, :, cols(t)])

                finish(t, part_ref[...])

            return carry

        lax.fori_loop(lead + 1, CHUNKS, chunk, 0)

    def turn(i, carry):
        @pl.when(i < nb)
        def _():
            sums(i)

        @pl.when(i == nb - 1)
        def _():
            def mass_start(d, carry):
                m_copy(d).start()
                return carry

            lax.fori_loop(1, n, mass_start, 0)

        pl.when(i == nb + 1)(swap)
        pl.when(i == nb + 1)(masses_in)

        @pl.when(i > 1)
        def _():
            send_z(i - 2)

        return carry

    lax.fori_loop(0, nb + 2, turn, 0)

    def last(t, carry):
        for zz in range(nb):

            @pl.when(z != zz)
            def _():
                z_copy(zz, 0, t).wait_send()

        return carry

    lax.fori_loop(lead + 1, CHUNKS, last, 0)
    swap_copy().wait()
    finish(lead, sides_ref[1] + wide_of(swap_in[...]))
    for group in row_copies:
        for copy in group:
            copy.wait_send()
    for cond, copy in started:
        pl.when(cond)(copy.wait_send)


def fused(allow, embeddings, centroids, nb, nf):
    rows = embeddings.shape[0] // nf
    local = rows // RB
    n = nb * nf
    own = K // n
    per = K // nb // CB
    kinds = 6
    vmem = pl.BlockSpec(memory_space=pltpu.VMEM)
    hbm = pl.BlockSpec(memory_space=pltpu.HBM)
    dma = pltpu.SemaphoreType.DMA
    bf16, f32 = jnp.bfloat16, jnp.float32
    return pl.pallas_call(
        functools.partial(fused_kernel, nb, nf),
        out_shape=(
            jax.ShapeDtypeStruct((own, D), f32),
            jax.ShapeDtypeStruct((rows // 128, 128), f32),
        ),
        in_specs=[pl.BlockSpec(memory_space=pltpu.SMEM), hbm, hbm],
        out_specs=(vmem,) * 2,
        scratch_shapes=[
            pltpu.VMEM((rows, D), bf16),
            pltpu.VMEM((K, D), bf16),
            pltpu.VMEM((NCB, CB, 1), f32),
            pltpu.VMEM((local, NCB, CB, RB), f32),
            pltpu.VMEM((local, 1, RB), f32),
            pltpu.VMEM((local, 1, RB), f32),
            pltpu.VMEM((2 * CB, rows), bf16),
            pltpu.VMEM((2 * nb, own, D), f32),
            pltpu.VMEM((2 * nb, own, D), bf16),
            pltpu.VMEM((2 * nb, own, D), bf16),
            pltpu.VMEM((nb, own, D), bf16),
            pltpu.VMEM((nb, own, D), bf16),
            pltpu.VMEM((own, D // CHUNKS), f32),
            pltpu.VMEM((nb, own, D), bf16),
            pltpu.VMEM((2, nb, own, D), bf16),
            pltpu.VMEM((2, own, D // CHUNKS), f32),
            pltpu.VMEM((nb, 2, own, D // CHUNKS), bf16),
            pltpu.VMEM((nb - 1, 2, own, D // CHUNKS), bf16),
            pltpu.VMEM((own, D // CHUNKS), bf16),
            pltpu.VMEM((own, D // CHUNKS), bf16),
            pltpu.VMEM((n, 8, own), f32),
            pltpu.VMEM((n, 8, own), f32),
            pltpu.VMEM((own, 1), f32),
            dma((nf, PIECES)),
            dma((nf, PIECES)),
            dma((kinds, 2 * nb * per)),
            dma((kinds, 2 * nb * per)),
            dma((2,)),
            dma((2 * nb, CHUNKS)),
            dma((2 * nb, CHUNKS)),
            dma((nb, CHUNKS)),
            dma((nb, CHUNKS)),
            dma((nb, CHUNKS)),
            dma((2, nb, CHUNKS)),
            dma((n,)),
            dma((n,)),
            dma((nb,)),
            dma((nb,)),
            dma((2,)),
        ],
        compiler_params=pltpu.CompilerParams(
            collective_id=2, has_side_effects=True, vmem_limit_bytes=58 * 2**20
        ),
        name="fused",
    )(allow, embeddings, centroids)


def body(embeddings, centroids, pair_list):
    nb, nf = lax.axis_size("blk"), lax.axis_size("feat")
    local_rows = embeddings.shape[0] // nf
    local_blocks = local_rows // RB
    device_index = lax.axis_index("blk") * nf + lax.axis_index("feat")
    mine = device_index * local_blocks + jnp.arange(local_blocks, dtype=jnp.int32)
    row_ids, col_ids = pair_list[:, 0], pair_list[:, 1]
    same = row_ids[None, :] == mine[:, None]
    if K // nb == 2 * CB and nf == 4 and local_blocks == 2:
        blocks = jnp.arange(NCB, dtype=jnp.int32)
        listed = same[:, None, :] & (col_ids[None, None, :] == blocks[None, :, None])
        allow = jnp.sum(listed.astype(jnp.int32), axis=2)
        new_centroids, log_norm = fused(allow, embeddings, centroids, nb, nf)
        return (new_centroids, log_norm.reshape(local_rows))
    before = jnp.sum((row_ids[None, :] < mine[:, None]).astype(jnp.int32), axis=1)
    counts = jnp.sum(same.astype(jnp.int32), axis=1)
    rank = jnp.arange(row_ids.shape[0], dtype=jnp.int32)[None, :] - before[:, None]
    slots = jnp.arange(SLOTS, dtype=jnp.int32)
    picked = same[:, None, :] & (rank[:, None, :] == slots[None, :, None])
    chosen = jnp.sum(jnp.where(picked, col_ids[None, None, :], 0), axis=2)
    table = jnp.concatenate([counts[:, None], chosen], axis=1)

    row_data, panels = fetch(embeddings, centroids, nb, nf)
    num, mass, log_norm = terms(table, row_data, panels, nb, nf)
    numerator, denominator = reduce_sums(num, mass, nb, nf)

    own_count = centroids.shape[0] // nf
    own_rows = lax.dynamic_slice_in_dim(
        centroids, lax.axis_index("feat") * own_count, own_count, 0
    ).astype(jnp.float32)
    new_centroids = (numerator + prior_mass * own_rows) / (denominator[0][:, None] + prior_mass)
    return (new_centroids, log_norm.reshape(local_rows))


def solution(mesh):
    return jax.shard_map(
        body,
        mesh=mesh,
        in_specs=(P(("groups", "blk"), "feat"), P(("groups", "blk"), None), P("groups", None)),
        out_specs=(P(("groups", "blk", "feat"), None), P(("groups", "blk", "feat"))),
        check_vma=False,
    )
```

```python
import functools
import math

import jax
import jax.numpy as jnp
from jax import lax
from jax.experimental import pallas as pl
from jax.experimental.pallas import tpu as pltpu
from jax.sharding import PartitionSpec as P

D = 2048
K = 2048
RB = 512
CB = 256
NCB = K // CB
SLOTS = 4
PARTS = 8
PIECES = 2
CHUNKS = 8
SPANS = 4

neg_big = -1e30
prior_mass = 16.0
MESH = pl.DeviceIdType.MESH


def meet(peers):
    barrier = pltpu.get_barrier_semaphore()
    for peer in peers:
        pl.semaphore_signal(barrier, inc=1, device_id=peer, device_id_type=MESH)
    pl.semaphore_wait(barrier, len(peers))


def fetch_kernel(
    nb, nf, emb_ref, cen_ref, rows_ref, all_ref, row_send, row_recv, send, recv, own_sem,
    emb_hold, cen_hold,
):
    z = lax.axis_index("blk")
    f = lax.axis_index("feat")
    nx = nf // 2
    c = lax.rem(f, 2)
    x = f // 2
    rows, width = rows_ref.shape[0], emb_ref.shape[1]
    half = cen_ref.shape[0] // 2
    thin = D * 3 // 8 // nx // 128 * 128
    wide = D - nx * thin
    sibling = x * 2 + 1 - c

    def across(dx):
        return lax.rem(x + dx, nx)

    meet(
        [{"blk": z, "feat": lax.rem(f + d, nf)} for d in range(1, nf)]
        + [{"blk": lax.rem(z + d, nb), "feat": f} for d in range(1, nb)]
    )

    def spot(zz, cc, col, size):
        return all_ref.at[
            pl.ds(pl.multiple_of(zz * 2 * half + cc * half, half), half),
            pl.ds(pl.multiple_of(col, 128), size),
        ]

    def remote(src, dst, kind, d, blk, feat):
        return pltpu.make_async_remote_copy(
            src_ref=src,
            dst_ref=dst,
            send_sem=send.at[kind, d],
            recv_sem=recv.at[kind, d],
            device_id={"blk": blk, "feat": feat},
            device_id_type=MESH,
        )

    def own_part(col, size):
        return cen_ref.at[
            pl.ds(pl.multiple_of(c * half, half), half), pl.ds(pl.multiple_of(col, 128), size)
        ]

    thin_col = wide + x * thin
    started = []

    def go(cond, copy):
        pl.when(cond)(copy.start)
        started.append((cond, copy))

    def row_copy(d, piece):
        to = lax.rem(f + d, nf)
        size = rows // PIECES
        return pltpu.make_async_remote_copy(
            src_ref=emb_ref.at[pl.ds(pl.multiple_of(to * rows + piece * size, size), size), :],
            dst_ref=rows_ref.at[
                pl.ds(piece * size, size), pl.ds(pl.multiple_of(f * width, width), width)
            ],
            send_sem=row_send.at[d, piece],
            recv_sem=row_recv.at[d, piece],
            device_id={"blk": z, "feat": to},
            device_id_type=MESH,
        )

    def step(way):
        return jnp.clip(z + 1 - 2 * way, 0, nb - 1)

    def onward(way):
        return (z + 1 < nb) if way == 0 else (z > 0)

    for way in range(2):
        go(
            onward(way),
            remote(own_part(thin_col, thin), spot(z, c, thin_col, thin), 1, way * nb + 1, step(way), f),
        )
    for way in range(2):
        go(onward(way), remote(own_part(0, wide), spot(z, c, 0, wide), 0, way * nb + 1, step(way), f))
    row_copies = [row_copy(d, piece) for piece in range(PIECES) for d in range(1, nf)]
    for copy in row_copies:
        copy.start()
    holds = [
        (
            emb_ref.at[pl.ds(pl.multiple_of(f * rows, rows), rows), :],
            emb_hold,
            rows_ref.at[:, pl.ds(pl.multiple_of(f * width, width), width)],
        ),
        (
            cen_ref,
            cen_hold,
            all_ref.at[pl.ds(pl.multiple_of(z * 2 * half, half), 2 * half), :],
        ),
    ]
    loads = [pltpu.make_async_copy(src, hold, own_sem.at[i]) for i, (src, hold, _) in enumerate(holds)]
    stores = [
        pltpu.make_async_copy(hold, dst, own_sem.at[2 + i]) for i, (_, hold, dst) in enumerate(holds)
    ]
    for copy in loads:
        copy.start()
    for load, store in zip(loads, stores):
        load.wait()
        store.start()

    def source(way, hop):
        zz = z - hop if way == 0 else z + hop
        return (zz >= 0) if way == 0 else (zz < nb), jnp.clip(zz, 0, nb - 1)

    def arrived(cond, kind, d, zz, cc, col, size):
        here = spot(zz, cc, col, size)
        pl.when(cond)(remote(here, here, kind, d, z, sibling).wait_recv)
        return here

    turns = [(way, hop) for hop in range(1, nb) for way in range(2)]

    def pass_thin(way, hop):
        cond, zz = source(way, hop)
        d = way * nb + hop
        here = arrived(cond, 1, d, zz, c, thin_col, thin)
        if hop + 1 < nb:
            go(jnp.logical_and(cond, onward(way)), remote(here, here, 1, d + 1, step(way), f))
        for dx in range(1, nx):
            go(cond, remote(here, here, 4 + dx, d, z, across(dx) * 2 + c))
        go(cond, remote(here, here, 3, d, z, sibling))

    def pass_wide(way, hop):
        cond, zz = source(way, hop)
        d = way * nb + hop
        here = arrived(cond, 0, d, zz, c, 0, wide)
        if hop + 1 < nb:
            go(jnp.logical_and(cond, onward(way)), remote(here, here, 0, d + 1, step(way), f))
        go(cond, remote(here, here, 2, d, z, sibling))

    def pass_across(way, hop):
        cond, zz = source(way, hop)
        d = way * nb + hop
        for dx in range(1, nx):
            col = wide + lax.rem(x + nx - dx, nx) * thin
            here = arrived(cond, 4 + dx, d, zz, c, col, thin)
            go(cond, remote(here, here, 4 + nx + dx, d, z, sibling))

    for hop in range(1, nb):
        for way in range(2):
            pass_thin(way, hop)
        for way in range(2):
            pass_wide(way, hop)
    for way, hop in turns:
        pass_across(way, hop)
    for way, hop in turns:
        cond, zz = source(way, hop)
        d = way * nb + hop
        arrived(cond, 2, d, zz, 1 - c, 0, wide)
        arrived(cond, 3, d, zz, 1 - c, thin_col, thin)
        for dx in range(1, nx):
            col = wide + lax.rem(x + nx - dx, nx) * thin
            arrived(cond, 4 + nx + dx, d, zz, 1 - c, col, thin)
    for copy in stores:
        copy.wait()
    for copy in row_copies:
        copy.wait()
    for cond, copy in started:
        pl.when(cond)(copy.wait_send)


def fetch(embeddings, centroids, nb, nf):
    rows = embeddings.shape[0] // nf
    kinds = 4 + 2 * (nf // 2) + 1
    return pl.pallas_call(
        functools.partial(fetch_kernel, nb, nf),
        out_shape=(
            jax.ShapeDtypeStruct((rows, D), jnp.bfloat16),
            jax.ShapeDtypeStruct((K, D), jnp.bfloat16),
        ),
        in_specs=[pl.BlockSpec(memory_space=pltpu.HBM)] * 2,
        out_specs=(pl.BlockSpec(memory_space=pl.ANY),) * 2,
        scratch_shapes=[
            pltpu.SemaphoreType.DMA((nf, PIECES)),
            pltpu.SemaphoreType.DMA((nf, PIECES)),
            pltpu.SemaphoreType.DMA((kinds, 2 * nb)),
            pltpu.SemaphoreType.DMA((kinds, 2 * nb)),
            pltpu.SemaphoreType.DMA((4,)),
            pltpu.VMEM((rows, D // nf), jnp.bfloat16),
            pltpu.VMEM((K // nb, D), jnp.bfloat16),
        ],
        compiler_params=pltpu.CompilerParams(
            collective_id=0, has_side_effects=True, vmem_limit_bytes=6 * 2**20
        ),
        name="fetch",
    )(embeddings, centroids)


def term_kernel(nb, nf, tab_ref, rows_ref, all_ref, num_ref, mass_ref, norm_ref, score_ref, weight_ref, acc_ref, row_mass):
    local = rows_ref.shape[0] // RB
    scale = 1.0 / math.sqrt(D)
    own = K // (nb * nf)
    nx = nf // 2
    transposed = (((1,), (1,)), ((), ()))

    for r in range(local):
        part = rows_ref[r * RB : (r + 1) * RB, :]
        count = tab_ref[r, 0]

        def score_turn(slot, top):
            col = tab_ref[r, 1 + slot]
            panel = all_ref[pl.ds(pl.multiple_of(col * CB, CB), CB), :]
            wide = panel.astype(jnp.float32)
            offs = 0.5 * jnp.sum(wide * wide, axis=1, keepdims=True)
            raw = lax.dot_general(panel, part, transposed, preferred_element_type=jnp.float32)
            scores = (raw - offs) * scale
            score_ref[slot] = scores
            return jnp.maximum(top, jnp.max(scores, axis=0, keepdims=True))

        top = lax.fori_loop(0, count, score_turn, jnp.full((1, RB), neg_big, jnp.float32))

        def sum_turn(slot, total):
            return total + jnp.sum(jnp.exp(score_ref[slot] - top), axis=0, keepdims=True)

        total = lax.fori_loop(0, count, sum_turn, jnp.zeros((1, RB), jnp.float32))
        norm = top + jnp.log(total)
        norm_ref[r] = norm

        def weight_turn(slot, carry):
            col = tab_ref[r, 1 + slot]
            weight_ref[r, col] = jnp.exp(score_ref[slot] - norm).astype(jnp.bfloat16)
            return carry

        lax.fori_loop(0, count, weight_turn, 0)

    def col_turn(col, carry):
        acc_ref[...] = jnp.zeros_like(acc_ref)
        row_mass[...] = jnp.zeros_like(row_mass)
        for r in range(local):
            hit = jnp.int32(0)
            for slot in range(SLOTS):
                found = jnp.logical_and(tab_ref[r, 1 + slot] == col, slot < tab_ref[r, 0])
                hit = hit + found.astype(jnp.int32)

            @pl.when(hit > 0)
            def _():
                weights = weight_ref[r, col]
                acc_ref[...] += jnp.dot(
                    weights, rows_ref[r * RB : (r + 1) * RB, :], preferred_element_type=jnp.float32
                )
                row_mass[...] += lax.dot_general(
                    jnp.ones((8, RB), jnp.bfloat16),
                    weights,
                    transposed,
                    preferred_element_type=jnp.float32,
                )

        for j in range(CB // own):
            owner = col * (CB // own) + j
            zz, ff = owner // nf, lax.rem(owner, nf)
            num_ref[lax.rem(ff, 2), ff // 2, zz] = acc_ref[j * own : (j + 1) * own, :].astype(
                jnp.bfloat16
            )
            mass_ref[owner] = row_mass[:, j * own : (j + 1) * own]
        return carry

    lax.fori_loop(0, NCB, col_turn, 0)


def terms(table, row_data, panels, nb, nf):
    local = row_data.shape[0] // RB
    own = K // (nb * nf)
    vmem = pl.BlockSpec(memory_space=pltpu.VMEM)
    return pl.pallas_call(
        functools.partial(term_kernel, nb, nf),
        out_shape=(
            jax.ShapeDtypeStruct((2, nf // 2, nb, own, D), jnp.bfloat16),
            jax.ShapeDtypeStruct((nb * nf, 8, own), jnp.float32),
            jax.ShapeDtypeStruct((local, 1, RB), jnp.float32),
        ),
        in_specs=[pl.BlockSpec(memory_space=pltpu.SMEM), vmem, vmem],
        out_specs=(vmem,) * 3,
        scratch_shapes=[
            pltpu.VMEM((SLOTS, CB, RB), jnp.float32),
            pltpu.VMEM((local, NCB, CB, RB), jnp.bfloat16),
            pltpu.VMEM((CB, D), jnp.float32),
            pltpu.VMEM((8, CB), jnp.float32),
        ],
        compiler_params=pltpu.CompilerParams(vmem_limit_bytes=32 * 2**20),
        name="terms",
    )(table, row_data, panels)


def reduce_kernel(
    nb, nf, num_ref, mass_ref, out_ref, out_mass,
    from_sib, to_x, from_x, to_z, from_z, from_mass,
    a_send, a_recv, b_send, b_recv, c_send, c_recv, m_send, m_recv,
):
    z = lax.axis_index("blk")
    f = lax.axis_index("feat")
    nx = nf // 2
    n = nb * nf
    me = z * nf + f
    c = lax.rem(f, 2)
    x = f // 2
    sibling = x * 2 + 1 - c
    size = D // PARTS

    def at_offset(d):
        other = lax.rem(me + d, n)
        return {"blk": other // nf, "feat": lax.rem(other, nf)}

    barrier = pltpu.get_barrier_semaphore()

    def greet(d, carry):
        pl.semaphore_signal(barrier, inc=1, device_id=at_offset(d), device_id_type=MESH)
        return carry

    lax.fori_loop(1, n, greet, 0)
    pl.semaphore_wait(barrier, n - 1)

    def cols(t):
        return pl.ds(t * size, size)

    def a_copy(dx, t):
        xx = lax.rem(x + dx, nx)
        return pltpu.make_async_remote_copy(
            src_ref=num_ref.at[1 - c, xx, :, :, cols(t)],
            dst_ref=from_sib.at[xx, :, :, cols(t)],
            send_sem=a_send.at[dx, t],
            recv_sem=a_recv.at[dx, t],
            device_id={"blk": z, "feat": sibling},
            device_id_type=MESH,
        )

    def b_copy(dx, t):
        return pltpu.make_async_remote_copy(
            src_ref=to_x.at[dx - 1, :, :, cols(t)],
            dst_ref=from_x.at[dx - 1, :, :, cols(t)],
            send_sem=b_send.at[dx, t],
            recv_sem=b_recv.at[dx, t],
            device_id={"blk": z, "feat": lax.rem(x + dx, nx) * 2 + c},
            device_id_type=MESH,
        )

    def c_copy(d, t):
        return pltpu.make_async_remote_copy(
            src_ref=to_z.at[d - 1, :, cols(t)],
            dst_ref=from_z.at[d - 1, :, cols(t)],
            send_sem=c_send.at[d, t],
            recv_sem=c_recv.at[d, t],
            device_id={"blk": lax.rem(z + d, nb), "feat": f},
            device_id_type=MESH,
        )

    def m_copy(d):
        return pltpu.make_async_remote_copy(
            src_ref=mass_ref.at[lax.rem(me + d, n)],
            dst_ref=from_mass.at[d],
            send_sem=m_send.at[d],
            recv_sem=m_recv.at[d],
            device_id=at_offset(d),
            device_id_type=MESH,
        )

    def wide(value):
        return value.astype(jnp.float32)

    for t in range(PARTS):
        for dx in range(1, nx):
            a_copy(dx, t).start()
    for t in range(PARTS):
        a_copy(0, t).start()

    def mass_start(d, carry):
        m_copy(d).start()
        return carry

    lax.fori_loop(1, n, mass_start, 0)

    for t in range(PARTS):
        for dx in range(1, nx):
            xx = lax.rem(x + dx, nx)
            a_copy(dx, t).wait()
            for zz in range(nb):
                to_x[dx - 1, zz, :, cols(t)] = (
                    wide(num_ref[c, xx, zz, :, cols(t)]) + wide(from_sib[xx, zz, :, cols(t)])
                ).astype(jnp.bfloat16)
            b_copy(dx, t).start()

    def blk_sum(zz, t):
        total = wide(num_ref[c, x, zz, :, cols(t)]) + wide(from_sib[x, zz, :, cols(t)])
        for dx in range(1, nx):
            total = total + wide(from_x[dx - 1, zz, :, cols(t)])
        return total

    for t in range(PARTS):
        a_copy(0, t).wait()
        for dx in range(1, nx):
            b_copy(dx, t).wait()
        for d in range(1, nb):
            to_z[d - 1, :, cols(t)] = blk_sum(lax.rem(z + d, nb), t).astype(jnp.bfloat16)
            c_copy(d, t).start()
        out_ref[:, cols(t)] = blk_sum(z, t)

    def mass_end(d, total):
        m_copy(d).wait()
        return total + from_mass[d]

    out_mass[...] = lax.fori_loop(1, n, mass_end, mass_ref[me])

    for t in range(PARTS):
        total = out_ref[:, cols(t)]
        for d in range(1, nb):
            c_copy(d, t).wait()
            total = total + wide(from_z[d - 1, :, cols(t)])
        out_ref[:, cols(t)] = total


def reduce_sums(num, mass, nb, nf):
    own = K // (nb * nf)
    nx = nf // 2
    n = nb * nf
    vmem = pl.BlockSpec(memory_space=pltpu.VMEM)
    dma = pltpu.SemaphoreType.DMA
    return pl.pallas_call(
        functools.partial(reduce_kernel, nb, nf),
        out_shape=(
            jax.ShapeDtypeStruct((own, D), jnp.float32),
            jax.ShapeDtypeStruct((8, own), jnp.float32),
        ),
        in_specs=[vmem] * 2,
        out_specs=(vmem,) * 2,
        scratch_shapes=[
            pltpu.VMEM((nx, nb, own, D), jnp.bfloat16),
            pltpu.VMEM((nx - 1, nb, own, D), jnp.bfloat16),
            pltpu.VMEM((nx - 1, nb, own, D), jnp.bfloat16),
            pltpu.VMEM((nb - 1, own, D), jnp.bfloat16),
            pltpu.VMEM((nb - 1, own, D), jnp.bfloat16),
            pltpu.VMEM((n, 8, own), jnp.float32),
        ]
        + [dma((nx, PARTS))] * 4
        + [dma((nb, PARTS))] * 2
        + [dma((n,))] * 2,
        compiler_params=pltpu.CompilerParams(
            collective_id=1, has_side_effects=True, vmem_limit_bytes=24 * 2**20
        ),
        name="reduce_sums",
    )(num, mass)


def fused_kernel(
    nb, nf, allow_ref, emb_ref, cen_ref, num_ref, norm_ref,
    rows_ref, all_ref, offs_ref, score_ref, top_ref, sum_ref, weight_ref, keep_ref,
    to_sib, from_sib, to_x, from_x, part_ref, to_z, from_z, sides_ref, to_line, from_line,
    swap_out, swap_in, to_mass, from_mass, inverse_ref,
    row_send, row_recv, send, recv, own_sem, a_send, a_recv, b_send, b_recv, z_send, z_recv,
    m_send, m_recv, line_send, line_recv, swap_sem,
):
    z = lax.axis_index("blk")
    f = lax.axis_index("feat")
    n = nb * nf
    me = z * nf + f
    c = lax.rem(f, 2)
    x = f // 2
    rows, width = rows_ref.shape[0], emb_ref.shape[1]
    local = rows // RB
    per = K // nb // CB
    half = CB // 2
    own = K // n
    thin = D * 3 // 16
    wide = D - 2 * thin
    sibling = x * 2 + 1 - c
    size = D // CHUNKS
    scale = 1.0 / math.sqrt(D)
    transposed = (((1,), (1,)), ((), ()))

    def at_offset(d):
        other = lax.rem(me + d, n)
        return {"blk": other // nf, "feat": lax.rem(other, nf)}

    barrier = pltpu.get_barrier_semaphore()

    def greet(d, carry):
        pl.semaphore_signal(barrier, inc=1, device_id=at_offset(d), device_id_type=MESH)
        return carry

    lax.fori_loop(1, n, greet, 0)
    pl.semaphore_wait(barrier, n - 1)

    def wide_spot(ref, block, p, cc):
        first = (block * per + p) * CB + cc * half
        return ref.at[pl.ds(pl.multiple_of(first, half), half), pl.ds(0, wide)]

    def thin_spot(ref, block, cc, xx):
        count = per * half
        return ref.at[
            pl.ds(pl.multiple_of((block * 2 + cc) * count, count), count),
            pl.ds(pl.multiple_of(wide + xx * thin, 128), thin),
        ]

    def remote(src, dst, kind, d, blk, feat):
        return pltpu.make_async_remote_copy(
            src_ref=src,
            dst_ref=dst,
            send_sem=send.at[kind, d],
            recv_sem=recv.at[kind, d],
            device_id={"blk": blk, "feat": feat},
            device_id_type=MESH,
        )

    started = []

    def go(cond, copy):
        pl.when(cond)(copy.start)
        started.append((cond, copy))

    piece_rows = rows // PIECES

    def row_copy(d, piece):
        to = lax.rem(f + d, nf)
        return pltpu.make_async_remote_copy(
            src_ref=emb_ref.at[
                pl.ds(pl.multiple_of(to * rows + piece * piece_rows, piece_rows), piece_rows), :
            ],
            dst_ref=rows_ref.at[
                pl.ds(piece * piece_rows, piece_rows),
                pl.ds(pl.multiple_of(f * width, width), width),
            ],
            send_sem=row_send.at[d, piece],
            recv_sem=row_recv.at[d, piece],
            device_id={"blk": z, "feat": to},
            device_id_type=MESH,
        )

    def step(way):
        return jnp.clip(z + 1 - 2 * way, 0, nb - 1)

    def onward(way):
        return (z + 1 < nb) if way == 0 else (z > 0)

    def source(way, hop):
        zz = z - hop if way == 0 else z + hop
        return (zz >= 0) if way == 0 else (zz < nb), jnp.clip(zz, 0, nb - 1)

    def arrived(cond, kind, d, here):
        pl.when(cond)(remote(here, here, kind, d, z, sibling).wait_recv)
        return here

    def pass_thin(way, hop):
        cond, zz = source(way, hop)
        d = (way * nb + hop) * per
        here = arrived(cond, 0, d, thin_spot(all_ref, zz, c, x))
        if hop + 1 < nb:
            go(jnp.logical_and(cond, onward(way)), remote(here, here, 0, d + per, step(way), f))
        go(cond, remote(here, here, 1, d, z, (1 - x) * 2 + c))
        go(cond, remote(here, here, 2, d, z, sibling))

    def pass_wide(way, hop, p):
        cond, zz = source(way, hop)
        d = (way * nb + hop) * per + p
        here = arrived(cond, 4, d, wide_spot(all_ref, zz, p, c))
        if hop + 1 < nb:
            go(jnp.logical_and(cond, onward(way)), remote(here, here, 4, d + per, step(way), f))
        go(cond, remote(here, here, 5, d, z, sibling))

    def pass_across(way, hop):
        cond, zz = source(way, hop)
        d = (way * nb + hop) * per
        here = arrived(cond, 1, d, thin_spot(all_ref, zz, c, 1 - x))
        go(cond, remote(here, here, 3, d, z, sibling))

    def have_thin(way, hop):
        cond, zz = source(way, hop)
        d = (way * nb + hop) * per
        arrived(cond, 2, d, thin_spot(all_ref, zz, 1 - c, x))
        arrived(cond, 3, d, thin_spot(all_ref, zz, 1 - c, 1 - x))

    def have_wide(way, hop, p):
        cond, zz = source(way, hop)
        arrived(cond, 5, (way * nb + hop) * per + p, wide_spot(all_ref, zz, p, 1 - c))

    def both(turn, *where):
        for way in range(2):
            turn(way, *where)

    def panel_turns(hop, first, last, turn):
        def one(t, carry):
            way, p = lax.rem(t, 2), t // 2
            zz = z + (2 * way - 1) * hop
            fits = jnp.logical_and(zz >= 0, zz < nb)
            fits = jnp.logical_and(fits, jnp.logical_or(hop > 0, way == 0))

            @pl.when(fits)
            def _():
                turn(zz * per + p)

            return carry

        lax.fori_loop(first * 2, last * 2, one, 0)

    def scores(hop, first, last, row_blocks):
        span = len(row_blocks) * RB
        low = row_blocks[0]

        def turn(col):
            panel = all_ref[pl.ds(pl.multiple_of(col * CB, CB), CB), :]
            if low == 0:
                wider = panel.astype(jnp.float32)
                offs = 0.5 * jnp.sum(wider * wider, axis=1, keepdims=True)
                if len(row_blocks) < local:
                    offs_ref[col] = offs
            else:
                offs = offs_ref[col]
            raw = lax.dot_general(
                panel,
                rows_ref[low * RB : low * RB + span, :],
                transposed,
                preferred_element_type=jnp.float32,
            )
            for r in row_blocks:
                part = raw[:, (r - low) * RB : (r - low + 1) * RB]
                value = jnp.where(
                    allow_ref[r, col] > 0, (part - offs) * scale, neg_big
                )
                score_ref[r, col] = value
                old = top_ref[r]
                top = jnp.maximum(old, jnp.max(value, axis=0, keepdims=True))
                sum_ref[r] = sum_ref[r] * jnp.exp(old - top) + jnp.sum(
                    jnp.exp(value - top), axis=0, keepdims=True
                )
                top_ref[r] = top

        panel_turns(hop, first, last, turn)

    first_pieces = PIECES // local
    for way in range(2):
        d = (way * nb + 1) * per
        mine = thin_spot(cen_ref, 0, c, x)
        go(onward(way), remote(mine, thin_spot(all_ref, z, c, x), 0, d, step(way), f))
    for p in range(per):
        for way in range(2):
            d = (way * nb + 1) * per + p
            mine = wide_spot(cen_ref, 0, p, c)
            go(onward(way), remote(mine, wide_spot(all_ref, z, p, c), 4, d, step(way), f))
    row_copies = [[row_copy(d, piece) for d in range(1, nf)] for piece in range(PIECES)]
    for piece in range(first_pieces):
        for copy in row_copies[piece]:
            copy.start()
    loads = [
        pltpu.make_async_copy(
            emb_ref.at[pl.ds(pl.multiple_of(f * rows, rows), rows), :],
            rows_ref.at[:, pl.ds(pl.multiple_of(f * width, width), width)],
            own_sem.at[0],
        ),
        pltpu.make_async_copy(
            cen_ref, all_ref.at[pl.ds(pl.multiple_of(z * per * CB, CB), per * CB), :], own_sem.at[1]
        ),
    ]
    for copy in loads:
        copy.start()
    top_ref[...] = jnp.full_like(top_ref, neg_big)
    sum_ref[...] = jnp.zeros_like(sum_ref)
    early = list(range(1))
    late = list(range(1, local))
    both(pass_thin, 1)
    for piece in range(first_pieces, PIECES):
        for copy in row_copies[piece]:
            copy.start()
    for copy in loads:
        copy.wait()
    for p in range(per):
        both(pass_wide, 1, p)
    both(pass_thin, 2)
    for piece in range(first_pieces):
        for copy in row_copies[piece]:
            copy.wait_recv()
    scores(0, 0, per, early)
    both(pass_across, 1)
    both(have_thin, 1)
    for p in range(per):
        both(have_wide, 1, p)
    scores(1, 0, per, early)
    for p in range(per):
        both(pass_wide, 2, p)
    for hop in range(3, nb):
        both(pass_thin, hop)
        for p in range(per):
            if hop < nb - 1 or p < per - 1:
                both(pass_wide, hop, p)
    for piece in range(first_pieces, PIECES):
        for copy in row_copies[piece]:
            copy.wait_recv()
    scores(0, 0, per, late)
    scores(1, 0, per, late)
    for hop in range(2, nb):
        both(pass_across, hop)
        both(have_thin, hop)
        for p in range(per):
            both(have_wide, hop, p)
            scores(hop, p, p + 1, early + late)
            if hop == nb - 2 and p == per - 2:
                both(pass_wide, nb - 1, per - 1)

    for r in range(local):
        norm = top_ref[r] + jnp.log(sum_ref[r])
        for j in range(RB // 128):
            norm_ref[r * (RB // 128) + j, :] = norm[0, j * 128 : (j + 1) * 128]
        top_ref[r] = norm

    lead = 0

    def cols(t):
        return pl.ds(pl.multiple_of(t * size, size), size)

    left, right = jnp.int32(0), jnp.int32(nb - 1)
    turns = []
    for _ in range(nb):
        pick = (z - left) >= (right - z)
        turns.append(jnp.where(pick, left, right))
        left, right = jnp.where(pick, left + 1, left), jnp.where(pick, right, right - 1)

    def a_copy(q, t):
        return pltpu.make_async_remote_copy(
            src_ref=to_sib.at[q, :, cols(t)],
            dst_ref=from_sib.at[q, :, cols(t)],
            send_sem=a_send.at[q, t],
            recv_sem=a_recv.at[q, t],
            device_id={"blk": z, "feat": sibling},
            device_id_type=MESH,
        )

    def b_copy(i, t):
        return pltpu.make_async_remote_copy(
            src_ref=to_x.at[i, :, cols(t)],
            dst_ref=from_x.at[i, :, cols(t)],
            send_sem=b_send.at[i, t],
            recv_sem=b_recv.at[i, t],
            device_id={"blk": z, "feat": (1 - x) * 2 + c},
            device_id_type=MESH,
        )

    def z_copy(zz, way, t):
        return pltpu.make_async_remote_copy(
            src_ref=to_z.at[zz, :, cols(t)],
            dst_ref=from_z.at[way, zz, :, cols(t)],
            send_sem=z_send.at[zz, t],
            recv_sem=z_recv.at[way, zz, t],
            device_id={"blk": jnp.clip(z + 1 - 2 * way, 0, nb - 1), "feat": f},
            device_id_type=MESH,
        )

    def line_copy(d):
        zz = lax.rem(z + d, nb)
        return pltpu.make_async_remote_copy(
            src_ref=to_line.at[zz],
            dst_ref=from_line.at[d - 1],
            send_sem=line_send.at[d],
            recv_sem=line_recv.at[d],
            device_id={"blk": zz, "feat": f},
            device_id_type=MESH,
        )

    def swap_copy():
        return pltpu.make_async_remote_copy(
            src_ref=swap_out,
            dst_ref=swap_in,
            send_sem=swap_sem.at[0],
            recv_sem=swap_sem.at[1],
            device_id={"blk": z, "feat": (1 - x) * 2 + c},
            device_id_type=MESH,
        )

    def m_copy(d):
        return pltpu.make_async_remote_copy(
            src_ref=to_mass.at[lax.rem(me + d, n)],
            dst_ref=from_mass.at[d],
            send_sem=m_send.at[d],
            recv_sem=m_recv.at[d],
            device_id=at_offset(d),
            device_id_type=MESH,
        )

    def wide_of(value):
        return value.astype(jnp.float32)

    def place(i):
        zz = turns[nb - 1]
        for t in range(nb - 1):
            zz = jnp.where(i == t, turns[t], zz)
        return zz

    group = CHUNKS // SPANS

    def weights(i, side):
        zz = place(i)
        xx = 1 - x if side == 0 else x
        col = zz * per + xx
        for cc in range(2):
            at = c if cc == 0 else 1 - c
            first = side * CB + cc * own
            for r in range(local):
                value = score_ref[r, col, pl.ds(pl.multiple_of(at * own, own), own), :]
                weight_ref[first : first + own, r * RB : (r + 1) * RB] = jnp.exp(
                    value - top_ref[r]
                ).astype(jnp.bfloat16)

    def masses(i, side):
        zz = place(i)
        xx = 1 - x if side == 0 else x
        part = slice(side * CB, (side + 1) * CB)
        mass = lax.dot_general(
            jnp.ones((8, rows), jnp.bfloat16),
            weight_ref[part, :],
            transposed,
            preferred_element_type=jnp.float32,
        )
        to_mass[zz * nf + xx * 2 + c] = mass[:, :own]
        to_mass[zz * nf + xx * 2 + 1 - c] = mass[:, own:]

    def sums(i):
        for side in range(2):
            weights(i, side)

        def span(u, carry):
            @pl.when(u < SPANS)
            def _():
                at = pl.ds(pl.multiple_of(u * group * size, group * size), group * size)
                total = jnp.dot(
                    weight_ref[...], rows_ref[:, at], preferred_element_type=jnp.float32
                )
                for side in range(2):
                    first = side * CB
                    keep_ref[side * nb + i, :, at] = total[first : first + own]
                    to_sib[side * nb + i, :, at] = total[first + own : first + CB].astype(jnp.bfloat16)
                for side in range(2):
                    for t in range(group):
                        a_copy(side * nb + i, u * group + t).start()

            @pl.when(u > 1)
            def _():
                for t in range(group):
                    at = (u - 2) * group + t
                    pl.when(at > lead)(functools.partial(send_x, i, at))

            @pl.when(u == 2)
            def _():
                send_line(i)

            return carry

        lax.fori_loop(0, SPANS + 2, span, 0)
        for side in range(2):
            masses(i, side)

    def send_x(i, t):
        a_copy(i, t).wait()
        to_x[i, :, cols(t)] = (
            keep_ref[i, :, cols(t)] + wide_of(from_sib[i, :, cols(t)])
        ).astype(jnp.bfloat16)
        b_copy(i, t).start()

    def course(i):
        zz = place(i)
        fed = jnp.logical_or(
            jnp.logical_and(zz > z, z > 0), jnp.logical_and(zz < z, z < nb - 1)
        )
        return zz, (zz < z).astype(jnp.int32), fed

    def send_line(i):
        zz = place(i)
        for side in range(2):
            q = side * nb + i
            a_copy(q, lead).wait()
            sides_ref[side] = keep_ref[q, :, cols(lead)] + wide_of(from_sib[q, :, cols(lead)])

        @pl.when(zz != z)
        def _():
            to_line[zz] = sides_ref[...].astype(jnp.bfloat16)
            line_copy(lax.rem(zz - z + nb, nb)).start()

    def swap():
        def one(d, carry):
            line_copy(d).wait()
            sides_ref[...] += wide_of(from_line[d - 1])
            return carry

        lax.fori_loop(1, nb, one, 0)
        swap_out[...] = sides_ref[0].astype(jnp.bfloat16)
        swap_copy().start()

    def mass_end(d, total):
        m_copy(d).wait()
        return total + from_mass[d]

    def masses_in():
        mass = lax.fori_loop(1, n, mass_end, to_mass[me])[:1]
        spread = jnp.broadcast_to(mass, (own, own))
        diagonal = lax.broadcasted_iota(jnp.int32, (own, own), 0) == lax.broadcasted_iota(
            jnp.int32, (own, own), 1
        )
        inverse_ref[...] = 1.0 / (
            jnp.sum(jnp.where(diagonal, spread, 0.0), axis=1, keepdims=True) + prior_mass
        )

    def finish(t, total):
        old = all_ref[pl.ds(pl.multiple_of(me * own, own), own), cols(t)]
        num_ref[:, cols(t)] = (total + prior_mass * wide_of(old)) * inverse_ref[...]

    def send_z(i):
        zz, way, fed = course(i)
        q = nb + i

        def chunk(t, carry):
            a_copy(q, t).wait()
            b_copy(i, t).wait()
            part_ref[...] = (
                keep_ref[q, :, cols(t)]
                + wide_of(from_sib[q, :, cols(t)])
                + wide_of(from_x[i, :, cols(t)])
            )

            @pl.when(fed)
            def _():
                z_copy(zz, way, t).wait_recv()
                part_ref[...] += wide_of(from_z[way, zz, :, cols(t)])

            @pl.when(zz != z)
            def _():
                to_z[zz, :, cols(t)] = part_ref[...].astype(jnp.bfloat16)
                z_copy(zz, way, t).start()

            @pl.when(zz == z)
            def _():
                for back in range(2):

                    @pl.when((z > 0) if back == 0 else (z < nb - 1))
                    def _():
                        z_copy(z, back, t).wait_recv()
                        part_ref[...] += wide_of(from_z[back, z, :, cols(t)])

                finish(t, part_ref[...])

            return carry

        lax.fori_loop(lead + 1, CHUNKS, chunk, 0)

    def turn(i, carry):
        @pl.when(i < nb)
        def _():
            sums(i)

        @pl.when(i == nb - 1)
        def _():
            def mass_start(d, carry):
                m_copy(d).start()
                return carry

            lax.fori_loop(1, n, mass_start, 0)

        pl.when(i == nb + 1)(swap)
        pl.when(i == nb + 1)(masses_in)

        @pl.when(i > 1)
        def _():
            send_z(i - 2)

        return carry

    lax.fori_loop(0, nb + 2, turn, 0)

    def last(t, carry):
        for zz in range(nb):

            @pl.when(z != zz)
            def _():
                z_copy(zz, 0, t).wait_send()

        return carry

    lax.fori_loop(lead + 1, CHUNKS, last, 0)
    swap_copy().wait()
    finish(lead, sides_ref[1] + wide_of(swap_in[...]))
    for group in row_copies:
        for copy in group:
            copy.wait_send()
    for cond, copy in started:
        pl.when(cond)(copy.wait_send)


def fused(allow, embeddings, centroids, nb, nf):
    rows = embeddings.shape[0] // nf
    local = rows // RB
    n = nb * nf
    own = K // n
    per = K // nb // CB
    kinds = 6
    vmem = pl.BlockSpec(memory_space=pltpu.VMEM)
    hbm = pl.BlockSpec(memory_space=pltpu.HBM)
    dma = pltpu.SemaphoreType.DMA
    bf16, f32 = jnp.bfloat16, jnp.float32
    return pl.pallas_call(
        functools.partial(fused_kernel, nb, nf),
        out_shape=(
            jax.ShapeDtypeStruct((own, D), f32),
            jax.ShapeDtypeStruct((rows // 128, 128), f32),
        ),
        in_specs=[pl.BlockSpec(memory_space=pltpu.SMEM), hbm, hbm],
        out_specs=(vmem,) * 2,
        scratch_shapes=[
            pltpu.VMEM((rows, D), bf16),
            pltpu.VMEM((K, D), bf16),
            pltpu.VMEM((NCB, CB, 1), f32),
            pltpu.VMEM((local, NCB, CB, RB), f32),
            pltpu.VMEM((local, 1, RB), f32),
            pltpu.VMEM((local, 1, RB), f32),
            pltpu.VMEM((2 * CB, rows), bf16),
            pltpu.VMEM((2 * nb, own, D), f32),
            pltpu.VMEM((2 * nb, own, D), bf16),
            pltpu.VMEM((2 * nb, own, D), bf16),
            pltpu.VMEM((nb, own, D), bf16),
            pltpu.VMEM((nb, own, D), bf16),
            pltpu.VMEM((own, D // CHUNKS), f32),
            pltpu.VMEM((nb, own, D), bf16),
            pltpu.VMEM((2, nb, own, D), bf16),
            pltpu.VMEM((2, own, D // CHUNKS), f32),
            pltpu.VMEM((nb, 2, own, D // CHUNKS), bf16),
            pltpu.VMEM((nb - 1, 2, own, D // CHUNKS), bf16),
            pltpu.VMEM((own, D // CHUNKS), bf16),
            pltpu.VMEM((own, D // CHUNKS), bf16),
            pltpu.VMEM((n, 8, own), f32),
            pltpu.VMEM((n, 8, own), f32),
            pltpu.VMEM((own, 1), f32),
            dma((nf, PIECES)),
            dma((nf, PIECES)),
            dma((kinds, 2 * nb * per)),
            dma((kinds, 2 * nb * per)),
            dma((2,)),
            dma((2 * nb, CHUNKS)),
            dma((2 * nb, CHUNKS)),
            dma((nb, CHUNKS)),
            dma((nb, CHUNKS)),
            dma((nb, CHUNKS)),
            dma((2, nb, CHUNKS)),
            dma((n,)),
            dma((n,)),
            dma((nb,)),
            dma((nb,)),
            dma((2,)),
        ],
        compiler_params=pltpu.CompilerParams(
            collective_id=2, has_side_effects=True, vmem_limit_bytes=58 * 2**20
        ),
        name="fused",
    )(allow, embeddings, centroids)


def body(embeddings, centroids, pair_list):
    nb, nf = lax.axis_size("blk"), lax.axis_size("feat")
    local_rows = embeddings.shape[0] // nf
    local_blocks = local_rows // RB
    device_index = lax.axis_index("blk") * nf + lax.axis_index("feat")
    mine = device_index * local_blocks + jnp.arange(local_blocks, dtype=jnp.int32)
    row_ids, col_ids = pair_list[:, 0], pair_list[:, 1]
    same = row_ids[None, :] == mine[:, None]
    if K // nb == 2 * CB and nf == 4 and local_blocks == 2:
        blocks = jnp.arange(NCB, dtype=jnp.int32)
        listed = same[:, None, :] & (col_ids[None, None, :] == blocks[None, :, None])
        allow = jnp.sum(listed.astype(jnp.int32), axis=2)
        new_centroids, log_norm = fused(allow, embeddings, centroids, nb, nf)
        return (new_centroids, log_norm.reshape(local_rows))
    before = jnp.sum((row_ids[None, :] < mine[:, None]).astype(jnp.int32), axis=1)
    counts = jnp.sum(same.astype(jnp.int32), axis=1)
    rank = jnp.arange(row_ids.shape[0], dtype=jnp.int32)[None, :] - before[:, None]
    slots = jnp.arange(SLOTS, dtype=jnp.int32)
    picked = same[:, None, :] & (rank[:, None, :] == slots[None, :, None])
    chosen = jnp.sum(jnp.where(picked, col_ids[None, None, :], 0), axis=2)
    table = jnp.concatenate([counts[:, None], chosen], axis=1)

    row_data, panels = fetch(embeddings, centroids, nb, nf)
    num, mass, log_norm = terms(table, row_data, panels, nb, nf)
    numerator, denominator = reduce_sums(num, mass, nb, nf)

    own_count = centroids.shape[0] // nf
    own_rows = lax.dynamic_slice_in_dim(
        centroids, lax.axis_index("feat") * own_count, own_count, 0
    ).astype(jnp.float32)
    new_centroids = (numerator + prior_mass * own_rows) / (denominator[0][:, None] + prior_mass)
    return (new_centroids, log_norm.reshape(local_rows))


def solution(mesh):
    return jax.shard_map(
        body,
        mesh=mesh,
        in_specs=(P(("groups", "blk"), "feat"), P(("groups", "blk"), None), P("groups", None)),
        out_specs=(P(("groups", "blk", "feat"), None), P(("groups", "blk", "feat"))),
        check_vma=False,
    )
```

```python
import functools
import math

import jax
import jax.numpy as jnp
from jax import lax
from jax.experimental import pallas as pl
from jax.experimental.pallas import tpu as pltpu
from jax.sharding import PartitionSpec as P

D = 2048
K = 2048
RB = 512
CB = 256
NCB = K // CB
SLOTS = 4
PARTS = 8
PIECES = 2
CHUNKS = 8
SPANS = 4

neg_big = -1e30
prior_mass = 16.0
MESH = pl.DeviceIdType.MESH


def meet(peers):
    barrier = pltpu.get_barrier_semaphore()
    for peer in peers:
        pl.semaphore_signal(barrier, inc=1, device_id=peer, device_id_type=MESH)
    pl.semaphore_wait(barrier, len(peers))


def fetch_kernel(
    nb, nf, emb_ref, cen_ref, rows_ref, all_ref, row_send, row_recv, send, recv, own_sem,
    emb_hold, cen_hold,
):
    z = lax.axis_index("blk")
    f = lax.axis_index("feat")
    nx = nf // 2
    c = lax.rem(f, 2)
    x = f // 2
    rows, width = rows_ref.shape[0], emb_ref.shape[1]
    half = cen_ref.shape[0] // 2
    thin = D * 3 // 8 // nx // 128 * 128
    wide = D - nx * thin
    sibling = x * 2 + 1 - c

    def across(dx):
        return lax.rem(x + dx, nx)

    meet(
        [{"blk": z, "feat": lax.rem(f + d, nf)} for d in range(1, nf)]
        + [{"blk": lax.rem(z + d, nb), "feat": f} for d in range(1, nb)]
    )

    def spot(zz, cc, col, size):
        return all_ref.at[
            pl.ds(pl.multiple_of(zz * 2 * half + cc * half, half), half),
            pl.ds(pl.multiple_of(col, 128), size),
        ]

    def remote(src, dst, kind, d, blk, feat):
        return pltpu.make_async_remote_copy(
            src_ref=src,
            dst_ref=dst,
            send_sem=send.at[kind, d],
            recv_sem=recv.at[kind, d],
            device_id={"blk": blk, "feat": feat},
            device_id_type=MESH,
        )

    def own_part(col, size):
        return cen_ref.at[
            pl.ds(pl.multiple_of(c * half, half), half), pl.ds(pl.multiple_of(col, 128), size)
        ]

    thin_col = wide + x * thin
    started = []

    def go(cond, copy):
        pl.when(cond)(copy.start)
        started.append((cond, copy))

    def row_copy(d, piece):
        to = lax.rem(f + d, nf)
        size = rows // PIECES
        return pltpu.make_async_remote_copy(
            src_ref=emb_ref.at[pl.ds(pl.multiple_of(to * rows + piece * size, size), size), :],
            dst_ref=rows_ref.at[
                pl.ds(piece * size, size), pl.ds(pl.multiple_of(f * width, width), width)
            ],
            send_sem=row_send.at[d, piece],
            recv_sem=row_recv.at[d, piece],
            device_id={"blk": z, "feat": to},
            device_id_type=MESH,
        )

    def step(way):
        return jnp.clip(z + 1 - 2 * way, 0, nb - 1)

    def onward(way):
        return (z + 1 < nb) if way == 0 else (z > 0)

    for way in range(2):
        go(
            onward(way),
            remote(own_part(thin_col, thin), spot(z, c, thin_col, thin), 1, way * nb + 1, step(way), f),
        )
    for way in range(2):
        go(onward(way), remote(own_part(0, wide), spot(z, c, 0, wide), 0, way * nb + 1, step(way), f))
    row_copies = [row_copy(d, piece) for piece in range(PIECES) for d in range(1, nf)]
    for copy in row_copies:
        copy.start()
    holds = [
        (
            emb_ref.at[pl.ds(pl.multiple_of(f * rows, rows), rows), :],
            emb_hold,
            rows_ref.at[:, pl.ds(pl.multiple_of(f * width, width), width)],
        ),
        (
            cen_ref,
            cen_hold,
            all_ref.at[pl.ds(pl.multiple_of(z * 2 * half, half), 2 * half), :],
        ),
    ]
    loads = [pltpu.make_async_copy(src, hold, own_sem.at[i]) for i, (src, hold, _) in enumerate(holds)]
    stores = [
        pltpu.make_async_copy(hold, dst, own_sem.at[2 + i]) for i, (_, hold, dst) in enumerate(holds)
    ]
    for copy in loads:
        copy.start()
    for load, store in zip(loads, stores):
        load.wait()
        store.start()

    def source(way, hop):
        zz = z - hop if way == 0 else z + hop
        return (zz >= 0) if way == 0 else (zz < nb), jnp.clip(zz, 0, nb - 1)

    def arrived(cond, kind, d, zz, cc, col, size):
        here = spot(zz, cc, col, size)
        pl.when(cond)(remote(here, here, kind, d, z, sibling).wait_recv)
        return here

    turns = [(way, hop) for hop in range(1, nb) for way in range(2)]

    def pass_thin(way, hop):
        cond, zz = source(way, hop)
        d = way * nb + hop
        here = arrived(cond, 1, d, zz, c, thin_col, thin)
        if hop + 1 < nb:
            go(jnp.logical_and(cond, onward(way)), remote(here, here, 1, d + 1, step(way), f))
        for dx in range(1, nx):
            go(cond, remote(here, here, 4 + dx, d, z, across(dx) * 2 + c))
        go(cond, remote(here, here, 3, d, z, sibling))

    def pass_wide(way, hop):
        cond, zz = source(way, hop)
        d = way * nb + hop
        here = arrived(cond, 0, d, zz, c, 0, wide)
        if hop + 1 < nb:
            go(jnp.logical_and(cond, onward(way)), remote(here, here, 0, d + 1, step(way), f))
        go(cond, remote(here, here, 2, d, z, sibling))

    def pass_across(way, hop):
        cond, zz = source(way, hop)
        d = way * nb + hop
        for dx in range(1, nx):
            col = wide + lax.rem(x + nx - dx, nx) * thin
            here = arrived(cond, 4 + dx, d, zz, c, col, thin)
            go(cond, remote(here, here, 4 + nx + dx, d, z, sibling))

    for hop in range(1, nb):
        for way in range(2):
            pass_thin(way, hop)
        for way in range(2):
            pass_wide(way, hop)
    for way, hop in turns:
        pass_across(way, hop)
    for way, hop in turns:
        cond, zz = source(way, hop)
        d = way * nb + hop
        arrived(cond, 2, d, zz, 1 - c, 0, wide)
        arrived(cond, 3, d, zz, 1 - c, thin_col, thin)
        for dx in range(1, nx):
            col = wide + lax.rem(x + nx - dx, nx) * thin
            arrived(cond, 4 + nx + dx, d, zz, 1 - c, col, thin)
    for copy in stores:
        copy.wait()
    for copy in row_copies:
        copy.wait()
    for cond, copy in started:
        pl.when(cond)(copy.wait_send)


def fetch(embeddings, centroids, nb, nf):
    rows = embeddings.shape[0] // nf
    kinds = 4 + 2 * (nf // 2) + 1
    return pl.pallas_call(
        functools.partial(fetch_kernel, nb, nf),
        out_shape=(
            jax.ShapeDtypeStruct((rows, D), jnp.bfloat16),
            jax.ShapeDtypeStruct((K, D), jnp.bfloat16),
        ),
        in_specs=[pl.BlockSpec(memory_space=pltpu.HBM)] * 2,
        out_specs=(pl.BlockSpec(memory_space=pl.ANY),) * 2,
        scratch_shapes=[
            pltpu.SemaphoreType.DMA((nf, PIECES)),
            pltpu.SemaphoreType.DMA((nf, PIECES)),
            pltpu.SemaphoreType.DMA((kinds, 2 * nb)),
            pltpu.SemaphoreType.DMA((kinds, 2 * nb)),
            pltpu.SemaphoreType.DMA((4,)),
            pltpu.VMEM((rows, D // nf), jnp.bfloat16),
            pltpu.VMEM((K // nb, D), jnp.bfloat16),
        ],
        compiler_params=pltpu.CompilerParams(
            collective_id=0, has_side_effects=True, vmem_limit_bytes=6 * 2**20
        ),
        name="fetch",
    )(embeddings, centroids)


def term_kernel(nb, nf, tab_ref, rows_ref, all_ref, num_ref, mass_ref, norm_ref, score_ref, weight_ref, acc_ref, row_mass):
    local = rows_ref.shape[0] // RB
    scale = 1.0 / math.sqrt(D)
    own = K // (nb * nf)
    nx = nf // 2
    transposed = (((1,), (1,)), ((), ()))

    for r in range(local):
        part = rows_ref[r * RB : (r + 1) * RB, :]
        count = tab_ref[r, 0]

        def score_turn(slot, top):
            col = tab_ref[r, 1 + slot]
            panel = all_ref[pl.ds(pl.multiple_of(col * CB, CB), CB), :]
            wide = panel.astype(jnp.float32)
            offs = 0.5 * jnp.sum(wide * wide, axis=1, keepdims=True)
            raw = lax.dot_general(panel, part, transposed, preferred_element_type=jnp.float32)
            scores = (raw - offs) * scale
            score_ref[slot] = scores
            return jnp.maximum(top, jnp.max(scores, axis=0, keepdims=True))

        top = lax.fori_loop(0, count, score_turn, jnp.full((1, RB), neg_big, jnp.float32))

        def sum_turn(slot, total):
            return total + jnp.sum(jnp.exp(score_ref[slot] - top), axis=0, keepdims=True)

        total = lax.fori_loop(0, count, sum_turn, jnp.zeros((1, RB), jnp.float32))
        norm = top + jnp.log(total)
        norm_ref[r] = norm

        def weight_turn(slot, carry):
            col = tab_ref[r, 1 + slot]
            weight_ref[r, col] = jnp.exp(score_ref[slot] - norm).astype(jnp.bfloat16)
            return carry

        lax.fori_loop(0, count, weight_turn, 0)

    def col_turn(col, carry):
        acc_ref[...] = jnp.zeros_like(acc_ref)
        row_mass[...] = jnp.zeros_like(row_mass)
        for r in range(local):
            hit = jnp.int32(0)
            for slot in range(SLOTS):
                found = jnp.logical_and(tab_ref[r, 1 + slot] == col, slot < tab_ref[r, 0])
                hit = hit + found.astype(jnp.int32)

            @pl.when(hit > 0)
            def _():
                weights = weight_ref[r, col]
                acc_ref[...] += jnp.dot(
                    weights, rows_ref[r * RB : (r + 1) * RB, :], preferred_element_type=jnp.float32
                )
                row_mass[...] += lax.dot_general(
                    jnp.ones((8, RB), jnp.bfloat16),
                    weights,
                    transposed,
                    preferred_element_type=jnp.float32,
                )

        for j in range(CB // own):
            owner = col * (CB // own) + j
            zz, ff = owner // nf, lax.rem(owner, nf)
            num_ref[lax.rem(ff, 2), ff // 2, zz] = acc_ref[j * own : (j + 1) * own, :].astype(
                jnp.bfloat16
            )
            mass_ref[owner] = row_mass[:, j * own : (j + 1) * own]
        return carry

    lax.fori_loop(0, NCB, col_turn, 0)


def terms(table, row_data, panels, nb, nf):
    local = row_data.shape[0] // RB
    own = K // (nb * nf)
    vmem = pl.BlockSpec(memory_space=pltpu.VMEM)
    return pl.pallas_call(
        functools.partial(term_kernel, nb, nf),
        out_shape=(
            jax.ShapeDtypeStruct((2, nf // 2, nb, own, D), jnp.bfloat16),
            jax.ShapeDtypeStruct((nb * nf, 8, own), jnp.float32),
            jax.ShapeDtypeStruct((local, 1, RB), jnp.float32),
        ),
        in_specs=[pl.BlockSpec(memory_space=pltpu.SMEM), vmem, vmem],
        out_specs=(vmem,) * 3,
        scratch_shapes=[
            pltpu.VMEM((SLOTS, CB, RB), jnp.float32),
            pltpu.VMEM((local, NCB, CB, RB), jnp.bfloat16),
            pltpu.VMEM((CB, D), jnp.float32),
            pltpu.VMEM((8, CB), jnp.float32),
        ],
        compiler_params=pltpu.CompilerParams(vmem_limit_bytes=32 * 2**20),
        name="terms",
    )(table, row_data, panels)


def reduce_kernel(
    nb, nf, num_ref, mass_ref, out_ref, out_mass,
    from_sib, to_x, from_x, to_z, from_z, from_mass,
    a_send, a_recv, b_send, b_recv, c_send, c_recv, m_send, m_recv,
):
    z = lax.axis_index("blk")
    f = lax.axis_index("feat")
    nx = nf // 2
    n = nb * nf
    me = z * nf + f
    c = lax.rem(f, 2)
    x = f // 2
    sibling = x * 2 + 1 - c
    size = D // PARTS

    def at_offset(d):
        other = lax.rem(me + d, n)
        return {"blk": other // nf, "feat": lax.rem(other, nf)}

    barrier = pltpu.get_barrier_semaphore()

    def greet(d, carry):
        pl.semaphore_signal(barrier, inc=1, device_id=at_offset(d), device_id_type=MESH)
        return carry

    lax.fori_loop(1, n, greet, 0)
    pl.semaphore_wait(barrier, n - 1)

    def cols(t):
        return pl.ds(t * size, size)

    def a_copy(dx, t):
        xx = lax.rem(x + dx, nx)
        return pltpu.make_async_remote_copy(
            src_ref=num_ref.at[1 - c, xx, :, :, cols(t)],
            dst_ref=from_sib.at[xx, :, :, cols(t)],
            send_sem=a_send.at[dx, t],
            recv_sem=a_recv.at[dx, t],
            device_id={"blk": z, "feat": sibling},
            device_id_type=MESH,
        )

    def b_copy(dx, t):
        return pltpu.make_async_remote_copy(
            src_ref=to_x.at[dx - 1, :, :, cols(t)],
            dst_ref=from_x.at[dx - 1, :, :, cols(t)],
            send_sem=b_send.at[dx, t],
            recv_sem=b_recv.at[dx, t],
            device_id={"blk": z, "feat": lax.rem(x + dx, nx) * 2 + c},
            device_id_type=MESH,
        )

    def c_copy(d, t):
        return pltpu.make_async_remote_copy(
            src_ref=to_z.at[d - 1, :, cols(t)],
            dst_ref=from_z.at[d - 1, :, cols(t)],
            send_sem=c_send.at[d, t],
            recv_sem=c_recv.at[d, t],
            device_id={"blk": lax.rem(z + d, nb), "feat": f},
            device_id_type=MESH,
        )

    def m_copy(d):
        return pltpu.make_async_remote_copy(
            src_ref=mass_ref.at[lax.rem(me + d, n)],
            dst_ref=from_mass.at[d],
            send_sem=m_send.at[d],
            recv_sem=m_recv.at[d],
            device_id=at_offset(d),
            device_id_type=MESH,
        )

    def wide(value):
        return value.astype(jnp.float32)

    for t in range(PARTS):
        for dx in range(1, nx):
            a_copy(dx, t).start()
    for t in range(PARTS):
        a_copy(0, t).start()

    def mass_start(d, carry):
        m_copy(d).start()
        return carry

    lax.fori_loop(1, n, mass_start, 0)

    for t in range(PARTS):
        for dx in range(1, nx):
            xx = lax.rem(x + dx, nx)
            a_copy(dx, t).wait()
            for zz in range(nb):
                to_x[dx - 1, zz, :, cols(t)] = (
                    wide(num_ref[c, xx, zz, :, cols(t)]) + wide(from_sib[xx, zz, :, cols(t)])
                ).astype(jnp.bfloat16)
            b_copy(dx, t).start()

    def blk_sum(zz, t):
        total = wide(num_ref[c, x, zz, :, cols(t)]) + wide(from_sib[x, zz, :, cols(t)])
        for dx in range(1, nx):
            total = total + wide(from_x[dx - 1, zz, :, cols(t)])
        return total

    for t in range(PARTS):
        a_copy(0, t).wait()
        for dx in range(1, nx):
            b_copy(dx, t).wait()
        for d in range(1, nb):
            to_z[d - 1, :, cols(t)] = blk_sum(lax.rem(z + d, nb), t).astype(jnp.bfloat16)
            c_copy(d, t).start()
        out_ref[:, cols(t)] = blk_sum(z, t)

    def mass_end(d, total):
        m_copy(d).wait()
        return total + from_mass[d]

    out_mass[...] = lax.fori_loop(1, n, mass_end, mass_ref[me])

    for t in range(PARTS):
        total = out_ref[:, cols(t)]
        for d in range(1, nb):
            c_copy(d, t).wait()
            total = total + wide(from_z[d - 1, :, cols(t)])
        out_ref[:, cols(t)] = total


def reduce_sums(num, mass, nb, nf):
    own = K // (nb * nf)
    nx = nf // 2
    n = nb * nf
    vmem = pl.BlockSpec(memory_space=pltpu.VMEM)
    dma = pltpu.SemaphoreType.DMA
    return pl.pallas_call(
        functools.partial(reduce_kernel, nb, nf),
        out_shape=(
            jax.ShapeDtypeStruct((own, D), jnp.float32),
            jax.ShapeDtypeStruct((8, own), jnp.float32),
        ),
        in_specs=[vmem] * 2,
        out_specs=(vmem,) * 2,
        scratch_shapes=[
            pltpu.VMEM((nx, nb, own, D), jnp.bfloat16),
            pltpu.VMEM((nx - 1, nb, own, D), jnp.bfloat16),
            pltpu.VMEM((nx - 1, nb, own, D), jnp.bfloat16),
            pltpu.VMEM((nb - 1, own, D), jnp.bfloat16),
            pltpu.VMEM((nb - 1, own, D), jnp.bfloat16),
            pltpu.VMEM((n, 8, own), jnp.float32),
        ]
        + [dma((nx, PARTS))] * 4
        + [dma((nb, PARTS))] * 2
        + [dma((n,))] * 2,
        compiler_params=pltpu.CompilerParams(
            collective_id=1, has_side_effects=True, vmem_limit_bytes=24 * 2**20
        ),
        name="reduce_sums",
    )(num, mass)


def fused_kernel(
    nb, nf, allow_ref, emb_ref, cen_ref, num_ref, norm_ref,
    rows_ref, all_ref, offs_ref, score_ref, top_ref, sum_ref, weight_ref, keep_ref,
    to_sib, from_sib, to_x, from_x, part_ref, to_z, from_z, sides_ref, to_line, from_line,
    swap_out, swap_in, to_mass, from_mass, inverse_ref,
    row_send, row_recv, send, recv, own_sem, a_send, a_recv, b_send, b_recv, z_send, z_recv,
    m_send, m_recv, line_send, line_recv, swap_sem,
):
    z = lax.axis_index("blk")
    f = lax.axis_index("feat")
    n = nb * nf
    me = z * nf + f
    c = lax.rem(f, 2)
    x = f // 2
    rows, width = rows_ref.shape[0], emb_ref.shape[1]
    local = rows // RB
    per = K // nb // CB
    half = CB // 2
    own = K // n
    thin = D * 3 // 16
    wide = D - 2 * thin
    sibling = x * 2 + 1 - c
    size = D // CHUNKS
    scale = 1.0 / math.sqrt(D)
    transposed = (((1,), (1,)), ((), ()))

    def at_offset(d):
        other = lax.rem(me + d, n)
        return {"blk": other // nf, "feat": lax.rem(other, nf)}

    barrier = pltpu.get_barrier_semaphore()

    def greet(d, carry):
        pl.semaphore_signal(barrier, inc=1, device_id=at_offset(d), device_id_type=MESH)
        return carry

    lax.fori_loop(1, n, greet, 0)
    pl.semaphore_wait(barrier, n - 1)

    def wide_spot(ref, block, p, cc):
        first = (block * per + p) * CB + cc * half
        return ref.at[pl.ds(pl.multiple_of(first, half), half), pl.ds(0, wide)]

    def thin_spot(ref, block, cc, xx):
        count = per * half
        return ref.at[
            pl.ds(pl.multiple_of((block * 2 + cc) * count, count), count),
            pl.ds(pl.multiple_of(wide + xx * thin, 128), thin),
        ]

    def remote(src, dst, kind, d, blk, feat):
        return pltpu.make_async_remote_copy(
            src_ref=src,
            dst_ref=dst,
            send_sem=send.at[kind, d],
            recv_sem=recv.at[kind, d],
            device_id={"blk": blk, "feat": feat},
            device_id_type=MESH,
        )

    started = []

    def go(cond, copy):
        pl.when(cond)(copy.start)
        started.append((cond, copy))

    piece_rows = rows // PIECES

    def row_copy(d, piece):
        to = lax.rem(f + d, nf)
        return pltpu.make_async_remote_copy(
            src_ref=emb_ref.at[
                pl.ds(pl.multiple_of(to * rows + piece * piece_rows, piece_rows), piece_rows), :
            ],
            dst_ref=rows_ref.at[
                pl.ds(piece * piece_rows, piece_rows),
                pl.ds(pl.multiple_of(f * width, width), width),
            ],
            send_sem=row_send.at[d, piece],
            recv_sem=row_recv.at[d, piece],
            device_id={"blk": z, "feat": to},
            device_id_type=MESH,
        )

    def step(way):
        return jnp.clip(z + 1 - 2 * way, 0, nb - 1)

    def onward(way):
        return (z + 1 < nb) if way == 0 else (z > 0)

    def source(way, hop):
        zz = z - hop if way == 0 else z + hop
        return (zz >= 0) if way == 0 else (zz < nb), jnp.clip(zz, 0, nb - 1)

    def arrived(cond, kind, d, here):
        pl.when(cond)(remote(here, here, kind, d, z, sibling).wait_recv)
        return here

    def pass_thin(way, hop):
        cond, zz = source(way, hop)
        d = (way * nb + hop) * per
        here = arrived(cond, 0, d, thin_spot(all_ref, zz, c, x))
        if hop + 1 < nb:
            go(jnp.logical_and(cond, onward(way)), remote(here, here, 0, d + per, step(way), f))
        go(cond, remote(here, here, 1, d, z, (1 - x) * 2 + c))
        go(cond, remote(here, here, 2, d, z, sibling))

    def pass_wide(way, hop, p):
        cond, zz = source(way, hop)
        d = (way * nb + hop) * per + p
        here = arrived(cond, 4, d, wide_spot(all_ref, zz, p, c))
        if hop + 1 < nb:
            go(jnp.logical_and(cond, onward(way)), remote(here, here, 4, d + per, step(way), f))
        go(cond, remote(here, here, 5, d, z, sibling))

    def pass_across(way, hop):
        cond, zz = source(way, hop)
        d = (way * nb + hop) * per
        here = arrived(cond, 1, d, thin_spot(all_ref, zz, c, 1 - x))
        go(cond, remote(here, here, 3, d, z, sibling))

    def have_thin(way, hop):
        cond, zz = source(way, hop)
        d = (way * nb + hop) * per
        arrived(cond, 2, d, thin_spot(all_ref, zz, 1 - c, x))
        arrived(cond, 3, d, thin_spot(all_ref, zz, 1 - c, 1 - x))

    def have_wide(way, hop, p):
        cond, zz = source(way, hop)
        arrived(cond, 5, (way * nb + hop) * per + p, wide_spot(all_ref, zz, p, 1 - c))

    def both(turn, *where):
        for way in range(2):
            turn(way, *where)

    def panel_turns(hop, first, last, turn):
        def one(t, carry):
            way, p = lax.rem(t, 2), t // 2
            zz = z + (2 * way - 1) * hop
            fits = jnp.logical_and(zz >= 0, zz < nb)
            fits = jnp.logical_and(fits, jnp.logical_or(hop > 0, way == 0))

            @pl.when(fits)
            def _():
                turn(zz * per + p)

            return carry

        lax.fori_loop(first * 2, last * 2, one, 0)

    def scores(hop, first, last, row_blocks):
        span = len(row_blocks) * RB
        low = row_blocks[0]

        def turn(col):
            panel = all_ref[pl.ds(pl.multiple_of(col * CB, CB), CB), :]
            if low == 0:
                wider = panel.astype(jnp.float32)
                offs = 0.5 * jnp.sum(wider * wider, axis=1, keepdims=True)
                if len(row_blocks) < local:
                    offs_ref[col] = offs
            else:
                offs = offs_ref[col]
            raw = lax.dot_general(
                panel,
                rows_ref[low * RB : low * RB + span, :],
                transposed,
                preferred_element_type=jnp.float32,
            )
            for r in row_blocks:
                part = raw[:, (r - low) * RB : (r - low + 1) * RB]
                value = jnp.where(
                    allow_ref[r, col] > 0, (part - offs) * scale, neg_big
                )
                score_ref[r, col] = value
                old = top_ref[r]
                top = jnp.maximum(old, jnp.max(value, axis=0, keepdims=True))
                sum_ref[r] = sum_ref[r] * jnp.exp(old - top) + jnp.sum(
                    jnp.exp(value - top), axis=0, keepdims=True
                )
                top_ref[r] = top

        panel_turns(hop, first, last, turn)

    first_pieces = PIECES // local
    row_copies = [[row_copy(d, piece) for d in range(1, nf)] for piece in range(PIECES)]
    for piece in range(first_pieces):
        for copy in row_copies[piece]:
            copy.start()
    for way in range(2):
        d = (way * nb + 1) * per
        mine = thin_spot(cen_ref, 0, c, x)
        go(onward(way), remote(mine, thin_spot(all_ref, z, c, x), 0, d, step(way), f))
    for p in range(per):
        for way in range(2):
            d = (way * nb + 1) * per + p
            mine = wide_spot(cen_ref, 0, p, c)
            go(onward(way), remote(mine, wide_spot(all_ref, z, p, c), 4, d, step(way), f))
    loads = [
        pltpu.make_async_copy(
            emb_ref.at[pl.ds(pl.multiple_of(f * rows, rows), rows), :],
            rows_ref.at[:, pl.ds(pl.multiple_of(f * width, width), width)],
            own_sem.at[0],
        ),
        pltpu.make_async_copy(
            cen_ref, all_ref.at[pl.ds(pl.multiple_of(z * per * CB, CB), per * CB), :], own_sem.at[1]
        ),
    ]
    for copy in loads:
        copy.start()
    top_ref[...] = jnp.full_like(top_ref, neg_big)
    sum_ref[...] = jnp.zeros_like(sum_ref)
    early = list(range(1))
    late = list(range(1, local))
    both(pass_thin, 1)
    for piece in range(first_pieces, PIECES):
        for copy in row_copies[piece]:
            copy.start()
    for copy in loads:
        copy.wait()
    for p in range(per):
        both(pass_wide, 1, p)
    both(pass_thin, 2)
    for piece in range(first_pieces):
        for copy in row_copies[piece]:
            copy.wait_recv()
    scores(0, 0, per, early)
    both(pass_across, 1)
    both(have_thin, 1)
    for p in range(per):
        both(have_wide, 1, p)
    scores(1, 0, per, early)
    for p in range(per):
        both(pass_wide, 2, p)
    for hop in range(3, nb):
        both(pass_thin, hop)
        for p in range(per):
            if hop < nb - 1 or p < per - 1:
                both(pass_wide, hop, p)
    for piece in range(first_pieces, PIECES):
        for copy in row_copies[piece]:
            copy.wait_recv()
    scores(0, 0, per, late)
    scores(1, 0, per, late)
    for hop in range(2, nb):
        both(pass_across, hop)
        both(have_thin, hop)
        for p in range(per):
            both(have_wide, hop, p)
            scores(hop, p, p + 1, early + late)
            if hop == nb - 2 and p == per - 2:
                both(pass_wide, nb - 1, per - 1)

    for r in range(local):
        norm = top_ref[r] + jnp.log(sum_ref[r])
        for j in range(RB // 128):
            norm_ref[r * (RB // 128) + j, :] = norm[0, j * 128 : (j + 1) * 128]
        top_ref[r] = norm

    lead = 0

    def cols(t):
        return pl.ds(pl.multiple_of(t * size, size), size)

    left, right = jnp.int32(0), jnp.int32(nb - 1)
    turns = []
    for _ in range(nb):
        pick = (z - left) >= (right - z)
        turns.append(jnp.where(pick, left, right))
        left, right = jnp.where(pick, left + 1, left), jnp.where(pick, right, right - 1)

    def a_copy(q, t):
        return pltpu.make_async_remote_copy(
            src_ref=to_sib.at[q, :, cols(t)],
            dst_ref=from_sib.at[q, :, cols(t)],
            send_sem=a_send.at[q, t],
            recv_sem=a_recv.at[q, t],
            device_id={"blk": z, "feat": sibling},
            device_id_type=MESH,
        )

    def b_copy(i, t):
        return pltpu.make_async_remote_copy(
            src_ref=to_x.at[i, :, cols(t)],
            dst_ref=from_x.at[i, :, cols(t)],
            send_sem=b_send.at[i, t],
            recv_sem=b_recv.at[i, t],
            device_id={"blk": z, "feat": (1 - x) * 2 + c},
            device_id_type=MESH,
        )

    def z_copy(zz, way, t):
        return pltpu.make_async_remote_copy(
            src_ref=to_z.at[zz, :, cols(t)],
            dst_ref=from_z.at[way, zz, :, cols(t)],
            send_sem=z_send.at[zz, t],
            recv_sem=z_recv.at[way, zz, t],
            device_id={"blk": jnp.clip(z + 1 - 2 * way, 0, nb - 1), "feat": f},
            device_id_type=MESH,
        )

    def line_copy(d):
        zz = lax.rem(z + d, nb)
        return pltpu.make_async_remote_copy(
            src_ref=to_line.at[zz],
            dst_ref=from_line.at[d - 1],
            send_sem=line_send.at[d],
            recv_sem=line_recv.at[d],
            device_id={"blk": zz, "feat": f},
            device_id_type=MESH,
        )

    def swap_copy():
        return pltpu.make_async_remote_copy(
            src_ref=swap_out,
            dst_ref=swap_in,
            send_sem=swap_sem.at[0],
            recv_sem=swap_sem.at[1],
            device_id={"blk": z, "feat": (1 - x) * 2 + c},
            device_id_type=MESH,
        )

    def m_copy(d):
        return pltpu.make_async_remote_copy(
            src_ref=to_mass.at[lax.rem(me + d, n)],
            dst_ref=from_mass.at[d],
            send_sem=m_send.at[d],
            recv_sem=m_recv.at[d],
            device_id=at_offset(d),
            device_id_type=MESH,
        )

    def wide_of(value):
        return value.astype(jnp.float32)

    def place(i):
        zz = turns[nb - 1]
        for t in range(nb - 1):
            zz = jnp.where(i == t, turns[t], zz)
        return zz

    group = CHUNKS // SPANS

    def weights(i, side):
        zz = place(i)
        xx = 1 - x if side == 0 else x
        col = zz * per + xx
        for cc in range(2):
            at = c if cc == 0 else 1 - c
            first = side * CB + cc * own
            for r in range(local):
                value = score_ref[r, col, pl.ds(pl.multiple_of(at * own, own), own), :]
                weight_ref[first : first + own, r * RB : (r + 1) * RB] = jnp.exp(
                    value - top_ref[r]
                ).astype(jnp.bfloat16)

    def masses(i, side):
        zz = place(i)
        xx = 1 - x if side == 0 else x
        part = slice(side * CB, (side + 1) * CB)
        mass = lax.dot_general(
            jnp.ones((8, rows), jnp.bfloat16),
            weight_ref[part, :],
            transposed,
            preferred_element_type=jnp.float32,
        )
        to_mass[zz * nf + xx * 2 + c] = mass[:, :own]
        to_mass[zz * nf + xx * 2 + 1 - c] = mass[:, own:]

    def sums(i):
        for side in range(2):
            weights(i, side)

        def span(u, carry):
            @pl.when(u < SPANS)
            def _():
                at = pl.ds(pl.multiple_of(u * group * size, group * size), group * size)
                total = jnp.dot(
                    weight_ref[...], rows_ref[:, at], preferred_element_type=jnp.float32
                )
                for side in range(2):
                    first = side * CB
                    keep_ref[side * nb + i, :, at] = total[first : first + own]
                    to_sib[side * nb + i, :, at] = total[first + own : first + CB].astype(jnp.bfloat16)
                for side in range(2):
                    for t in range(group):
                        a_copy(side * nb + i, u * group + t).start()

            @pl.when(u > 1)
            def _():
                for t in range(group):
                    at = (u - 2) * group + t
                    pl.when(at > lead)(functools.partial(send_x, i, at))

            @pl.when(u == 2)
            def _():
                send_line(i)

            return carry

        lax.fori_loop(0, SPANS + 2, span, 0)
        for side in range(2):
            masses(i, side)

    def send_x(i, t):
        a_copy(i, t).wait()
        to_x[i, :, cols(t)] = (
            keep_ref[i, :, cols(t)] + wide_of(from_sib[i, :, cols(t)])
        ).astype(jnp.bfloat16)
        b_copy(i, t).start()

    def course(i):
        zz = place(i)
        fed = jnp.logical_or(
            jnp.logical_and(zz > z, z > 0), jnp.logical_and(zz < z, z < nb - 1)
        )
        return zz, (zz < z).astype(jnp.int32), fed

    def send_line(i):
        zz = place(i)
        for side in range(2):
            q = side * nb + i
            a_copy(q, lead).wait()
            sides_ref[side] = keep_ref[q, :, cols(lead)] + wide_of(from_sib[q, :, cols(lead)])

        @pl.when(zz != z)
        def _():
            to_line[zz] = sides_ref[...].astype(jnp.bfloat16)
            line_copy(lax.rem(zz - z + nb, nb)).start()

    def swap():
        def one(d, carry):
            line_copy(d).wait()
            sides_ref[...] += wide_of(from_line[d - 1])
            return carry

        lax.fori_loop(1, nb, one, 0)
        swap_out[...] = sides_ref[0].astype(jnp.bfloat16)
        swap_copy().start()

    def mass_end(d, total):
        m_copy(d).wait()
        return total + from_mass[d]

    def masses_in():
        mass = lax.fori_loop(1, n, mass_end, to_mass[me])[:1]
        spread = jnp.broadcast_to(mass, (own, own))
        diagonal = lax.broadcasted_iota(jnp.int32, (own, own), 0) == lax.broadcasted_iota(
            jnp.int32, (own, own), 1
        )
        inverse_ref[...] = 1.0 / (
            jnp.sum(jnp.where(diagonal, spread, 0.0), axis=1, keepdims=True) + prior_mass
        )

    def finish(t, total):
        old = all_ref[pl.ds(pl.multiple_of(me * own, own), own), cols(t)]
        num_ref[:, cols(t)] = (total + prior_mass * wide_of(old)) * inverse_ref[...]

    def send_z(i):
        zz, way, fed = course(i)
        q = nb + i

        def chunk(t, carry):
            a_copy(q, t).wait()
            b_copy(i, t).wait()
            part_ref[...] = (
                keep_ref[q, :, cols(t)]
                + wide_of(from_sib[q, :, cols(t)])
                + wide_of(from_x[i, :, cols(t)])
            )

            @pl.when(fed)
            def _():
                z_copy(zz, way, t).wait_recv()
                part_ref[...] += wide_of(from_z[way, zz, :, cols(t)])

            @pl.when(zz != z)
            def _():
                to_z[zz, :, cols(t)] = part_ref[...].astype(jnp.bfloat16)
                z_copy(zz, way, t).start()

            @pl.when(zz == z)
            def _():
                for back in range(2):

                    @pl.when((z > 0) if back == 0 else (z < nb - 1))
                    def _():
                        z_copy(z, back, t).wait_recv()
                        part_ref[...] += wide_of(from_z[back, z, :, cols(t)])

                finish(t, part_ref[...])

            return carry

        lax.fori_loop(lead + 1, CHUNKS, chunk, 0)

    def turn(i, carry):
        @pl.when(i < nb)
        def _():
            sums(i)

        @pl.when(i == nb - 1)
        def _():
            def mass_start(d, carry):
                m_copy(d).start()
                return carry

            lax.fori_loop(1, n, mass_start, 0)

        pl.when(i == nb + 1)(swap)
        pl.when(i == nb + 1)(masses_in)

        @pl.when(i > 1)
        def _():
            send_z(i - 2)

        return carry

    lax.fori_loop(0, nb + 2, turn, 0)

    def last(t, carry):
        for zz in range(nb):

            @pl.when(z != zz)
            def _():
                z_copy(zz, 0, t).wait_send()

        return carry

    lax.fori_loop(lead + 1, CHUNKS, last, 0)
    swap_copy().wait()
    finish(lead, sides_ref[1] + wide_of(swap_in[...]))
    for group in row_copies:
        for copy in group:
            copy.wait_send()
    for cond, copy in started:
        pl.when(cond)(copy.wait_send)


def fused(allow, embeddings, centroids, nb, nf):
    rows = embeddings.shape[0] // nf
    local = rows // RB
    n = nb * nf
    own = K // n
    per = K // nb // CB
    kinds = 6
    vmem = pl.BlockSpec(memory_space=pltpu.VMEM)
    hbm = pl.BlockSpec(memory_space=pltpu.HBM)
    dma = pltpu.SemaphoreType.DMA
    bf16, f32 = jnp.bfloat16, jnp.float32
    return pl.pallas_call(
        functools.partial(fused_kernel, nb, nf),
        out_shape=(
            jax.ShapeDtypeStruct((own, D), f32),
            jax.ShapeDtypeStruct((rows // 128, 128), f32),
        ),
        in_specs=[pl.BlockSpec(memory_space=pltpu.SMEM), hbm, hbm],
        out_specs=(vmem,) * 2,
        scratch_shapes=[
            pltpu.VMEM((rows, D), bf16),
            pltpu.VMEM((K, D), bf16),
            pltpu.VMEM((NCB, CB, 1), f32),
            pltpu.VMEM((local, NCB, CB, RB), f32),
            pltpu.VMEM((local, 1, RB), f32),
            pltpu.VMEM((local, 1, RB), f32),
            pltpu.VMEM((2 * CB, rows), bf16),
            pltpu.VMEM((2 * nb, own, D), f32),
            pltpu.VMEM((2 * nb, own, D), bf16),
            pltpu.VMEM((2 * nb, own, D), bf16),
            pltpu.VMEM((nb, own, D), bf16),
            pltpu.VMEM((nb, own, D), bf16),
            pltpu.VMEM((own, D // CHUNKS), f32),
            pltpu.VMEM((nb, own, D), bf16),
            pltpu.VMEM((2, nb, own, D), bf16),
            pltpu.VMEM((2, own, D // CHUNKS), f32),
            pltpu.VMEM((nb, 2, own, D // CHUNKS), bf16),
            pltpu.VMEM((nb - 1, 2, own, D // CHUNKS), bf16),
            pltpu.VMEM((own, D // CHUNKS), bf16),
            pltpu.VMEM((own, D // CHUNKS), bf16),
            pltpu.VMEM((n, 8, own), f32),
            pltpu.VMEM((n, 8, own), f32),
            pltpu.VMEM((own, 1), f32),
            dma((nf, PIECES)),
            dma((nf, PIECES)),
            dma((kinds, 2 * nb * per)),
            dma((kinds, 2 * nb * per)),
            dma((2,)),
            dma((2 * nb, CHUNKS)),
            dma((2 * nb, CHUNKS)),
            dma((nb, CHUNKS)),
            dma((nb, CHUNKS)),
            dma((nb, CHUNKS)),
            dma((2, nb, CHUNKS)),
            dma((n,)),
            dma((n,)),
            dma((nb,)),
            dma((nb,)),
            dma((2,)),
        ],
        compiler_params=pltpu.CompilerParams(
            collective_id=2, has_side_effects=True, vmem_limit_bytes=58 * 2**20
        ),
        name="fused",
    )(allow, embeddings, centroids)


def body(embeddings, centroids, pair_list):
    nb, nf = lax.axis_size("blk"), lax.axis_size("feat")
    local_rows = embeddings.shape[0] // nf
    local_blocks = local_rows // RB
    device_index = lax.axis_index("blk") * nf + lax.axis_index("feat")
    mine = device_index * local_blocks + jnp.arange(local_blocks, dtype=jnp.int32)
    row_ids, col_ids = pair_list[:, 0], pair_list[:, 1]
    same = row_ids[None, :] == mine[:, None]
    if K // nb == 2 * CB and nf == 4 and local_blocks == 2:
        blocks = jnp.arange(NCB, dtype=jnp.int32)
        listed = same[:, None, :] & (col_ids[None, None, :] == blocks[None, :, None])
        allow = jnp.sum(listed.astype(jnp.int32), axis=2)
        new_centroids, log_norm = fused(allow, embeddings, centroids, nb, nf)
        return (new_centroids, log_norm.reshape(local_rows))
    before = jnp.sum((row_ids[None, :] < mine[:, None]).astype(jnp.int32), axis=1)
    counts = jnp.sum(same.astype(jnp.int32), axis=1)
    rank = jnp.arange(row_ids.shape[0], dtype=jnp.int32)[None, :] - before[:, None]
    slots = jnp.arange(SLOTS, dtype=jnp.int32)
    picked = same[:, None, :] & (rank[:, None, :] == slots[None, :, None])
    chosen = jnp.sum(jnp.where(picked, col_ids[None, None, :], 0), axis=2)
    table = jnp.concatenate([counts[:, None], chosen], axis=1)

    row_data, panels = fetch(embeddings, centroids, nb, nf)
    num, mass, log_norm = terms(table, row_data, panels, nb, nf)
    numerator, denominator = reduce_sums(num, mass, nb, nf)

    own_count = centroids.shape[0] // nf
    own_rows = lax.dynamic_slice_in_dim(
        centroids, lax.axis_index("feat") * own_count, own_count, 0
    ).astype(jnp.float32)
    new_centroids = (numerator + prior_mass * own_rows) / (denominator[0][:, None] + prior_mass)
    return (new_centroids, log_norm.reshape(local_rows))


def solution(mesh):
    return jax.shard_map(
        body,
        mesh=mesh,
        in_specs=(P(("groups", "blk"), "feat"), P(("groups", "blk"), None), P("groups", None)),
        out_specs=(P(("groups", "blk", "feat"), None), P(("groups", "blk", "feat"))),
        check_vma=False,
    )
```

```python
import functools
import math

import jax
import jax.numpy as jnp
from jax import lax
from jax.experimental import pallas as pl
from jax.experimental.pallas import tpu as pltpu
from jax.sharding import PartitionSpec as P

D = 2048
K = 2048
RB = 512
CB = 256
NCB = K // CB
SLOTS = 4
PARTS = 8
PIECES = 2
CHUNKS = 8
SPANS = 4

neg_big = -1e30
prior_mass = 16.0
MESH = pl.DeviceIdType.MESH


def meet(peers):
    barrier = pltpu.get_barrier_semaphore()
    for peer in peers:
        pl.semaphore_signal(barrier, inc=1, device_id=peer, device_id_type=MESH)
    pl.semaphore_wait(barrier, len(peers))


def fetch_kernel(
    nb, nf, emb_ref, cen_ref, rows_ref, all_ref, row_send, row_recv, send, recv, own_sem,
    emb_hold, cen_hold,
):
    z = lax.axis_index("blk")
    f = lax.axis_index("feat")
    nx = nf // 2
    c = lax.rem(f, 2)
    x = f // 2
    rows, width = rows_ref.shape[0], emb_ref.shape[1]
    half = cen_ref.shape[0] // 2
    thin = D * 3 // 8 // nx // 128 * 128
    wide = D - nx * thin
    sibling = x * 2 + 1 - c

    def across(dx):
        return lax.rem(x + dx, nx)

    meet(
        [{"blk": z, "feat": lax.rem(f + d, nf)} for d in range(1, nf)]
        + [{"blk": lax.rem(z + d, nb), "feat": f} for d in range(1, nb)]
    )

    def spot(zz, cc, col, size):
        return all_ref.at[
            pl.ds(pl.multiple_of(zz * 2 * half + cc * half, half), half),
            pl.ds(pl.multiple_of(col, 128), size),
        ]

    def remote(src, dst, kind, d, blk, feat):
        return pltpu.make_async_remote_copy(
            src_ref=src,
            dst_ref=dst,
            send_sem=send.at[kind, d],
            recv_sem=recv.at[kind, d],
            device_id={"blk": blk, "feat": feat},
            device_id_type=MESH,
        )

    def own_part(col, size):
        return cen_ref.at[
            pl.ds(pl.multiple_of(c * half, half), half), pl.ds(pl.multiple_of(col, 128), size)
        ]

    thin_col = wide + x * thin
    started = []

    def go(cond, copy):
        pl.when(cond)(copy.start)
        started.append((cond, copy))

    def row_copy(d, piece):
        to = lax.rem(f + d, nf)
        size = rows // PIECES
        return pltpu.make_async_remote_copy(
            src_ref=emb_ref.at[pl.ds(pl.multiple_of(to * rows + piece * size, size), size), :],
            dst_ref=rows_ref.at[
                pl.ds(piece * size, size), pl.ds(pl.multiple_of(f * width, width), width)
            ],
            send_sem=row_send.at[d, piece],
            recv_sem=row_recv.at[d, piece],
            device_id={"blk": z, "feat": to},
            device_id_type=MESH,
        )

    def step(way):
        return jnp.clip(z + 1 - 2 * way, 0, nb - 1)

    def onward(way):
        return (z + 1 < nb) if way == 0 else (z > 0)

    for way in range(2):
        go(
            onward(way),
            remote(own_part(thin_col, thin), spot(z, c, thin_col, thin), 1, way * nb + 1, step(way), f),
        )
    for way in range(2):
        go(onward(way), remote(own_part(0, wide), spot(z, c, 0, wide), 0, way * nb + 1, step(way), f))
    row_copies = [row_copy(d, piece) for piece in range(PIECES) for d in range(1, nf)]
    for copy in row_copies:
        copy.start()
    holds = [
        (
            emb_ref.at[pl.ds(pl.multiple_of(f * rows, rows), rows), :],
            emb_hold,
            rows_ref.at[:, pl.ds(pl.multiple_of(f * width, width), width)],
        ),
        (
            cen_ref,
            cen_hold,
            all_ref.at[pl.ds(pl.multiple_of(z * 2 * half, half), 2 * half), :],
        ),
    ]
    loads = [pltpu.make_async_copy(src, hold, own_sem.at[i]) for i, (src, hold, _) in enumerate(holds)]
    stores = [
        pltpu.make_async_copy(hold, dst, own_sem.at[2 + i]) for i, (_, hold, dst) in enumerate(holds)
    ]
    for copy in loads:
        copy.start()
    for load, store in zip(loads, stores):
        load.wait()
        store.start()

    def source(way, hop):
        zz = z - hop if way == 0 else z + hop
        return (zz >= 0) if way == 0 else (zz < nb), jnp.clip(zz, 0, nb - 1)

    def arrived(cond, kind, d, zz, cc, col, size):
        here = spot(zz, cc, col, size)
        pl.when(cond)(remote(here, here, kind, d, z, sibling).wait_recv)
        return here

    turns = [(way, hop) for hop in range(1, nb) for way in range(2)]

    def pass_thin(way, hop):
        cond, zz = source(way, hop)
        d = way * nb + hop
        here = arrived(cond, 1, d, zz, c, thin_col, thin)
        if hop + 1 < nb:
            go(jnp.logical_and(cond, onward(way)), remote(here, here, 1, d + 1, step(way), f))
        for dx in range(1, nx):
            go(cond, remote(here, here, 4 + dx, d, z, across(dx) * 2 + c))
        go(cond, remote(here, here, 3, d, z, sibling))

    def pass_wide(way, hop):
        cond, zz = source(way, hop)
        d = way * nb + hop
        here = arrived(cond, 0, d, zz, c, 0, wide)
        if hop + 1 < nb:
            go(jnp.logical_and(cond, onward(way)), remote(here, here, 0, d + 1, step(way), f))
        go(cond, remote(here, here, 2, d, z, sibling))

    def pass_across(way, hop):
        cond, zz = source(way, hop)
        d = way * nb + hop
        for dx in range(1, nx):
            col = wide + lax.rem(x + nx - dx, nx) * thin
            here = arrived(cond, 4 + dx, d, zz, c, col, thin)
            go(cond, remote(here, here, 4 + nx + dx, d, z, sibling))

    for hop in range(1, nb):
        for way in range(2):
            pass_thin(way, hop)
        for way in range(2):
            pass_wide(way, hop)
    for way, hop in turns:
        pass_across(way, hop)
    for way, hop in turns:
        cond, zz = source(way, hop)
        d = way * nb + hop
        arrived(cond, 2, d, zz, 1 - c, 0, wide)
        arrived(cond, 3, d, zz, 1 - c, thin_col, thin)
        for dx in range(1, nx):
            col = wide + lax.rem(x + nx - dx, nx) * thin
            arrived(cond, 4 + nx + dx, d, zz, 1 - c, col, thin)
    for copy in stores:
        copy.wait()
    for copy in row_copies:
        copy.wait()
    for cond, copy in started:
        pl.when(cond)(copy.wait_send)


def fetch(embeddings, centroids, nb, nf):
    rows = embeddings.shape[0] // nf
    kinds = 4 + 2 * (nf // 2) + 1
    return pl.pallas_call(
        functools.partial(fetch_kernel, nb, nf),
        out_shape=(
            jax.ShapeDtypeStruct((rows, D), jnp.bfloat16),
            jax.ShapeDtypeStruct((K, D), jnp.bfloat16),
        ),
        in_specs=[pl.BlockSpec(memory_space=pltpu.HBM)] * 2,
        out_specs=(pl.BlockSpec(memory_space=pl.ANY),) * 2,
        scratch_shapes=[
            pltpu.SemaphoreType.DMA((nf, PIECES)),
            pltpu.SemaphoreType.DMA((nf, PIECES)),
            pltpu.SemaphoreType.DMA((kinds, 2 * nb)),
            pltpu.SemaphoreType.DMA((kinds, 2 * nb)),
            pltpu.SemaphoreType.DMA((4,)),
            pltpu.VMEM((rows, D // nf), jnp.bfloat16),
            pltpu.VMEM((K // nb, D), jnp.bfloat16),
        ],
        compiler_params=pltpu.CompilerParams(
            collective_id=0, has_side_effects=True, vmem_limit_bytes=6 * 2**20
        ),
        name="fetch",
    )(embeddings, centroids)


def term_kernel(nb, nf, tab_ref, rows_ref, all_ref, num_ref, mass_ref, norm_ref, score_ref, weight_ref, acc_ref, row_mass):
    local = rows_ref.shape[0] // RB
    scale = 1.0 / math.sqrt(D)
    own = K // (nb * nf)
    nx = nf // 2
    transposed = (((1,), (1,)), ((), ()))

    for r in range(local):
        part = rows_ref[r * RB : (r + 1) * RB, :]
        count = tab_ref[r, 0]

        def score_turn(slot, top):
            col = tab_ref[r, 1 + slot]
            panel = all_ref[pl.ds(pl.multiple_of(col * CB, CB), CB), :]
            wide = panel.astype(jnp.float32)
            offs = 0.5 * jnp.sum(wide * wide, axis=1, keepdims=True)
            raw = lax.dot_general(panel, part, transposed, preferred_element_type=jnp.float32)
            scores = (raw - offs) * scale
            score_ref[slot] = scores
            return jnp.maximum(top, jnp.max(scores, axis=0, keepdims=True))

        top = lax.fori_loop(0, count, score_turn, jnp.full((1, RB), neg_big, jnp.float32))

        def sum_turn(slot, total):
            return total + jnp.sum(jnp.exp(score_ref[slot] - top), axis=0, keepdims=True)

        total = lax.fori_loop(0, count, sum_turn, jnp.zeros((1, RB), jnp.float32))
        norm = top + jnp.log(total)
        norm_ref[r] = norm

        def weight_turn(slot, carry):
            col = tab_ref[r, 1 + slot]
            weight_ref[r, col] = jnp.exp(score_ref[slot] - norm).astype(jnp.bfloat16)
            return carry

        lax.fori_loop(0, count, weight_turn, 0)

    def col_turn(col, carry):
        acc_ref[...] = jnp.zeros_like(acc_ref)
        row_mass[...] = jnp.zeros_like(row_mass)
        for r in range(local):
            hit = jnp.int32(0)
            for slot in range(SLOTS):
                found = jnp.logical_and(tab_ref[r, 1 + slot] == col, slot < tab_ref[r, 0])
                hit = hit + found.astype(jnp.int32)

            @pl.when(hit > 0)
            def _():
                weights = weight_ref[r, col]
                acc_ref[...] += jnp.dot(
                    weights, rows_ref[r * RB : (r + 1) * RB, :], preferred_element_type=jnp.float32
                )
                row_mass[...] += lax.dot_general(
                    jnp.ones((8, RB), jnp.bfloat16),
                    weights,
                    transposed,
                    preferred_element_type=jnp.float32,
                )

        for j in range(CB // own):
            owner = col * (CB // own) + j
            zz, ff = owner // nf, lax.rem(owner, nf)
            num_ref[lax.rem(ff, 2), ff // 2, zz] = acc_ref[j * own : (j + 1) * own, :].astype(
                jnp.bfloat16
            )
            mass_ref[owner] = row_mass[:, j * own : (j + 1) * own]
        return carry

    lax.fori_loop(0, NCB, col_turn, 0)


def terms(table, row_data, panels, nb, nf):
    local = row_data.shape[0] // RB
    own = K // (nb * nf)
    vmem = pl.BlockSpec(memory_space=pltpu.VMEM)
    return pl.pallas_call(
        functools.partial(term_kernel, nb, nf),
        out_shape=(
            jax.ShapeDtypeStruct((2, nf // 2, nb, own, D), jnp.bfloat16),
            jax.ShapeDtypeStruct((nb * nf, 8, own), jnp.float32),
            jax.ShapeDtypeStruct((local, 1, RB), jnp.float32),
        ),
        in_specs=[pl.BlockSpec(memory_space=pltpu.SMEM), vmem, vmem],
        out_specs=(vmem,) * 3,
        scratch_shapes=[
            pltpu.VMEM((SLOTS, CB, RB), jnp.float32),
            pltpu.VMEM((local, NCB, CB, RB), jnp.bfloat16),
            pltpu.VMEM((CB, D), jnp.float32),
            pltpu.VMEM((8, CB), jnp.float32),
        ],
        compiler_params=pltpu.CompilerParams(vmem_limit_bytes=32 * 2**20),
        name="terms",
    )(table, row_data, panels)


def reduce_kernel(
    nb, nf, num_ref, mass_ref, out_ref, out_mass,
    from_sib, to_x, from_x, to_z, from_z, from_mass,
    a_send, a_recv, b_send, b_recv, c_send, c_recv, m_send, m_recv,
):
    z = lax.axis_index("blk")
    f = lax.axis_index("feat")
    nx = nf // 2
    n = nb * nf
    me = z * nf + f
    c = lax.rem(f, 2)
    x = f // 2
    sibling = x * 2 + 1 - c
    size = D // PARTS

    def at_offset(d):
        other = lax.rem(me + d, n)
        return {"blk": other // nf, "feat": lax.rem(other, nf)}

    barrier = pltpu.get_barrier_semaphore()

    def greet(d, carry):
        pl.semaphore_signal(barrier, inc=1, device_id=at_offset(d), device_id_type=MESH)
        return carry

    lax.fori_loop(1, n, greet, 0)
    pl.semaphore_wait(barrier, n - 1)

    def cols(t):
        return pl.ds(t * size, size)

    def a_copy(dx, t):
        xx = lax.rem(x + dx, nx)
        return pltpu.make_async_remote_copy(
            src_ref=num_ref.at[1 - c, xx, :, :, cols(t)],
            dst_ref=from_sib.at[xx, :, :, cols(t)],
            send_sem=a_send.at[dx, t],
            recv_sem=a_recv.at[dx, t],
            device_id={"blk": z, "feat": sibling},
            device_id_type=MESH,
        )

    def b_copy(dx, t):
        return pltpu.make_async_remote_copy(
            src_ref=to_x.at[dx - 1, :, :, cols(t)],
            dst_ref=from_x.at[dx - 1, :, :, cols(t)],
            send_sem=b_send.at[dx, t],
            recv_sem=b_recv.at[dx, t],
            device_id={"blk": z, "feat": lax.rem(x + dx, nx) * 2 + c},
            device_id_type=MESH,
        )

    def c_copy(d, t):
        return pltpu.make_async_remote_copy(
            src_ref=to_z.at[d - 1, :, cols(t)],
            dst_ref=from_z.at[d - 1, :, cols(t)],
            send_sem=c_send.at[d, t],
            recv_sem=c_recv.at[d, t],
            device_id={"blk": lax.rem(z + d, nb), "feat": f},
            device_id_type=MESH,
        )

    def m_copy(d):
        return pltpu.make_async_remote_copy(
            src_ref=mass_ref.at[lax.rem(me + d, n)],
            dst_ref=from_mass.at[d],
            send_sem=m_send.at[d],
            recv_sem=m_recv.at[d],
            device_id=at_offset(d),
            device_id_type=MESH,
        )

    def wide(value):
        return value.astype(jnp.float32)

    for t in range(PARTS):
        for dx in range(1, nx):
            a_copy(dx, t).start()
    for t in range(PARTS):
        a_copy(0, t).start()

    def mass_start(d, carry):
        m_copy(d).start()
        return carry

    lax.fori_loop(1, n, mass_start, 0)

    for t in range(PARTS):
        for dx in range(1, nx):
            xx = lax.rem(x + dx, nx)
            a_copy(dx, t).wait()
            for zz in range(nb):
                to_x[dx - 1, zz, :, cols(t)] = (
                    wide(num_ref[c, xx, zz, :, cols(t)]) + wide(from_sib[xx, zz, :, cols(t)])
                ).astype(jnp.bfloat16)
            b_copy(dx, t).start()

    def blk_sum(zz, t):
        total = wide(num_ref[c, x, zz, :, cols(t)]) + wide(from_sib[x, zz, :, cols(t)])
        for dx in range(1, nx):
            total = total + wide(from_x[dx - 1, zz, :, cols(t)])
        return total

    for t in range(PARTS):
        a_copy(0, t).wait()
        for dx in range(1, nx):
            b_copy(dx, t).wait()
        for d in range(1, nb):
            to_z[d - 1, :, cols(t)] = blk_sum(lax.rem(z + d, nb), t).astype(jnp.bfloat16)
            c_copy(d, t).start()
        out_ref[:, cols(t)] = blk_sum(z, t)

    def mass_end(d, total):
        m_copy(d).wait()
        return total + from_mass[d]

    out_mass[...] = lax.fori_loop(1, n, mass_end, mass_ref[me])

    for t in range(PARTS):
        total = out_ref[:, cols(t)]
        for d in range(1, nb):
            c_copy(d, t).wait()
            total = total + wide(from_z[d - 1, :, cols(t)])
        out_ref[:, cols(t)] = total


def reduce_sums(num, mass, nb, nf):
    own = K // (nb * nf)
    nx = nf // 2
    n = nb * nf
    vmem = pl.BlockSpec(memory_space=pltpu.VMEM)
    dma = pltpu.SemaphoreType.DMA
    return pl.pallas_call(
        functools.partial(reduce_kernel, nb, nf),
        out_shape=(
            jax.ShapeDtypeStruct((own, D), jnp.float32),
            jax.ShapeDtypeStruct((8, own), jnp.float32),
        ),
        in_specs=[vmem] * 2,
        out_specs=(vmem,) * 2,
        scratch_shapes=[
            pltpu.VMEM((nx, nb, own, D), jnp.bfloat16),
            pltpu.VMEM((nx - 1, nb, own, D), jnp.bfloat16),
            pltpu.VMEM((nx - 1, nb, own, D), jnp.bfloat16),
            pltpu.VMEM((nb - 1, own, D), jnp.bfloat16),
            pltpu.VMEM((nb - 1, own, D), jnp.bfloat16),
            pltpu.VMEM((n, 8, own), jnp.float32),
        ]
        + [dma((nx, PARTS))] * 4
        + [dma((nb, PARTS))] * 2
        + [dma((n,))] * 2,
        compiler_params=pltpu.CompilerParams(
            collective_id=1, has_side_effects=True, vmem_limit_bytes=24 * 2**20
        ),
        name="reduce_sums",
    )(num, mass)


def fused_kernel(
    nb, nf, allow_ref, emb_ref, cen_ref, num_ref, norm_ref,
    rows_ref, all_ref, offs_ref, score_ref, top_ref, sum_ref, weight_ref, keep_ref,
    to_sib, from_sib, to_x, from_x, part_ref, to_z, from_z, sides_ref, to_line, from_line,
    swap_out, swap_in, to_mass, from_mass, inverse_ref,
    row_send, row_recv, send, recv, own_sem, a_send, a_recv, b_send, b_recv, z_send, z_recv,
    m_send, m_recv, line_send, line_recv, swap_sem,
):
    z = lax.axis_index("blk")
    f = lax.axis_index("feat")
    n = nb * nf
    me = z * nf + f
    c = lax.rem(f, 2)
    x = f // 2
    rows, width = rows_ref.shape[0], emb_ref.shape[1]
    local = rows // RB
    per = K // nb // CB
    half = CB // 2
    own = K // n
    thin = D * 3 // 16
    wide = D - 2 * thin
    sibling = x * 2 + 1 - c
    size = D // CHUNKS
    scale = 1.0 / math.sqrt(D)
    transposed = (((1,), (1,)), ((), ()))

    def at_offset(d):
        other = lax.rem(me + d, n)
        return {"blk": other // nf, "feat": lax.rem(other, nf)}

    barrier = pltpu.get_barrier_semaphore()

    def greet(d, carry):
        pl.semaphore_signal(barrier, inc=1, device_id=at_offset(d), device_id_type=MESH)
        return carry

    lax.fori_loop(1, n, greet, 0)
    pl.semaphore_wait(barrier, n - 1)

    def wide_spot(ref, block, p, cc):
        first = (block * per + p) * CB + cc * half
        return ref.at[pl.ds(pl.multiple_of(first, half), half), pl.ds(0, wide)]

    def thin_spot(ref, block, cc, xx):
        count = per * half
        return ref.at[
            pl.ds(pl.multiple_of((block * 2 + cc) * count, count), count),
            pl.ds(pl.multiple_of(wide + xx * thin, 128), thin),
        ]

    def remote(src, dst, kind, d, blk, feat):
        return pltpu.make_async_remote_copy(
            src_ref=src,
            dst_ref=dst,
            send_sem=send.at[kind, d],
            recv_sem=recv.at[kind, d],
            device_id={"blk": blk, "feat": feat},
            device_id_type=MESH,
        )

    started = []

    def go(cond, copy):
        pl.when(cond)(copy.start)
        started.append((cond, copy))

    piece_rows = rows // PIECES

    def row_copy(d, piece):
        to = lax.rem(f + d, nf)
        return pltpu.make_async_remote_copy(
            src_ref=emb_ref.at[
                pl.ds(pl.multiple_of(to * rows + piece * piece_rows, piece_rows), piece_rows), :
            ],
            dst_ref=rows_ref.at[
                pl.ds(piece * piece_rows, piece_rows),
                pl.ds(pl.multiple_of(f * width, width), width),
            ],
            send_sem=row_send.at[d, piece],
            recv_sem=row_recv.at[d, piece],
            device_id={"blk": z, "feat": to},
            device_id_type=MESH,
        )

    def step(way):
        return jnp.clip(z + 1 - 2 * way, 0, nb - 1)

    def onward(way):
        return (z + 1 < nb) if way == 0 else (z > 0)

    def source(way, hop):
        zz = z - hop if way == 0 else z + hop
        return (zz >= 0) if way == 0 else (zz < nb), jnp.clip(zz, 0, nb - 1)

    def arrived(cond, kind, d, here):
        pl.when(cond)(remote(here, here, kind, d, z, sibling).wait_recv)
        return here

    def pass_thin(way, hop):
        cond, zz = source(way, hop)
        d = (way * nb + hop) * per
        here = arrived(cond, 0, d, thin_spot(all_ref, zz, c, x))
        if hop + 1 < nb:
            go(jnp.logical_and(cond, onward(way)), remote(here, here, 0, d + per, step(way), f))
        go(cond, remote(here, here, 1, d, z, (1 - x) * 2 + c))
        go(cond, remote(here, here, 2, d, z, sibling))

    def pass_wide(way, hop, p):
        cond, zz = source(way, hop)
        d = (way * nb + hop) * per + p
        here = arrived(cond, 4, d, wide_spot(all_ref, zz, p, c))
        if hop + 1 < nb:
            go(jnp.logical_and(cond, onward(way)), remote(here, here, 4, d + per, step(way), f))
        go(cond, remote(here, here, 5, d, z, sibling))

    def pass_across(way, hop):
        cond, zz = source(way, hop)
        d = (way * nb + hop) * per
        here = arrived(cond, 1, d, thin_spot(all_ref, zz, c, 1 - x))
        go(cond, remote(here, here, 3, d, z, sibling))

    def have_thin(way, hop):
        cond, zz = source(way, hop)
        d = (way * nb + hop) * per
        arrived(cond, 2, d, thin_spot(all_ref, zz, 1 - c, x))
        arrived(cond, 3, d, thin_spot(all_ref, zz, 1 - c, 1 - x))

    def have_wide(way, hop, p):
        cond, zz = source(way, hop)
        arrived(cond, 5, (way * nb + hop) * per + p, wide_spot(all_ref, zz, p, 1 - c))

    def both(turn, *where):
        for way in range(2):
            turn(way, *where)

    def panel_turns(hop, first, last, turn):
        def one(t, carry):
            way, p = lax.rem(t, 2), t // 2
            zz = z + (2 * way - 1) * hop
            fits = jnp.logical_and(zz >= 0, zz < nb)
            fits = jnp.logical_and(fits, jnp.logical_or(hop > 0, way == 0))

            @pl.when(fits)
            def _():
                turn(zz * per + p)

            return carry

        lax.fori_loop(first * 2, last * 2, one, 0)

    def scores(hop, first, last, row_blocks):
        span = len(row_blocks) * RB
        low = row_blocks[0]

        def turn(col):
            panel = all_ref[pl.ds(pl.multiple_of(col * CB, CB), CB), :]
            if low == 0:
                wider = panel.astype(jnp.float32)
                offs = 0.5 * jnp.sum(wider * wider, axis=1, keepdims=True)
                if len(row_blocks) < local:
                    offs_ref[col] = offs
            else:
                offs = offs_ref[col]
            raw = lax.dot_general(
                panel,
                rows_ref[low * RB : low * RB + span, :],
                transposed,
                preferred_element_type=jnp.float32,
            )
            for r in row_blocks:
                part = raw[:, (r - low) * RB : (r - low + 1) * RB]
                value = jnp.where(
                    allow_ref[r, col] > 0, (part - offs) * scale, neg_big
                )
                score_ref[r, col] = value
                old = top_ref[r]
                top = jnp.maximum(old, jnp.max(value, axis=0, keepdims=True))
                sum_ref[r] = sum_ref[r] * jnp.exp(old - top) + jnp.sum(
                    jnp.exp(value - top), axis=0, keepdims=True
                )
                top_ref[r] = top

        panel_turns(hop, first, last, turn)

    first_pieces = PIECES // local
    row_copies = [[row_copy(d, piece) for d in range(1, nf)] for piece in range(PIECES)]
    for piece in range(first_pieces):
        for copy in row_copies[piece]:
            copy.start()
    for way in range(2):
        d = (way * nb + 1) * per
        mine = thin_spot(cen_ref, 0, c, x)
        go(onward(way), remote(mine, thin_spot(all_ref, z, c, x), 0, d, step(way), f))
    for p in range(per):
        for way in range(2):
            d = (way * nb + 1) * per + p
            mine = wide_spot(cen_ref, 0, p, c)
            go(onward(way), remote(mine, wide_spot(all_ref, z, p, c), 4, d, step(way), f))
    loads = [
        pltpu.make_async_copy(
            emb_ref.at[pl.ds(pl.multiple_of(f * rows, rows), rows), :],
            rows_ref.at[:, pl.ds(pl.multiple_of(f * width, width), width)],
            own_sem.at[0],
        ),
        pltpu.make_async_copy(
            cen_ref, all_ref.at[pl.ds(pl.multiple_of(z * per * CB, CB), per * CB), :], own_sem.at[1]
        ),
    ]
    for copy in loads:
        copy.start()
    top_ref[...] = jnp.full_like(top_ref, neg_big)
    sum_ref[...] = jnp.zeros_like(sum_ref)
    early = list(range(1))
    late = list(range(1, local))
    both(pass_thin, 1)
    for piece in range(first_pieces, PIECES):
        for copy in row_copies[piece]:
            copy.start()
    for copy in loads:
        copy.wait()
    for p in range(per):
        both(pass_wide, 1, p)
    for piece in range(first_pieces):
        for copy in row_copies[piece]:
            copy.wait_recv()
    scores(0, 0, per, early)
    both(pass_thin, 2)
    both(pass_across, 1)
    both(have_thin, 1)
    for p in range(per):
        both(have_wide, 1, p)
    scores(1, 0, per, early)
    for p in range(per):
        both(pass_wide, 2, p)
    for hop in range(3, nb):
        both(pass_thin, hop)
        for p in range(per):
            if hop < nb - 1 or p < per - 1:
                both(pass_wide, hop, p)
    for piece in range(first_pieces, PIECES):
        for copy in row_copies[piece]:
            copy.wait_recv()
    scores(0, 0, per, late)
    scores(1, 0, per, late)
    for hop in range(2, nb):
        both(pass_across, hop)
        both(have_thin, hop)
        for p in range(per):
            both(have_wide, hop, p)
            scores(hop, p, p + 1, early + late)
            if hop == nb - 2 and p == per - 2:
                both(pass_wide, nb - 1, per - 1)

    for r in range(local):
        norm = top_ref[r] + jnp.log(sum_ref[r])
        for j in range(RB // 128):
            norm_ref[r * (RB // 128) + j, :] = norm[0, j * 128 : (j + 1) * 128]
        top_ref[r] = norm

    lead = 0

    def cols(t):
        return pl.ds(pl.multiple_of(t * size, size), size)

    left, right = jnp.int32(0), jnp.int32(nb - 1)
    turns = []
    for _ in range(nb):
        pick = (z - left) >= (right - z)
        turns.append(jnp.where(pick, left, right))
        left, right = jnp.where(pick, left + 1, left), jnp.where(pick, right, right - 1)

    def a_copy(q, t):
        return pltpu.make_async_remote_copy(
            src_ref=to_sib.at[q, :, cols(t)],
            dst_ref=from_sib.at[q, :, cols(t)],
            send_sem=a_send.at[q, t],
            recv_sem=a_recv.at[q, t],
            device_id={"blk": z, "feat": sibling},
            device_id_type=MESH,
        )

    def b_copy(i, t):
        return pltpu.make_async_remote_copy(
            src_ref=to_x.at[i, :, cols(t)],
            dst_ref=from_x.at[i, :, cols(t)],
            send_sem=b_send.at[i, t],
            recv_sem=b_recv.at[i, t],
            device_id={"blk": z, "feat": (1 - x) * 2 + c},
            device_id_type=MESH,
        )

    def z_copy(zz, way, t):
        return pltpu.make_async_remote_copy(
            src_ref=to_z.at[zz, :, cols(t)],
            dst_ref=from_z.at[way, zz, :, cols(t)],
            send_sem=z_send.at[zz, t],
            recv_sem=z_recv.at[way, zz, t],
            device_id={"blk": jnp.clip(z + 1 - 2 * way, 0, nb - 1), "feat": f},
            device_id_type=MESH,
        )

    def line_copy(d):
        zz = lax.rem(z + d, nb)
        return pltpu.make_async_remote_copy(
            src_ref=to_line.at[zz],
            dst_ref=from_line.at[d - 1],
            send_sem=line_send.at[d],
            recv_sem=line_recv.at[d],
            device_id={"blk": zz, "feat": f},
            device_id_type=MESH,
        )

    def swap_copy():
        return pltpu.make_async_remote_copy(
            src_ref=swap_out,
            dst_ref=swap_in,
            send_sem=swap_sem.at[0],
            recv_sem=swap_sem.at[1],
            device_id={"blk": z, "feat": (1 - x) * 2 + c},
            device_id_type=MESH,
        )

    def m_copy(d):
        return pltpu.make_async_remote_copy(
            src_ref=to_mass.at[lax.rem(me + d, n)],
            dst_ref=from_mass.at[d],
            send_sem=m_send.at[d],
            recv_sem=m_recv.at[d],
            device_id=at_offset(d),
            device_id_type=MESH,
        )

    def wide_of(value):
        return value.astype(jnp.float32)

    def place(i):
        zz = turns[nb - 1]
        for t in range(nb - 1):
            zz = jnp.where(i == t, turns[t], zz)
        return zz

    group = CHUNKS // SPANS

    def weights(i, side):
        zz = place(i)
        xx = 1 - x if side == 0 else x
        col = zz * per + xx
        for cc in range(2):
            at = c if cc == 0 else 1 - c
            first = side * CB + cc * own
            for r in range(local):
                value = score_ref[r, col, pl.ds(pl.multiple_of(at * own, own), own), :]
                weight_ref[first : first + own, r * RB : (r + 1) * RB] = jnp.exp(
                    value - top_ref[r]
                ).astype(jnp.bfloat16)

    def masses(i, side):
        zz = place(i)
        xx = 1 - x if side == 0 else x
        part = slice(side * CB, (side + 1) * CB)
        mass = lax.dot_general(
            jnp.ones((8, rows), jnp.bfloat16),
            weight_ref[part, :],
            transposed,
            preferred_element_type=jnp.float32,
        )
        to_mass[zz * nf + xx * 2 + c] = mass[:, :own]
        to_mass[zz * nf + xx * 2 + 1 - c] = mass[:, own:]

    def sums(i):
        for side in range(2):
            weights(i, side)

        def span(u, carry):
            @pl.when(u < SPANS)
            def _():
                at = pl.ds(pl.multiple_of(u * group * size, group * size), group * size)
                total = jnp.dot(
                    weight_ref[...], rows_ref[:, at], preferred_element_type=jnp.float32
                )
                for side in range(2):
                    first = side * CB
                    keep_ref[side * nb + i, :, at] = total[first : first + own]
                    to_sib[side * nb + i, :, at] = total[first + own : first + CB].astype(jnp.bfloat16)
                for side in range(2):
                    for t in range(group):
                        a_copy(side * nb + i, u * group + t).start()

            @pl.when(u > 1)
            def _():
                for t in range(group):
                    at = (u - 2) * group + t
                    pl.when(at > lead)(functools.partial(send_x, i, at))

            @pl.when(u == 2)
            def _():
                send_line(i)

            return carry

        lax.fori_loop(0, SPANS + 2, span, 0)
        for side in range(2):
            masses(i, side)

    def send_x(i, t):
        a_copy(i, t).wait()
        to_x[i, :, cols(t)] = (
            keep_ref[i, :, cols(t)] + wide_of(from_sib[i, :, cols(t)])
        ).astype(jnp.bfloat16)
        b_copy(i, t).start()

    def course(i):
        zz = place(i)
        fed = jnp.logical_or(
            jnp.logical_and(zz > z, z > 0), jnp.logical_and(zz < z, z < nb - 1)
        )
        return zz, (zz < z).astype(jnp.int32), fed

    def send_line(i):
        zz = place(i)
        for side in range(2):
            q = side * nb + i
            a_copy(q, lead).wait()
            sides_ref[side] = keep_ref[q, :, cols(lead)] + wide_of(from_sib[q, :, cols(lead)])

        @pl.when(zz != z)
        def _():
            to_line[zz] = sides_ref[...].astype(jnp.bfloat16)
            line_copy(lax.rem(zz - z + nb, nb)).start()

    def swap():
        def one(d, carry):
            line_copy(d).wait()
            sides_ref[...] += wide_of(from_line[d - 1])
            return carry

        lax.fori_loop(1, nb, one, 0)
        swap_out[...] = sides_ref[0].astype(jnp.bfloat16)
        swap_copy().start()

    def mass_end(d, total):
        m_copy(d).wait()
        return total + from_mass[d]

    def masses_in():
        mass = lax.fori_loop(1, n, mass_end, to_mass[me])[:1]
        spread = jnp.broadcast_to(mass, (own, own))
        diagonal = lax.broadcasted_iota(jnp.int32, (own, own), 0) == lax.broadcasted_iota(
            jnp.int32, (own, own), 1
        )
        inverse_ref[...] = 1.0 / (
            jnp.sum(jnp.where(diagonal, spread, 0.0), axis=1, keepdims=True) + prior_mass
        )

    def finish(t, total):
        old = all_ref[pl.ds(pl.multiple_of(me * own, own), own), cols(t)]
        num_ref[:, cols(t)] = (total + prior_mass * wide_of(old)) * inverse_ref[...]

    def send_z(i):
        zz, way, fed = course(i)
        q = nb + i

        def chunk(t, carry):
            a_copy(q, t).wait()
            b_copy(i, t).wait()
            part_ref[...] = (
                keep_ref[q, :, cols(t)]
                + wide_of(from_sib[q, :, cols(t)])
                + wide_of(from_x[i, :, cols(t)])
            )

            @pl.when(fed)
            def _():
                z_copy(zz, way, t).wait_recv()
                part_ref[...] += wide_of(from_z[way, zz, :, cols(t)])

            @pl.when(zz != z)
            def _():
                to_z[zz, :, cols(t)] = part_ref[...].astype(jnp.bfloat16)
                z_copy(zz, way, t).start()

            @pl.when(zz == z)
            def _():
                for back in range(2):

                    @pl.when((z > 0) if back == 0 else (z < nb - 1))
                    def _():
                        z_copy(z, back, t).wait_recv()
                        part_ref[...] += wide_of(from_z[back, z, :, cols(t)])

                finish(t, part_ref[...])

            return carry

        lax.fori_loop(lead + 1, CHUNKS, chunk, 0)

    def turn(i, carry):
        @pl.when(i < nb)
        def _():
            sums(i)

        @pl.when(i == nb - 1)
        def _():
            def mass_start(d, carry):
                m_copy(d).start()
                return carry

            lax.fori_loop(1, n, mass_start, 0)

        pl.when(i == nb + 1)(swap)
        pl.when(i == nb + 1)(masses_in)

        @pl.when(i > 1)
        def _():
            send_z(i - 2)

        return carry

    lax.fori_loop(0, nb + 2, turn, 0)

    def last(t, carry):
        for zz in range(nb):

            @pl.when(z != zz)
            def _():
                z_copy(zz, 0, t).wait_send()

        return carry

    lax.fori_loop(lead + 1, CHUNKS, last, 0)
    swap_copy().wait()
    finish(lead, sides_ref[1] + wide_of(swap_in[...]))
    for group in row_copies:
        for copy in group:
            copy.wait_send()
    for cond, copy in started:
        pl.when(cond)(copy.wait_send)


def fused(allow, embeddings, centroids, nb, nf):
    rows = embeddings.shape[0] // nf
    local = rows // RB
    n = nb * nf
    own = K // n
    per = K // nb // CB
    kinds = 6
    vmem = pl.BlockSpec(memory_space=pltpu.VMEM)
    hbm = pl.BlockSpec(memory_space=pltpu.HBM)
    dma = pltpu.SemaphoreType.DMA
    bf16, f32 = jnp.bfloat16, jnp.float32
    return pl.pallas_call(
        functools.partial(fused_kernel, nb, nf),
        out_shape=(
            jax.ShapeDtypeStruct((own, D), f32),
            jax.ShapeDtypeStruct((rows // 128, 128), f32),
        ),
        in_specs=[pl.BlockSpec(memory_space=pltpu.SMEM), hbm, hbm],
        out_specs=(vmem,) * 2,
        scratch_shapes=[
            pltpu.VMEM((rows, D), bf16),
            pltpu.VMEM((K, D), bf16),
            pltpu.VMEM((NCB, CB, 1), f32),
            pltpu.VMEM((local, NCB, CB, RB), f32),
            pltpu.VMEM((local, 1, RB), f32),
            pltpu.VMEM((local, 1, RB), f32),
            pltpu.VMEM((2 * CB, rows), bf16),
            pltpu.VMEM((2 * nb, own, D), f32),
            pltpu.VMEM((2 * nb, own, D), bf16),
            pltpu.VMEM((2 * nb, own, D), bf16),
            pltpu.VMEM((nb, own, D), bf16),
            pltpu.VMEM((nb, own, D), bf16),
            pltpu.VMEM((own, D // CHUNKS), f32),
            pltpu.VMEM((nb, own, D), bf16),
            pltpu.VMEM((2, nb, own, D), bf16),
            pltpu.VMEM((2, own, D // CHUNKS), f32),
            pltpu.VMEM((nb, 2, own, D // CHUNKS), bf16),
            pltpu.VMEM((nb - 1, 2, own, D // CHUNKS), bf16),
            pltpu.VMEM((own, D // CHUNKS), bf16),
            pltpu.VMEM((own, D // CHUNKS), bf16),
            pltpu.VMEM((n, 8, own), f32),
            pltpu.VMEM((n, 8, own), f32),
            pltpu.VMEM((own, 1), f32),
            dma((nf, PIECES)),
            dma((nf, PIECES)),
            dma((kinds, 2 * nb * per)),
            dma((kinds, 2 * nb * per)),
            dma((2,)),
            dma((2 * nb, CHUNKS)),
            dma((2 * nb, CHUNKS)),
            dma((nb, CHUNKS)),
            dma((nb, CHUNKS)),
            dma((nb, CHUNKS)),
            dma((2, nb, CHUNKS)),
            dma((n,)),
            dma((n,)),
            dma((nb,)),
            dma((nb,)),
            dma((2,)),
        ],
        compiler_params=pltpu.CompilerParams(
            collective_id=2, has_side_effects=True, vmem_limit_bytes=58 * 2**20
        ),
        name="fused",
    )(allow, embeddings, centroids)


def body(embeddings, centroids, pair_list):
    nb, nf = lax.axis_size("blk"), lax.axis_size("feat")
    local_rows = embeddings.shape[0] // nf
    local_blocks = local_rows // RB
    device_index = lax.axis_index("blk") * nf + lax.axis_index("feat")
    mine = device_index * local_blocks + jnp.arange(local_blocks, dtype=jnp.int32)
    row_ids, col_ids = pair_list[:, 0], pair_list[:, 1]
    same = row_ids[None, :] == mine[:, None]
    if K // nb == 2 * CB and nf == 4 and local_blocks == 2:
        blocks = jnp.arange(NCB, dtype=jnp.int32)
        listed = same[:, None, :] & (col_ids[None, None, :] == blocks[None, :, None])
        allow = jnp.sum(listed.astype(jnp.int32), axis=2)
        new_centroids, log_norm = fused(allow, embeddings, centroids, nb, nf)
        return (new_centroids, log_norm.reshape(local_rows))
    before = jnp.sum((row_ids[None, :] < mine[:, None]).astype(jnp.int32), axis=1)
    counts = jnp.sum(same.astype(jnp.int32), axis=1)
    rank = jnp.arange(row_ids.shape[0], dtype=jnp.int32)[None, :] - before[:, None]
    slots = jnp.arange(SLOTS, dtype=jnp.int32)
    picked = same[:, None, :] & (rank[:, None, :] == slots[None, :, None])
    chosen = jnp.sum(jnp.where(picked, col_ids[None, None, :], 0), axis=2)
    table = jnp.concatenate([counts[:, None], chosen], axis=1)

    row_data, panels = fetch(embeddings, centroids, nb, nf)
    num, mass, log_norm = terms(table, row_data, panels, nb, nf)
    numerator, denominator = reduce_sums(num, mass, nb, nf)

    own_count = centroids.shape[0] // nf
    own_rows = lax.dynamic_slice_in_dim(
        centroids, lax.axis_index("feat") * own_count, own_count, 0
    ).astype(jnp.float32)
    new_centroids = (numerator + prior_mass * own_rows) / (denominator[0][:, None] + prior_mass)
    return (new_centroids, log_norm.reshape(local_rows))


def solution(mesh):
    return jax.shard_map(
        body,
        mesh=mesh,
        in_specs=(P(("groups", "blk"), "feat"), P(("groups", "blk"), None), P("groups", None)),
        out_specs=(P(("groups", "blk", "feat"), None), P(("groups", "blk", "feat"))),
        check_vma=False,
    )
```
